32 devices in a mesh: dp: 8 (over z, y), seq: 4 (over x, core).
Axes of the slice: x: 2, y: 2, z: 4, core: 2. Of those that a mesh axis runs over, the one named last changes fastest.
Arguments:
- target: bfloat16 [8, 1024, 768], P('dp', 'seq'), may hold values from -6 to 6
- memory: bfloat16 [8, 1024, 768], P('dp', 'seq'), may hold values from -6 to 6
- cotangent: bfloat16 [8, 1024, 768], P('dp', 'seq'), may hold values from -6 to 6
- target_segments: int32 [8, 1024], P('dp', 'seq'), may hold values from 0 to 3, never falling along the last dimension, each value on 1 to 512 neighbouring positions
- memory_segments: int32 [8, 1024], P('dp', 'seq'), may hold values from 0 to 3, never falling along the last dimension, each value on 1 to 512 neighbouring positions
- query_weight: bfloat16 [768, 768], P(('dp', 'seq')), may hold values from -0.21875 to 0.21875
- query_bias: bfloat16 [768], P(('dp', 'seq')), may hold values from -2 to 2
- key_weight: bfloat16 [768, 768], P(('dp', 'seq')), may hold values from -0.21875 to 0.21875
- value_weight: bfloat16 [768, 768], P(('dp', 'seq')), may hold values from -0.21875 to 0.21875
- value_bias: bfloat16 [768], P(('dp', 'seq')), may hold values from -2 to 2
- output_weight: bfloat16 [768, 768], P(('dp', 'seq')), may hold values from -0.875 to 0.875
- output_bias: bfloat16 [768], P(('dp', 'seq')), may hold values from -2 to 2
- first_gain: bfloat16 [768], P(('dp', 'seq')), may hold values from 0.5 to 1.5
- first_shift: bfloat16 [768], P(('dp', 'seq')), may hold values from -2 to 2
- probe_weight: bfloat16 [768, 768], P(('dp', 'seq')), may hold values from -0.21875 to 0.21875
- probe_bias: bfloat16 [768], P(('dp', 'seq')), may hold values from -2 to 2
- lookup_weight: bfloat16 [768, 768], P(('dp', 'seq')), may hold values from -0.21875 to 0.21875
- content_weight: bfloat16 [768, 768], P(('dp', 'seq')), may hold values from -0.21875 to 0.21875
- content_bias: bfloat16 [768], P(('dp', 'seq')), may hold values from -2 to 2
- merge_weight: bfloat16 [768, 768], P(('dp', 'seq')), may hold values from -0.875 to 0.875
- merge_bias: bfloat16 [768], P(('dp', 'seq')), may hold values from -2 to 2
- second_gain: bfloat16 [768], P(('dp', 'seq')), may hold values from 0.5 to 1.5
- second_shift: bfloat16 [768], P(('dp', 'seq')), may hold values from -2 to 2
- expand_weight: bfloat16 [768, 3072], P(('dp', 'seq')), may hold values from -0.21875 to 0.21875
- expand_bias: bfloat16 [3072], P(('dp', 'seq')), may hold values from -2 to 2
- shrink_weight: bfloat16 [3072, 768], P(('dp', 'seq')), may hold values from -0.109375 to 0.109375
- shrink_bias: bfloat16 [768], P(('dp', 'seq')), may hold values from -2 to 2
- third_gain: bfloat16 [768], P(('dp', 'seq')), may hold values from 0.5 to 1.5
- third_shift: bfloat16 [768], P(('dp', 'seq')), may hold values from -2 to 2
Outputs:
- layer_output: bfloat16 [8, 1024, 768], P('dp', 'seq')
- target_grad: float32 [8, 1024, 768], P('dp', 'seq')
- memory_grad: float32 [8, 1024, 768], P('dp', 'seq')
- query_weight_grad: float32 [768, 768], P(('dp', 'seq'))
- query_bias_grad: float32 [768], P(('dp', 'seq'))
- key_weight_grad: float32 [768, 768], P(('dp', 'seq'))
- value_weight_grad: float32 [768, 768], P(('dp', 'seq'))
- value_bias_grad: float32 [768], P(('dp', 'seq'))
- output_weight_grad: float32 [768, 768], P(('dp', 'seq'))
- output_bias_grad: float32 [768], P(('dp', 'seq'))
- first_gain_grad: float32 [768], P(('dp', 'seq'))
- first_shift_grad: float32 [768], P(('dp', 'seq'))
- probe_weight_grad: float32 [768, 768], P(('dp', 'seq'))
- probe_bias_grad: float32 [768], P(('dp', 'seq'))
- lookup_weight_grad: float32 [768, 768], P(('dp', 'seq'))
- content_weight_grad: float32 [768, 768], P(('dp', 'seq'))
- content_bias_grad: float32 [768], P(('dp', 'seq'))
- merge_weight_grad: float32 [768, 768], P(('dp', 'seq'))
- merge_bias_grad: float32 [768], P(('dp', 'seq'))
- second_gain_grad: float32 [768], P(('dp', 'seq'))
- second_shift_grad: float32 [768], P(('dp', 'seq'))
- expand_weight_grad: float32 [768, 3072], P(('dp', 'seq'))
- expand_bias_grad: float32 [3072], P(('dp', 'seq'))
- shrink_weight_grad: float32 [3072, 768], P(('dp', 'seq'))
- shrink_bias_grad: float32 [768], P(('dp', 'seq'))
- third_gain_grad: float32 [768], P(('dp', 'seq'))
- third_shift_grad: float32 [768], P(('dp', 'seq'))
The draws below stay inside these ranges and needn't reach their ends.
Inputs may be any that keep to these rules, and one draw needn't show every extreme that they name: `target_segments`: in every row the ids never fall and each of the 4 documents has 1 to 512 tokens, one exactly 512. `memory_segments`: in every row the ids never fall and each of the 4 documents has 1 to 512 tokens, one exactly 512.
All inputs are finite; a program needn't handle non-finite values.
Results may differ from the reference program's by a relative error of at most 0.02.
Values may be sent and summed in bfloat16 or wider, within the bound.
No kernel may reach another device: no remote copies, remote signals or barrier semaphores. Data moves between devices by JAX's collectives and lax.ppermute only.
A program may use at most 256 MiB of HBM per device.

```python
import math
import jax
import jax.numpy as jnp
import numpy as np
from jax import lax

D = 768
HEADS = 12
HEAD_DIM = 64
FF = 3072
L = 1024
DOCS = 4
ROWS = 8


def level_of(own_key, extent, split, least, largest):
    loudness = 1.0
    for dim, blocks in split:
        steps = jax.random.uniform(jax.random.fold_in(jax.random.fold_in(own_key, 6), dim), (blocks,), jnp.float32, least / len(split), largest / len(split))
        loudness = loudness * jnp.repeat(jnp.exp(steps), extent[dim] // blocks).reshape((-1,) + (1,) * (len(extent) - 1 - dim))
    return loudness


def split_up(count, total, bound, skew):
    loads = [(1 << 20) // math.isqrt(rank ** skew) + 1 for rank in range(2, count + 1)]
    spare, holding = total - bound - (count - 1), [1] * (count - 1)
    while spare > 0:
        candidates = [i for i in range(count - 1) if holding[i] < bound]
        whole, left = sum([loads[i] for i in candidates]), spare
        for i in candidates:
            more = min(bound - holding[i], max(1, left * loads[i] // whole), spare)
            holding[i] = holding[i] + more
            spare = spare - more
    return np.array([bound] + holding)


def ragged(own_key, amount, total, bound, skew):
    if amount == 2:
        one = jax.random.randint(own_key, (), max(1, total - bound), min(bound, total - 1) + 1)
        return jnp.stack([one, total - one])
    tallies = jnp.asarray(split_up(amount, total, bound, skew), jnp.int32)
    couples = (amount - 1) // 2
    giver, sink = tallies[1:1 + 2 * couples:2], tallies[2:2 + 2 * couples:2]
    room = jnp.minimum(giver - 1, bound - sink)
    moved = jax.random.randint(jax.random.fold_in(own_key, 1), (couples,), 0, 1 << 20) % (room + 1)
    tallies = tallies.at[1:1 + 2 * couples:2].set(giver - moved).at[2:2 + 2 * couples:2].set(sink + moved)
    return tallies[jax.random.permutation(jax.random.fold_in(own_key, 2), amount)]


def gaussian(key, shape, spread, limit, shards=(), held_as=jnp.bfloat16):
    entries = jax.random.normal(key, shape, jnp.float32) * spread
    if len(shards) > 0:
        entries = level_of(key, shape, shards, -0.22, 0.18) * entries
    return jnp.clip(entries, min=-limit, max=limit).astype(held_as)


def setup_inputs(seed: int = 0) -> dict:
    key_of = jax.random.split(jax.random.key(seed), 30)
    return {
        "target": gaussian(key_of[0], (ROWS, L, D), 1.0, 6.0, ((0, 8), (1, 4))),
        "memory": gaussian(key_of[1], (ROWS, L, D), 1.0, 6.0, ((0, 8), (1, 4))),
        "cotangent": gaussian(key_of[2], (ROWS, L, D), 1.0, 6.0, ((0, 8), (1, 4))),
        "target_segments": jax.vmap(lambda own: jnp.searchsorted(jnp.cumsum(ragged(own, DOCS, L, L // 2, 2)), jnp.arange(L), side="right"))(jax.random.split(key_of[3], ROWS)).reshape((ROWS, L)).astype(jnp.int32),
        "memory_segments": jax.vmap(lambda own: jnp.searchsorted(jnp.cumsum(ragged(own, DOCS, L, L // 2, 2)), jnp.arange(L), side="right"))(jax.random.split(key_of[4], ROWS)).reshape((ROWS, L)).astype(jnp.int32),
        "query_weight": gaussian(key_of[5], (D, D), D ** -0.5, 0.21875, ((0, 32),)),
        "query_bias": gaussian(key_of[6], (D,), 0.3, 2.0, ((0, 32),)),
        "key_weight": gaussian(key_of[7], (D, D), D ** -0.5, 0.21875, ((0, 32),)),
        "value_weight": gaussian(key_of[8], (D, D), D ** -0.5, 0.21875, ((0, 32),)),
        "value_bias": gaussian(key_of[9], (D,), 0.3, 2.0, ((0, 32),)),
        "output_weight": gaussian(key_of[10], (D, D), (D // 16) ** -0.5, 0.875, ((0, 32),)),
        "output_bias": gaussian(key_of[11], (D,), 0.3, 2.0, ((0, 32),)),
        "first_gain": jnp.clip(1.0 + 0.1 * jax.random.normal(key_of[12], (D,), jnp.float32), 0.5, 1.5).astype(jnp.bfloat16),
        "first_shift": gaussian(key_of[13], (D,), 0.3, 2.0, ((0, 32),)),
        "probe_weight": gaussian(key_of[14], (D, D), D ** -0.5, 0.21875, ((0, 32),)),
        "probe_bias": gaussian(key_of[15], (D,), 0.3, 2.0, ((0, 32),)),
        "lookup_weight": gaussian(key_of[16], (D, D), D ** -0.5, 0.21875, ((0, 32),)),
        "content_weight": gaussian(key_of[17], (D, D), D ** -0.5, 0.21875, ((0, 32),)),
        "content_bias": gaussian(key_of[18], (D,), 0.3, 2.0, ((0, 32),)),
        "merge_weight": gaussian(key_of[19], (D, D), (D // 16) ** -0.5, 0.875, ((0, 32),)),
        "merge_bias": gaussian(key_of[20], (D,), 0.3, 2.0, ((0, 32),)),
        "second_gain": jnp.clip(1.0 + 0.1 * jax.random.normal(key_of[21], (D,), jnp.float32), 0.5, 1.5).astype(jnp.bfloat16),
        "second_shift": gaussian(key_of[22], (D,), 0.3, 2.0, ((0, 32),)),
        "expand_weight": gaussian(key_of[23], (D, FF), D ** -0.5, 0.21875, ((0, 32),)),
        "expand_bias": gaussian(key_of[24], (FF,), 0.3, 2.0, ((0, 32),)),
        "shrink_weight": gaussian(key_of[25], (FF, D), FF ** -0.5, 0.109375, ((0, 32),)),
        "shrink_bias": gaussian(key_of[26], (D,), 0.3, 2.0, ((0, 32),)),
        "third_gain": jnp.clip(1.0 + 0.1 * jax.random.normal(key_of[27], (D,), jnp.float32), 0.5, 1.5).astype(jnp.bfloat16),
        "third_shift": gaussian(key_of[28], (D,), 0.3, 2.0, ((0, 32),)),
    }


@jax.custom_vjp
def low(v):
    return lax.optimization_barrier(v.astype(jnp.bfloat16)).astype(jnp.float32)

@jax.custom_vjp
def low_back(v):
    return v

def low_keep(v):
    return (low(v), None)

def low_pass(kept, grad):
    return (grad,)

def back_keep(v):
    return (v, None)

def back_low(kept, grad):
    return (low(grad),)
low.defvjp(low_keep, low_pass)
low_back.defvjp(back_keep, back_low)
NEG_FILL = -1e+30
EPSILON = 1e-05
HIGHEST = lax.Precision.HIGHEST

def matmul(left, right):
    return jnp.dot(left, right, precision=HIGHEST, preferred_element_type=jnp.float32)

def both_round(value):
    return low_back(low(value))

def layer_norm(hidden, gain, shift):
    centred = hidden - lax.optimization_barrier(jnp.mean(hidden, axis=-1, keepdims=True))
    scaled = centred * lax.rsqrt(lax.optimization_barrier(jnp.mean(centred * centred, axis=-1, keepdims=True)) + EPSILON)
    return scaled * gain + shift

def attend(query_rows, key_rows, value_rows, allowed):
    count_q = query_rows.shape[0]
    count_k = key_rows.shape[0]
    query_heads = query_rows.reshape(count_q, HEADS, HEAD_DIM)
    key_heads = key_rows.reshape(count_k, HEADS, HEAD_DIM)
    value_heads = value_rows.reshape(count_k, HEADS, HEAD_DIM)
    scores = low_back(jnp.einsum('qhd,khd->hqk', query_heads, key_heads, precision=HIGHEST))
    scores = jnp.where(allowed[None], scores, NEG_FILL)
    weights = low(jax.nn.softmax(scores, axis=-1))
    mixed = jnp.einsum('hqk,khd->qhd', weights, value_heads, precision=HIGHEST)
    return both_round(mixed.reshape(count_q, HEADS * HEAD_DIM))

def layer(params, target_row, memory_row, seg_target, seg_memory, causal):
    query_weight, query_bias, key_weight, value_weight, value_bias, output_weight, output_bias, first_gain, first_shift, probe_weight, probe_bias, lookup_weight, content_weight, content_bias, merge_weight, merge_bias, second_gain, second_shift, expand_weight, expand_bias, shrink_weight, shrink_bias, third_gain, third_shift = params
    query_one = both_round((matmul(target_row, query_weight) + query_bias) * 0.125)
    key_one = both_round(matmul(target_row, key_weight))
    value_one = both_round(matmul(target_row, value_weight) + value_bias)
    self_allowed = causal & (seg_target[:, None] == seg_target[None, :])
    mixed_one = attend(query_one, key_one, value_one, self_allowed)
    first_sum = target_row + low_back(matmul(mixed_one, output_weight) + output_bias)
    first_out = low(layer_norm(first_sum, first_gain, first_shift))
    query_two = both_round((matmul(first_out, probe_weight) + probe_bias) * 0.125)
    key_two = both_round(matmul(memory_row, lookup_weight))
    value_two = both_round(matmul(memory_row, content_weight) + content_bias)
    cross_allowed = seg_target[:, None] == seg_memory[None, :]
    mixed_two = attend(query_two, key_two, value_two, cross_allowed)
    second_sum = first_out + low_back(matmul(mixed_two, merge_weight) + merge_bias)
    second_out = low(layer_norm(second_sum, second_gain, second_shift))
    pre_act = low_back(matmul(second_out, expand_weight) + expand_bias)
    hidden = low(jax.nn.gelu(pre_act, approximate=False))
    third_sum = second_out + low_back(matmul(hidden, shrink_weight) + shrink_bias)
    return layer_norm(third_sum, third_gain, third_shift)

def reference(target, memory, cotangent, target_segments, memory_segments, query_weight, query_bias, key_weight, value_weight, value_bias, output_weight, output_bias, first_gain, first_shift, probe_weight, probe_bias, lookup_weight, content_weight, content_bias, merge_weight, merge_bias, second_gain, second_shift, expand_weight, expand_bias, shrink_weight, shrink_bias, third_gain, third_shift):
    params = tuple((item.astype(jnp.float32) for item in (query_weight, query_bias, key_weight, value_weight, value_bias, output_weight, output_bias, first_gain, first_shift, probe_weight, probe_bias, lookup_weight, content_weight, content_bias, merge_weight, merge_bias, second_gain, second_shift, expand_weight, expand_bias, shrink_weight, shrink_bias, third_gain, third_shift)))
    places = jnp.arange(L, dtype=jnp.int32)
    causal = places[:, None] >= places[None, :]

    def row_step(totals, items):
        target_row, memory_row, cot_row, seg_target, seg_memory = items

        def run(weights, tgt, mem):
            return layer(weights, tgt, mem, seg_target, seg_memory, causal)
        result, pull = jax.vjp(run, params, target_row.astype(jnp.float32), memory_row.astype(jnp.float32))
        grads, tgt_grad, mem_grad = pull(cot_row.astype(jnp.float32))
        totals = jax.tree.map(lambda first, second: first + second, totals, grads)
        return (totals, (result.astype(jnp.bfloat16), tgt_grad, mem_grad))
    start = jax.tree.map(jnp.zeros_like, params)
    totals, stacked = lax.scan(row_step, start, (target, memory, cotangent, target_segments, memory_segments))
    layer_output, target_grad, memory_grad = stacked
    grad_a, grad_b, grad_c, grad_d, grad_e, grad_f, grad_g, grad_h, grad_i, grad_j, grad_k, grad_l, grad_m, grad_n, grad_o, grad_p, grad_q, grad_r, grad_s, grad_t, grad_u, grad_v, grad_w, grad_x = totals
    return (layer_output, target_grad, memory_grad, grad_a, grad_b, grad_c, grad_d, grad_e, grad_f, grad_g, grad_h, grad_i, grad_j, grad_k, grad_l, grad_m, grad_n, grad_o, grad_p, grad_q, grad_r, grad_s, grad_t, grad_u, grad_v, grad_w, grad_x)
```

```python
import jax
import jax.numpy as jnp
from jax import lax
from jax.experimental import pallas as pl
from jax.experimental.pallas import tpu as pltpu
from jax.sharding import PartitionSpec as P

HEAD_DIM = 64
PAIR = 2 * HEAD_DIM
NEG_FILL = -1e30
EPSILON = 1e-05
BF16 = jnp.bfloat16
F32 = jnp.float32
ALL = ("dp", "seq")

SELF_WEIGHTS = ("query_weight", "key_weight", "value_weight", "output_weight")
CROSS_WEIGHTS = ("probe_weight", "lookup_weight", "content_weight", "merge_weight")
VECTORS = (
    "query_bias",
    "value_bias",
    "output_bias",
    "first_gain",
    "first_shift",
    "probe_bias",
    "content_bias",
    "merge_bias",
    "second_gain",
    "second_shift",
    "shrink_bias",
    "third_gain",
    "third_shift",
)
ARGS = (
    "target",
    "memory",
    "cotangent",
    "target_segments",
    "memory_segments",
    "query_weight",
    "query_bias",
    "key_weight",
    "value_weight",
    "value_bias",
    "output_weight",
    "output_bias",
    "first_gain",
    "first_shift",
    "probe_weight",
    "probe_bias",
    "lookup_weight",
    "content_weight",
    "content_bias",
    "merge_weight",
    "merge_bias",
    "second_gain",
    "second_shift",
    "expand_weight",
    "expand_bias",
    "shrink_weight",
    "shrink_bias",
    "third_gain",
    "third_shift",
)


def dot(left, right):
    return jnp.dot(left, right, preferred_element_type=F32)


def dot_t(left, right):
    return lax.dot_general(left, right, (((1,), (1,)), ((), ())), preferred_element_type=F32)


def t_dot(left, right):
    return lax.dot_general(left, right, (((0,), (0,)), ((), ())), preferred_element_type=F32)


def token_sum(values):
    return jnp.sum(values.astype(F32), axis=0)


def fill_mask(block, q0_ref, qseg_ref, kseg_ref, kpos_ref, bias, flags):
    rows = bias.shape[0]
    place = q0_ref[0] + lax.broadcasted_iota(jnp.int32, (rows, block), 0)
    for j in range(bias.shape[1] // block):
        cols = pl.ds(j * block, block)
        allowed = (kseg_ref[:, cols] == qseg_ref[...]) & (kpos_ref[:, cols] <= place)
        term = jnp.where(allowed, 0.0, NEG_FILL)
        bias[:, cols] = term
        flags[j] = (jnp.max(term) > -1.0).astype(jnp.int32)


def one_head(value, head):
    lane = lax.broadcasted_iota(jnp.int32, value.shape, 1)
    return jnp.where((lane < HEAD_DIM) == (head == 0), value, jnp.zeros_like(value))


def attend_kernel(block, q0_ref, q_ref, k_ref, v_ref, qseg_ref, kseg_ref, kpos_ref, o_ref, log_ref, bias, flags, scores, weights, sums):
    blocks = bias.shape[1] // block

    @pl.when(pl.program_id(0) == 0)
    def _():
        fill_mask(block, q0_ref, qseg_ref, kseg_ref, kpos_ref, bias, flags)
        scores[...] = jnp.full(scores.shape, NEG_FILL, F32)
        weights[...] = jnp.zeros(weights.shape, BF16)

    outs = []
    logs = []
    for head in range(2):
        query = one_head(q_ref[...], head)
        for j in range(blocks):

            @pl.when(flags[j] > 0)
            def _():
                cols = pl.ds(j * block, block)
                scores[:, cols] = dot_t(query, k_ref[cols, :]) + bias[:, cols]

        peak = jnp.max(scores[...], axis=-1, keepdims=True)
        sums[...] = jnp.zeros(sums.shape, F32)
        for j in range(blocks):

            @pl.when(flags[j] > 0)
            def _():
                cols = pl.ds(j * block, block)
                part = jnp.exp(scores[:, cols] - peak)
                sums[...] += jnp.sum(part, axis=-1, keepdims=True)
                weights[:, cols] = part.astype(BF16)

        total = sums[...]
        outs.append(dot(weights[...], v_ref[...]) * (1.0 / total))
        logs.append(peak + jnp.log(total))
    lane = lax.broadcasted_iota(jnp.int32, o_ref.shape, 1)
    o_ref[...] = jnp.where(lane < HEAD_DIM, outs[0], outs[1]).astype(BF16)
    log_ref[...] = jnp.where(lane < HEAD_DIM, logs[0], logs[1])


def attend_back_kernel(block, q0_ref, q_ref, k_ref, v_ref, g_ref, log_ref, qseg_ref, kseg_ref, kpos_ref, dq_ref, dk_ref, dv_ref, bias, flags, probs, slopes, score_grads, weights, along):
    rows = bias.shape[0]
    blocks = bias.shape[1] // block

    @pl.when(pl.program_id(0) == 0)
    def _():
        fill_mask(block, q0_ref, qseg_ref, kseg_ref, kpos_ref, bias, flags)
        score_grads[...] = jnp.zeros(score_grads.shape, BF16)

    queries = []
    grads = []
    for head in range(2):
        query = one_head(q_ref[...], head)
        grad = one_head(g_ref[...], head)
        queries.append(query)
        grads.append(grad)
        log = log_ref[:, head * HEAD_DIM : head * HEAD_DIM + 1]
        along[...] = jnp.zeros(along.shape, F32)
        own = pl.ds(head * rows, rows)
        for j in range(blocks):

            @pl.when(flags[j] > 0)
            def _():
                cols = pl.ds(j * block, block)
                part = jnp.exp(dot_t(query, k_ref[cols, :]) + bias[:, cols] - log)
                slope = dot_t(grad, v_ref[cols, :])
                probs[:, cols] = part
                slopes[:, cols] = slope
                weights[own, cols] = part.astype(BF16)
                along[...] += jnp.sum(part * slope, axis=-1, keepdims=True)

        inner = along[...]
        for j in range(blocks):

            @pl.when(flags[j] > 0)
            def _():
                cols = pl.ds(j * block, block)
                score_grads[own, cols] = (probs[:, cols] * (slopes[:, cols] - inner)).astype(BF16)

    both_queries = jnp.concatenate(queries, axis=0)
    both_grads = jnp.concatenate(grads, axis=0)
    for j in range(blocks):
        cols = pl.ds(j * block, block)

        @pl.when(flags[j] > 0)
        def _():
            dk_ref[cols, :] = t_dot(score_grads[:, cols], both_queries).astype(BF16)
            dv_ref[cols, :] = t_dot(weights[:, cols], both_grads).astype(BF16)

        @pl.when(flags[j] == 0)
        def _():
            dk_ref[cols, :] = jnp.zeros((block, PAIR), BF16)
            dv_ref[cols, :] = jnp.zeros((block, PAIR), BF16)

    lane = lax.broadcasted_iota(jnp.int32, dq_ref.shape, 1)
    both = dot(score_grads[...], k_ref[...])
    dq_ref[...] = (jnp.where(lane < HEAD_DIM, both[:rows], both[rows:]).astype(BF16) * 0.125).astype(BF16)


def attend_specs(rows, total):
    whole = lambda shape: pl.BlockSpec(shape, lambda i: (0, 0))
    strip = lambda count: pl.BlockSpec((count, PAIR), lambda i: (0, i))
    return (
        pl.BlockSpec(memory_space=pltpu.SMEM),
        strip(rows),
        strip(total),
        [whole((rows, 1)), whole((1, total)), whole((1, total))],
    )


def attend_forward(query, key, value, masks, block):
    rows, width = query.shape
    total = key.shape[0]
    scalar, narrow, tall, marks = attend_specs(rows, total)
    q0, qseg, kseg, kpos = masks
    return pl.pallas_call(
        lambda *refs: attend_kernel(block, *refs),
        grid=(width // PAIR,),
        in_specs=[scalar, narrow, tall, tall] + marks,
        out_specs=[narrow, narrow],
        out_shape=[jax.ShapeDtypeStruct((rows, width), BF16), jax.ShapeDtypeStruct((rows, width), F32)],
        scratch_shapes=[
            pltpu.VMEM((rows, total), F32),
            pltpu.SMEM((total // block,), jnp.int32),
            pltpu.VMEM((rows, total), F32),
            pltpu.VMEM((rows, total), BF16),
            pltpu.VMEM((rows, 1), F32),
        ],
        cost_estimate=pl.CostEstimate(flops=8 * rows * total * width, bytes_accessed=8 * total * width, transcendentals=rows * total * 12),
        compiler_params=pltpu.CompilerParams(dimension_semantics=("arbitrary",)),
        name="attend_forward",
    )(q0, query, key, value, qseg, kseg, kpos)


def attend_backward(query, key, value, grad, log, masks, block):
    rows, width = query.shape
    total = key.shape[0]
    scalar, narrow, tall, marks = attend_specs(rows, total)
    q0, qseg, kseg, kpos = masks
    return pl.pallas_call(
        lambda *refs: attend_back_kernel(block, *refs),
        grid=(width // PAIR,),
        in_specs=[scalar, narrow, tall, tall, narrow, narrow] + marks,
        out_specs=[narrow, tall, tall],
        out_shape=[
            jax.ShapeDtypeStruct((rows, width), BF16),
            jax.ShapeDtypeStruct((total, width), BF16),
            jax.ShapeDtypeStruct((total, width), BF16),
        ],
        scratch_shapes=[
            pltpu.VMEM((rows, total), F32),
            pltpu.SMEM((total // block,), jnp.int32),
            pltpu.VMEM((rows, total), F32),
            pltpu.VMEM((rows, total), F32),
            pltpu.VMEM((2 * rows, total), BF16),
            pltpu.VMEM((2 * rows, total), BF16),
            pltpu.VMEM((rows, 1), F32),
        ],
        cost_estimate=pl.CostEstimate(flops=20 * rows * total * width, bytes_accessed=16 * total * width, transcendentals=rows * total * 12),
        compiler_params=pltpu.CompilerParams(dimension_semantics=("arbitrary",)),
        name="attend_backward",
    )(q0, query, key, value, grad, log, qseg, kseg, kpos)


def norm_forward(hidden, gain, shift):
    centred = hidden - jnp.mean(hidden, axis=-1, keepdims=True)
    inverse = lax.rsqrt(jnp.mean(centred * centred, axis=-1, keepdims=True) + EPSILON)
    normed = centred * inverse
    return normed * gain + shift, normed, inverse


def norm_backward(upstream, normed, inverse, gain):
    scaled = upstream * gain
    inner = jnp.mean(scaled, axis=-1, keepdims=True)
    along = jnp.mean(scaled * normed, axis=-1, keepdims=True)
    return inverse * (scaled - inner - normed * along), token_sum(upstream * normed), token_sum(upstream)


def exact_gelu(values):
    return jax.nn.gelu(values, approximate=False)


def seq_offsets(count):
    offsets = [0]
    bit = count // 2
    while bit:
        offsets = offsets + [o ^ bit for o in offsets]
        bit //= 2
    return offsets


def swap(value, axis, bit):
    count = lax.axis_size(axis)
    return lax.ppermute(value, axis, [(i, i ^ bit) for i in range(count)])


def seq_gather(rows):
    bit = lax.axis_size("seq") // 2
    while bit:
        rows = jnp.concatenate([rows, swap(rows, "seq", bit)], axis=0)
        bit //= 2
    return rows


def seq_reduce(parts):
    count = lax.axis_size("seq")
    bit = 1
    total = parts
    while bit < count:
        half = total.shape[0] // 2
        got = swap(total[half:].astype(BF16), "seq", bit)
        total = total[:half].astype(F32) + got.astype(F32)
        bit *= 2
    return total[0]


STAGES = ((16, 8, 2, 4), (8, 16, 4, 2))
BLOCK = 8


def owners():
    return lax.axis_size("dp") * lax.axis_size("seq")


def staged():
    return owners() == 2 ** (len(STAGES[0]) + 1)


def slot_masks(core):
    masks = [0]
    for bit in STAGES[core]:
        masks = masks + [o ^ bit for o in masks]
    return masks


def slot_owners():
    me = lax.axis_index(ALL)
    even = jnp.array(slot_masks(0) + [1 ^ m for m in slot_masks(1)], jnp.int32)
    odd = jnp.array(slot_masks(1) + [1 ^ m for m in slot_masks(0)], jnp.int32)
    return me ^ jnp.where((me & 1) == 0, even, odd)


def stage_swap(value, stage):
    return lax.ppermute(value, ALL, [(d, d ^ STAGES[d & 1][stage]) for d in range(owners())])


def core_swap(value):
    return lax.ppermute(value, ALL, [(d, d ^ 1) for d in range(owners())])


def place_kernel(groups, rows, order, own, other, out, sem):
    half = own.shape[0]
    for index, ref in enumerate((own, other)):

        def put(slot, carry):
            device = order[index * half + slot]
            for g in range(groups):
                pltpu.make_async_copy(ref.at[slot, pl.ds(g * rows, rows)], out.at[g, device], sem).start()
            return carry

        lax.fori_loop(0, half, put, 0)

    def finish(slot, carry):
        for g in range(groups):
            pltpu.make_async_copy(own.at[0, pl.ds(g * rows, rows)], out.at[g, 0], sem).wait()
        return carry

    lax.fori_loop(0, 2 * half, finish, 0)


def place(own, other, order, groups, rows):
    half, _, _, width = own.shape
    return pl.pallas_call(
        lambda *refs: place_kernel(groups, rows, *refs),
        out_shape=jax.ShapeDtypeStruct((groups, 2 * half, rows, BLOCK, width), BF16),
        in_specs=[pl.BlockSpec(memory_space=pltpu.SMEM)] + [pl.BlockSpec(memory_space=pltpu.VMEM)] * 2,
        out_specs=pl.BlockSpec(memory_space=pl.ANY),
        scratch_shapes=[pltpu.SemaphoreType.DMA],
        cost_estimate=pl.CostEstimate(flops=0, bytes_accessed=4 * own.size * 2, transcendentals=0),
        name="place",
    )(order, own, other)


def spread_kernel(rows, tail, order, *refs):
    terms, (own, other, sem) = refs[:-3], refs[-3:]
    half = own.shape[0]
    sizes = [rows] * (len(terms) - 1) + [tail]
    for index, ref in enumerate((own, other)):

        def put(slot, carry):
            device = order[index * half + slot]
            at = 0
            for term, size in zip(terms, sizes):
                pltpu.make_async_copy(term.at[device], ref.at[slot, pl.ds(at, size)], sem).start()
                at += size
            return carry

        lax.fori_loop(0, half, put, 0)

    def finish(slot, carry):
        at = 0
        for term, size in zip(terms, sizes):
            pltpu.make_async_copy(term.at[0], own.at[0, pl.ds(at, size)], sem).wait()
            at += size
        return carry

    lax.fori_loop(0, 2 * half, finish, 0)


def spread(terms, order):
    devices, rows, _, width = terms[0].shape
    tail = terms[-1].shape[1]
    blocks = rows * (len(terms) - 1) + tail
    shape = jax.ShapeDtypeStruct((devices // 2, blocks, BLOCK, width), BF16)
    return pl.pallas_call(
        lambda *refs: spread_kernel(rows, tail, *refs),
        out_shape=[shape, shape],
        in_specs=[pl.BlockSpec(memory_space=pltpu.SMEM)] + [pl.BlockSpec(memory_space=pltpu.VMEM)] * len(terms),
        out_specs=[pl.BlockSpec(memory_space=pl.ANY)] * 2,
        scratch_shapes=[pltpu.SemaphoreType.DMA],
        cost_estimate=pl.CostEstimate(flops=0, bytes_accessed=4 * shape.size * 2, transcendentals=0),
        name="spread",
    )(order, *terms)


def gather_parts(parts):
    held = [p[None] for p in parts]
    step = len(STAGES[0])
    halves = []
    for g, value in enumerate(held):
        for stage in range(step):
            value = jnp.concatenate([value, stage_swap(value, stage)], axis=0)
        halves.append((value, core_swap(value)))
    return halves


def reduce_slots(own, other):
    total = own.astype(F32) + core_swap(other).astype(F32)
    for stage in reversed(range(len(STAGES[0]))):
        half = total.shape[0] // 2
        got = stage_swap(total[half:].astype(BF16), stage)
        total = total[:half].astype(F32) + got.astype(F32)
    return total[0]


def gather_weights(shards, tail=None):
    rows, width = shards[0].shape
    count = len(shards)
    parts = jnp.concatenate(list(shards) + ([] if tail is None else [tail]), axis=0)
    if not staged():
        whole = lax.all_gather(parts, ALL, axis=0, tiled=False)
        weights = whole[:, : count * rows].reshape(-1, count, rows, width).transpose(1, 0, 2, 3).reshape(count, -1, width)
        return weights, None if tail is None else whole[:, count * rows]
    order = slot_owners()
    own, other = gather_parts([parts.reshape(-1, BLOCK, width)])[0]
    weights = place(own, other, order, count, rows // BLOCK).reshape(count, -1, width)
    if tail is None:
        return weights, None
    tails = jnp.concatenate([own[:, -1, 0], other[:, -1, 0]], axis=0)
    chosen = (order[None, :] == jnp.arange(owners(), dtype=jnp.int32)[:, None]).astype(BF16)
    return weights, dot(chosen, tails)


def reduce_weights(terms, tail=None):
    devices = owners()
    width = terms[0].shape[1]
    parts = [t.astype(BF16).reshape(devices, -1, width) for t in terms]
    rows = parts[0].shape[1]
    if tail is not None:
        parts.append(jnp.pad(tail.astype(BF16)[:, None], ((0, 0), (0, BLOCK - 1), (0, 0))))
    if not staged():
        total = lax.psum_scatter(jnp.concatenate(parts, axis=1), ALL, scatter_dimension=0, tiled=False).astype(F32)
    else:
        own, other = spread([p.reshape(devices, -1, BLOCK, width) for p in parts], slot_owners())
        total = reduce_slots(own, other).reshape(-1, width)
    sums = total[: len(terms) * rows].reshape(len(terms), rows, width)
    return sums, None if tail is None else total[len(terms) * rows]


def per_device(*arrays):
    named = dict(zip(ARGS, arrays))
    target = named["target"][0]
    memory = named["memory"][0]
    local, width = target.shape
    seq = lax.axis_size("seq")
    place = lax.axis_index("seq")
    offsets = seq_offsets(seq)
    block = local

    slab = named["expand_weight"].shape[1] // width
    rows = width // owners()
    vector_count = len(VECTORS)
    vectors = jnp.concatenate([named[n] for n in VECTORS] + [named["expand_bias"]])
    vectors = jnp.pad(vectors, (0, -vectors.shape[0] % width)).reshape(-1, width)
    vectors = jnp.pad(vectors, ((0, 8 - vectors.shape[0]), (0, 0)))
    self_weights, flat = gather_weights([named[n] for n in SELF_WEIGHTS], vectors)
    flat = flat.astype(F32)
    vector_rows = flat[:, : vector_count * rows].reshape(-1, vector_count, rows).transpose(1, 0, 2).reshape(vector_count, width)
    vec = {n: vector_rows[i] for i, n in enumerate(VECTORS)}
    expand_bias = flat[:, vector_count * rows : (vector_count + slab) * rows].reshape(slab, width)
    cross_weights, _ = gather_weights([named[n] for n in CROSS_WEIGHTS])
    expand_parts = named["expand_weight"].reshape(rows, slab, width).transpose(1, 0, 2)
    expand_weights, _ = gather_weights([expand_parts[i] for i in range(slab)])
    shrink_weights, _ = gather_weights([named["shrink_weight"]])
    shrink_weights = shrink_weights.reshape(slab, width, width)

    marks = jnp.stack([named["target_segments"][0], named["memory_segments"][0]]).astype(BF16)
    marks = jnp.pad(marks, ((0, 6), (0, width - local)))
    target_pack = seq_gather(jnp.concatenate([target, marks], axis=0)[None])
    memory_row = seq_gather(memory[None]).reshape(-1, width)
    target_row = target_pack[:, :local].reshape(-1, width)
    key_places = jnp.concatenate([(place ^ o) * local + jnp.arange(local, dtype=jnp.int32) for o in offsets])[None]
    target_marks = target_pack[:, local, :local].reshape(1, -1).astype(jnp.int32)
    memory_marks = target_pack[:, local + 1, :local].reshape(1, -1).astype(jnp.int32)
    own_marks = named["target_segments"].reshape(local, 1)
    start = (place * local).astype(jnp.int32).reshape(1)
    self_masks = (start, own_marks, target_marks, key_places)
    cross_masks = (start, own_marks, memory_marks, jnp.zeros_like(key_places))

    wq, wk, wv, wo = (self_weights[i] for i in range(4))
    wp, wl, wc, wm = (cross_weights[i] for i in range(4))
    query_one = ((dot(target, wq) + vec["query_bias"]) * 0.125).astype(BF16)
    key_one = dot(target_row, wk).astype(BF16)
    value_one = (dot(target_row, wv) + vec["value_bias"]).astype(BF16)
    mixed_one, log_one = attend_forward(query_one, key_one, value_one, self_masks, block)
    first_sum = target.astype(F32) + dot(mixed_one, wo) + vec["output_bias"]
    first_full, normed_one, inverse_one = norm_forward(first_sum, vec["first_gain"], vec["first_shift"])
    first_out = first_full.astype(BF16)
    query_two = ((dot(first_out, wp) + vec["probe_bias"]) * 0.125).astype(BF16)
    key_two = dot(memory_row, wl).astype(BF16)
    value_two = (dot(memory_row, wc) + vec["content_bias"]).astype(BF16)
    mixed_two, log_two = attend_forward(query_two, key_two, value_two, cross_masks, block)
    second_sum = first_out.astype(F32) + dot(mixed_two, wm) + vec["merge_bias"]
    second_full, normed_two, inverse_two = norm_forward(second_sum, vec["second_gain"], vec["second_shift"])
    second_out = second_full.astype(BF16)
    pre_act = [dot(second_out, expand_weights[s]) + expand_bias[s] for s in range(slab)]
    hidden = [exact_gelu(a).astype(BF16) for a in pre_act]
    third_sum = second_out.astype(F32) + sum(dot(h, shrink_weights[s]) for s, h in enumerate(hidden)) + vec["shrink_bias"]
    third_full, normed_three, inverse_three = norm_forward(third_sum, vec["third_gain"], vec["third_shift"])
    layer_output = third_full.astype(BF16)

    grads = {}
    upstream = named["cotangent"][0].astype(F32)
    third_grad, grads["third_gain"], grads["third_shift"] = norm_backward(upstream, normed_three, inverse_three, vec["third_gain"])
    shrink_in = third_grad.astype(BF16)
    shrink_grads = [t_dot(h, shrink_in).astype(BF16) for h in hidden]
    grads["shrink_bias"] = token_sum(shrink_in)
    act_grads = []
    for s in range(slab):
        hidden_grad = dot_t(shrink_in, shrink_weights[s])
        act_grads.append(jax.vjp(exact_gelu, pre_act[s])[1](hidden_grad)[0].astype(BF16))
    expand_grads = [t_dot(second_out, a).astype(BF16) for a in act_grads]
    expand_bias_grad = jnp.stack([token_sum(a) for a in act_grads])
    second_grad = third_grad + sum(dot_t(a, expand_weights[s]) for s, a in enumerate(act_grads))
    second_sum_grad, grads["second_gain"], grads["second_shift"] = norm_backward(second_grad, normed_two, inverse_two, vec["second_gain"])
    merge_in = second_sum_grad.astype(BF16)
    grads["merge_bias"] = token_sum(merge_in)
    mixed_two_grad = dot_t(merge_in, wm).astype(BF16)
    probe_in, lookup_part, content_part = attend_backward(query_two, key_two, value_two, mixed_two_grad, log_two, cross_masks, block)
    grads["probe_bias"] = token_sum(probe_in)
    grads["content_bias"] = token_sum(content_part)
    cross_grads = [t_dot(first_out, probe_in), t_dot(memory_row, lookup_part), t_dot(memory_row, content_part), t_dot(mixed_two, merge_in)]
    memory_part = dot_t(lookup_part, wl) + dot_t(content_part, wc)
    memory_grad = seq_reduce(memory_part.reshape(seq, local, width))
    first_grad = second_sum_grad + dot_t(probe_in, wp)
    first_sum_grad, grads["first_gain"], grads["first_shift"] = norm_backward(first_grad, normed_one, inverse_one, vec["first_gain"])
    output_in = first_sum_grad.astype(BF16)
    grads["output_bias"] = token_sum(output_in)
    mixed_one_grad = dot_t(output_in, wo).astype(BF16)
    query_in, key_part, value_part = attend_backward(query_one, key_one, value_one, mixed_one_grad, log_one, self_masks, block)
    grads["query_bias"] = token_sum(query_in)
    grads["value_bias"] = token_sum(value_part)
    self_grads = [t_dot(target, query_in), t_dot(target_row, key_part), t_dot(target_row, value_part), t_dot(mixed_one, output_in)]
    target_part = dot_t(key_part, wk) + dot_t(value_part, wv)
    target_grad = first_sum_grad + dot_t(query_in, wq) + seq_reduce(target_part.reshape(seq, local, width))

    vector_grads = jnp.stack([grads[n] for n in VECTORS]).astype(BF16).reshape(vector_count, owners(), rows)
    vector_grads = jnp.concatenate(
        [vector_grads.transpose(1, 0, 2).reshape(owners(), -1), expand_bias_grad.astype(BF16).reshape(owners(), -1)], axis=1
    )
    vector_grads = jnp.pad(vector_grads, ((0, 0), (0, width - vector_grads.shape[1])))
    shrink_sum, _ = reduce_weights([jnp.concatenate(shrink_grads, axis=0)])
    expand_sum, _ = reduce_weights(expand_grads)
    cross_sum, _ = reduce_weights(cross_grads)
    self_sum, vector_sum = reduce_weights(self_grads, vector_grads)
    result = {n: self_sum[i] for i, n in enumerate(SELF_WEIGHTS)}
    result.update({n: cross_sum[i] for i, n in enumerate(CROSS_WEIGHTS)})
    result.update({n: vector_sum[i * rows : (i + 1) * rows] for i, n in enumerate(VECTORS)})
    result["expand_bias"] = vector_sum[vector_count * rows : (vector_count + slab) * rows]
    result["expand_weight"] = expand_sum.transpose(1, 0, 2).reshape(rows, slab * width)
    result["shrink_weight"] = shrink_sum[0]
    return (layer_output[None], target_grad[None], memory_grad[None]) + tuple(result[n] for n in ARGS[5:])


def solution(mesh):
    tokens = P("dp", "seq", None)
    matrix = P(ALL, None)
    vector = P(ALL)
    params = tuple(matrix if n.endswith("_weight") else vector for n in ARGS[5:])
    return jax.shard_map(
        per_device,
        mesh=mesh,
        in_specs=(tokens, tokens, tokens, P("dp", "seq"), P("dp", "seq")) + params,
        out_specs=(tokens, tokens, tokens) + params,
        check_vma=False,
    )
```

```python
from typing import Any, NamedTuple

import jax
import jax.numpy as jnp
from jax import lax
from jax.experimental import pallas as pl
from jax.experimental.pallas import tpu as pltpu
from jax.sharding import PartitionSpec as P

HEAD_DIM = 64
PAIR = 2 * HEAD_DIM
NEG_FILL = -1e30
EPSILON = 1e-05
BF16 = jnp.bfloat16
F32 = jnp.float32
ALL = ("dp", "seq")

class Params(NamedTuple):
    query_weight: Any
    query_bias: Any
    key_weight: Any
    value_weight: Any
    value_bias: Any
    output_weight: Any
    output_bias: Any
    first_gain: Any
    first_shift: Any
    probe_weight: Any
    probe_bias: Any
    lookup_weight: Any
    content_weight: Any
    content_bias: Any
    merge_weight: Any
    merge_bias: Any
    second_gain: Any
    second_shift: Any
    expand_weight: Any
    expand_bias: Any
    shrink_weight: Any
    shrink_bias: Any
    third_gain: Any
    third_shift: Any


def vectors_of(p):
    return (
        p.query_bias,
        p.value_bias,
        p.output_bias,
        p.first_gain,
        p.first_shift,
        p.probe_bias,
        p.content_bias,
        p.merge_bias,
        p.second_gain,
        p.second_shift,
        p.shrink_bias,
        p.third_gain,
        p.third_shift,
    )


VECTORS = 13
LANES = 128


def dot(left, right):
    return jnp.dot(left, right, preferred_element_type=F32)


def dot_t(left, right):
    return lax.dot_general(left, right, (((1,), (1,)), ((), ())), preferred_element_type=F32)


def t_dot(left, right):
    return lax.dot_general(left, right, (((0,), (0,)), ((), ())), preferred_element_type=F32)


def token_sum(values):
    return jnp.sum(values.astype(F32), axis=0, keepdims=True)


def fill_mask(block, q0_ref, qseg_ref, kseg_ref, kpos_ref, bias, flags):
    rows = bias.shape[0]
    place = q0_ref[0] + lax.broadcasted_iota(jnp.int32, (rows, block), 0)
    for j in range(bias.shape[1] // block):
        cols = pl.ds(j * block, block)
        allowed = (kseg_ref[:, cols] == qseg_ref[...]) & (kpos_ref[:, cols] <= place)
        term = jnp.where(allowed, 0.0, NEG_FILL)
        bias[:, cols] = term
        flags[j] = (jnp.max(term) > -1.0).astype(jnp.int32)


def one_head(value, head):
    lane = lax.broadcasted_iota(jnp.int32, value.shape, 1)
    return jnp.where((lane < HEAD_DIM) == (head == 0), value, jnp.zeros_like(value))


def attend_kernel(block, q0_ref, q_ref, k_ref, v_ref, qseg_ref, kseg_ref, kpos_ref, o_ref, log_ref, bias, flags, scores, weights, sums):
    blocks = bias.shape[1] // block

    @pl.when(pl.program_id(0) == 0)
    def _():
        fill_mask(block, q0_ref, qseg_ref, kseg_ref, kpos_ref, bias, flags)
        scores[...] = jnp.full(scores.shape, NEG_FILL, F32)
        weights[...] = jnp.zeros(weights.shape, BF16)

    outs = []
    logs = []
    for head in range(2):
        query = one_head(q_ref[...], head)
        for j in range(blocks):

            @pl.when(flags[j] > 0)
            def _():
                cols = pl.ds(j * block, block)
                scores[:, cols] = dot_t(query, k_ref[cols, :]) + bias[:, cols]

        peak = jnp.max(scores[...], axis=-1, keepdims=True)
        sums[...] = jnp.zeros(sums.shape, F32)
        for j in range(blocks):

            @pl.when(flags[j] > 0)
            def _():
                cols = pl.ds(j * block, block)
                part = jnp.exp(scores[:, cols] - peak)
                sums[...] += jnp.sum(part, axis=-1, keepdims=True)
                weights[:, cols] = part.astype(BF16)

        total = sums[...]
        outs.append(dot(weights[...], v_ref[...]) * (1.0 / total))
        logs.append(peak + jnp.log(total))
    lane = lax.broadcasted_iota(jnp.int32, o_ref.shape, 1)
    o_ref[...] = jnp.where(lane < HEAD_DIM, outs[0], outs[1]).astype(BF16)
    log_ref[...] = jnp.where(lane < HEAD_DIM, logs[0], logs[1])


def attend_back_kernel(block, q0_ref, q_ref, k_ref, v_ref, g_ref, log_ref, qseg_ref, kseg_ref, kpos_ref, dq_ref, dk_ref, dv_ref, bias, flags, probs, slopes, score_grads, weights, along):
    rows = bias.shape[0]
    blocks = bias.shape[1] // block

    @pl.when(pl.program_id(0) == 0)
    def _():
        fill_mask(block, q0_ref, qseg_ref, kseg_ref, kpos_ref, bias, flags)
        score_grads[...] = jnp.zeros(score_grads.shape, BF16)

    queries = []
    grads = []
    for head in range(2):
        query = one_head(q_ref[...], head)
        grad = one_head(g_ref[...], head)
        queries.append(query)
        grads.append(grad)
        log = log_ref[:, head * HEAD_DIM : head * HEAD_DIM + 1]
        along[...] = jnp.zeros(along.shape, F32)
        own = pl.ds(head * rows, rows)
        for j in range(blocks):

            @pl.when(flags[j] > 0)
            def _():
                cols = pl.ds(j * block, block)
                part = jnp.exp(dot_t(query, k_ref[cols, :]) + bias[:, cols] - log)
                slope = dot_t(grad, v_ref[cols, :])
                probs[:, cols] = part
                slopes[:, cols] = slope
                weights[own, cols] = part.astype(BF16)
                along[...] += jnp.sum(part * slope, axis=-1, keepdims=True)

        inner = along[...]
        for j in range(blocks):

            @pl.when(flags[j] > 0)
            def _():
                cols = pl.ds(j * block, block)
                score_grads[own, cols] = (probs[:, cols] * (slopes[:, cols] - inner)).astype(BF16)

    both_queries = jnp.concatenate(queries, axis=0)
    both_grads = jnp.concatenate(grads, axis=0)
    for j in range(blocks):
        cols = pl.ds(j * block, block)

        @pl.when(flags[j] > 0)
        def _():
            dk_ref[cols, :] = t_dot(score_grads[:, cols], both_queries).astype(BF16)
            dv_ref[cols, :] = t_dot(weights[:, cols], both_grads).astype(BF16)

        @pl.when(flags[j] == 0)
        def _():
            dk_ref[cols, :] = jnp.zeros((block, PAIR), BF16)
            dv_ref[cols, :] = jnp.zeros((block, PAIR), BF16)

    lane = lax.broadcasted_iota(jnp.int32, dq_ref.shape, 1)
    both = dot(score_grads[...], k_ref[...])
    dq_ref[...] = (jnp.where(lane < HEAD_DIM, both[:rows], both[rows:]).astype(BF16) * 0.125).astype(BF16)


def attend_specs(rows, total):
    whole = lambda shape: pl.BlockSpec(shape, lambda i: (0, 0))
    strip = lambda count: pl.BlockSpec((count, PAIR), lambda i: (0, i))
    return (
        pl.BlockSpec(memory_space=pltpu.SMEM),
        strip(rows),
        strip(total),
        [whole((rows, 1)), whole((1, total)), whole((1, total))],
    )


def attend_forward(query, key, value, masks, block):
    rows, width = query.shape
    total = key.shape[0]
    scalar, narrow, tall, marks = attend_specs(rows, total)
    q0, qseg, kseg, kpos = masks
    return pl.pallas_call(
        lambda *refs: attend_kernel(block, *refs),
        grid=(width // PAIR,),
        in_specs=[scalar, narrow, tall, tall] + marks,
        out_specs=[narrow, narrow],
        out_shape=[jax.ShapeDtypeStruct((rows, width), BF16), jax.ShapeDtypeStruct((rows, width), F32)],
        scratch_shapes=[
            pltpu.VMEM((rows, total), F32),
            pltpu.SMEM((total // block,), jnp.int32),
            pltpu.VMEM((rows, total), F32),
            pltpu.VMEM((rows, total), BF16),
            pltpu.VMEM((rows, 1), F32),
        ],
        cost_estimate=pl.CostEstimate(flops=8 * rows * total * width, bytes_accessed=8 * total * width, transcendentals=rows * total * 12),
        compiler_params=pltpu.CompilerParams(dimension_semantics=("arbitrary",)),
        name="attend_forward",
    )(q0, query, key, value, qseg, kseg, kpos)


def attend_backward(query, key, value, grad, log, masks, block):
    rows, width = query.shape
    total = key.shape[0]
    scalar, narrow, tall, marks = attend_specs(rows, total)
    q0, qseg, kseg, kpos = masks
    return pl.pallas_call(
        lambda *refs: attend_back_kernel(block, *refs),
        grid=(width // PAIR,),
        in_specs=[scalar, narrow, tall, tall, narrow, narrow] + marks,
        out_specs=[narrow, tall, tall],
        out_shape=[
            jax.ShapeDtypeStruct((rows, width), BF16),
            jax.ShapeDtypeStruct((total, width), BF16),
            jax.ShapeDtypeStruct((total, width), BF16),
        ],
        scratch_shapes=[
            pltpu.VMEM((rows, total), F32),
            pltpu.SMEM((total // block,), jnp.int32),
            pltpu.VMEM((rows, total), F32),
            pltpu.VMEM((rows, total), F32),
            pltpu.VMEM((2 * rows, total), BF16),
            pltpu.VMEM((2 * rows, total), BF16),
            pltpu.VMEM((rows, 1), F32),
        ],
        cost_estimate=pl.CostEstimate(flops=20 * rows * total * width, bytes_accessed=16 * total * width, transcendentals=rows * total * 12),
        compiler_params=pltpu.CompilerParams(dimension_semantics=("arbitrary",)),
        name="attend_backward",
    )(q0, query, key, value, grad, log, qseg, kseg, kpos)


def norm_forward(hidden, gain, shift):
    centred = hidden - jnp.mean(hidden, axis=-1, keepdims=True)
    inverse = lax.rsqrt(jnp.mean(centred * centred, axis=-1, keepdims=True) + EPSILON)
    normed = centred * inverse
    return normed * gain + shift, normed, inverse


def norm_backward(upstream, normed, inverse, gain):
    scaled = upstream * gain
    inner = jnp.mean(scaled, axis=-1, keepdims=True)
    along = jnp.mean(scaled * normed, axis=-1, keepdims=True)
    return inverse * (scaled - inner - normed * along), token_sum(upstream * normed), token_sum(upstream)


def exact_gelu(values):
    return jax.nn.gelu(values, approximate=False)


def seq_offsets(count):
    offsets = [0]
    bit = count // 2
    while bit:
        offsets = offsets + [o ^ bit for o in offsets]
        bit //= 2
    return offsets


def swap(value, axis, bit):
    count = lax.axis_size(axis)
    return lax.ppermute(value, axis, [(i, i ^ bit) for i in range(count)])


def seq_bits():
    bit = lax.axis_size("seq") // 2
    bits = []
    while bit:
        bits.append(bit)
        bit //= 2
    return bits


def seq_gather(rows, bits):
    for bit in bits:
        rows = jnp.concatenate([rows, swap(rows, "seq", bit)], axis=0)
    return rows


def seq_reduce(total, bits):
    for bit in bits:
        half = total.shape[0] // 2
        got = swap(total[half:].astype(BF16), "seq", bit)
        total = total[:half].astype(F32) + got.astype(F32)
    return total


def tie(*values):
    return lax.optimization_barrier(values)


NEAR_LAST = ((16, 8, 2, 4), (8, 16, 4, 2))
NEAR_FIRST = ((2, 4, 8, 16), (4, 2, 16, 8))
BLOCK = 8


def owners():
    return lax.axis_size("dp") * lax.axis_size("seq")


def staged():
    return owners() == 2 ** (len(NEAR_LAST[0]) + 1)


def slot_owners(plan):
    def masks(core):
        found = [0]
        for bit in plan[core]:
            found = found + [o ^ bit for o in found]
        return found

    me = lax.axis_index(ALL)
    even = jnp.array(masks(0) + [1 ^ m for m in masks(1)], jnp.int32)
    odd = jnp.array(masks(1) + [1 ^ m for m in masks(0)], jnp.int32)
    return me ^ jnp.where((me & 1) == 0, even, odd)


def stage_swap(value, plan, stage):
    return lax.ppermute(value, ALL, [(d, d ^ plan[d & 1][stage]) for d in range(owners())])


def core_swap(value):
    return lax.ppermute(value, ALL, [(d, d ^ 1) for d in range(owners())])


def place_kernel(groups, rows, counts, order, *refs):
    pieces, refs = refs[: len(counts)], refs[len(counts) :]
    outs, (held, came, left) = refs[:-3], refs[-3:]
    blocks = held.shape[1]
    sizes = [rows] * groups + [blocks - groups * rows] * (len(outs) - groups)
    base = 0
    for piece, count in zip(pieces, counts):

        def fetch(slot, carry):
            pltpu.make_async_copy(piece.at[slot], held.at[base + slot], came.at[base + slot]).start()
            return carry

        lax.fori_loop(0, count, fetch, 0)
        base += count

    def put(slot, carry):
        pltpu.make_async_copy(pieces[0].at[0], held.at[slot], came.at[slot]).wait()
        at = 0
        for out, size in zip(outs, sizes):
            pltpu.make_async_copy(held.at[slot, pl.ds(at, size)], out.at[order[slot]], left).start()
            at += size
        return carry

    lax.fori_loop(0, base, put, 0)

    def finish(slot, carry):
        at = 0
        for out, size in zip(outs, sizes):
            pltpu.make_async_copy(held.at[slot, pl.ds(at, size)], out.at[slot], left).wait()
            at += size
        return carry

    lax.fori_loop(0, base, finish, 0)


def place(pieces, order, groups, rows):
    counts = tuple(p.shape[0] for p in pieces)
    _, blocks, _, width = pieces[0].shape
    devices = sum(counts)
    sizes = [rows] * groups + [blocks - groups * rows] * (blocks > groups * rows)
    anywhere = pl.BlockSpec(memory_space=pl.ANY)
    return pl.pallas_call(
        lambda *refs: place_kernel(groups, rows, counts, *refs),
        out_shape=[jax.ShapeDtypeStruct((devices, size, BLOCK, width), BF16) for size in sizes],
        in_specs=[pl.BlockSpec(memory_space=pltpu.SMEM)] + [anywhere] * len(pieces),
        out_specs=[anywhere] * len(sizes),
        scratch_shapes=[
            pltpu.VMEM((devices, blocks, BLOCK, width), BF16),
            pltpu.SemaphoreType.DMA((devices,)),
            pltpu.SemaphoreType.DMA,
        ],
        cost_estimate=pl.CostEstimate(flops=0, bytes_accessed=4 * devices * blocks * BLOCK * width, transcendentals=0),
        name="place",
    )(order, *pieces)


def spread_kernel(sizes, order, *refs):
    terms, refs = refs[: len(sizes)], refs[len(sizes) :]
    outs, (held, came, left) = refs[:2], refs[2:]
    half = outs[0].shape[0]
    spans = [pl.ds(sum(sizes[:i]), size) for i, size in enumerate(sizes)]
    for i, term in enumerate(terms):
        pltpu.make_async_copy(term, held.at[:, spans[i]], came.at[i]).start()
    for i, term in enumerate(terms):
        pltpu.make_async_copy(term, held.at[:, spans[i]], came.at[i]).wait()
        for index, out in enumerate(outs):

            def put(slot, carry):
                pltpu.make_async_copy(held.at[order[index * half + slot], spans[i]], out.at[slot, spans[i]], left).start()
                return carry

            lax.fori_loop(0, half, put, 0)

    def finish(slot, carry):
        for out in outs:
            for span in spans:
                pltpu.make_async_copy(held.at[slot, span], out.at[slot, span], left).wait()
        return carry

    lax.fori_loop(0, half, finish, 0)


def spread(terms, order):
    devices, _, _, width = terms[0].shape
    sizes = tuple(t.shape[1] for t in terms)
    blocks = sum(sizes)
    shape = jax.ShapeDtypeStruct((devices // 2, blocks, BLOCK, width), BF16)
    anywhere = pl.BlockSpec(memory_space=pl.ANY)
    return pl.pallas_call(
        lambda *refs: spread_kernel(sizes, *refs),
        out_shape=[shape, shape],
        in_specs=[pl.BlockSpec(memory_space=pltpu.SMEM)] + [anywhere] * len(terms),
        out_specs=[anywhere] * 2,
        scratch_shapes=[
            pltpu.VMEM((devices, blocks, BLOCK, width), BF16),
            pltpu.SemaphoreType.DMA((len(sizes),)),
            pltpu.SemaphoreType.DMA,
        ],
        cost_estimate=pl.CostEstimate(flops=0, bytes_accessed=4 * devices * blocks * BLOCK * width, transcendentals=0),
        name="spread",
    )(order, *terms)


def seat(index):
    return index % BLOCK, LANES * (index // BLOCK)


def pack_vectors_kernel(*refs):
    out, held = refs[-2:]
    held[...] = jnp.zeros(held.shape, F32)
    for i, ref in enumerate(refs[:-2]):
        row, lane = seat(i)
        held[row : row + 1, lane : lane + ref.shape[1]] = ref[...].astype(F32)
    out[...] = held[...].astype(BF16)


def pack_vectors(vectors, width):
    return pl.pallas_call(
        pack_vectors_kernel,
        out_shape=jax.ShapeDtypeStruct((BLOCK, width), BF16),
        in_specs=[pl.BlockSpec(memory_space=pltpu.VMEM)] * len(vectors),
        out_specs=pl.BlockSpec(memory_space=pltpu.VMEM),
        scratch_shapes=[pltpu.VMEM((BLOCK, width), F32)],
        name="pack_vectors",
    )(*[v.reshape(1, -1) for v in vectors])


def unpack_vectors_kernel(blocks, out, wide):
    rows = out.shape[1] // blocks.shape[0]
    span = wide.shape[1] // blocks.shape[0]
    row, lane = seat(VECTORS)
    for d in range(blocks.shape[0]):
        for half in range(2):
            part = blocks[d, :, LANES * half : LANES * (half + 1)].astype(F32)
            out[half * BLOCK : (half + 1) * BLOCK, d * rows : (d + 1) * rows] = part[:, :rows]
            if half == lane // LANES:
                wide[:, d * span : (d + 1) * span] = part[row : row + 1, :span]


def unpack_vectors(blocks, width, wide):
    return pl.pallas_call(
        unpack_vectors_kernel,
        grid=(1,),
        in_specs=[pl.BlockSpec((blocks.shape[0], BLOCK, 2 * LANES), lambda i: (0, 0, 0))],
        out_specs=[pl.BlockSpec((2 * BLOCK, width), lambda i: (0, 0)), pl.BlockSpec((1, wide), lambda i: (0, 0))],
        out_shape=[jax.ShapeDtypeStruct((2 * BLOCK, width), F32), jax.ShapeDtypeStruct((1, wide), F32)],
        name="unpack_vectors",
    )(blocks)


def pack_sums_kernel(*refs):
    out = refs[-1]
    vectors, wide = refs[:-2], refs[-2]
    devices = out.shape[0]
    rows = vectors[0].shape[1] // devices
    span = wide.shape[1] // devices
    table = jnp.concatenate([v[...] for v in vectors] + [jnp.zeros((2 * BLOCK - len(vectors), vectors[0].shape[1]), F32)], axis=0)
    row, lane = seat(VECTORS)
    blank = jnp.zeros((BLOCK, LANES - rows), F32)
    empty = jnp.zeros((BLOCK, out.shape[2] - 2 * LANES), F32)
    line = lax.broadcasted_iota(jnp.int32, (BLOCK, LANES), 0)
    for d in range(devices):
        parts = [table[half * BLOCK : (half + 1) * BLOCK, d * rows : (d + 1) * rows] for half in range(2)]
        parts = [jnp.concatenate([part, blank], axis=1) for part in parts]
        strip = jnp.concatenate([wide[:, d * span : (d + 1) * span], jnp.zeros((1, LANES - span), F32)], axis=1)
        parts[lane // LANES] = jnp.where(line == row, strip, parts[lane // LANES])
        out[d] = jnp.concatenate(parts + [empty], axis=1).astype(BF16)


def pack_sums(vectors, wide, width):
    return pl.pallas_call(
        pack_sums_kernel,
        out_shape=jax.ShapeDtypeStruct((owners(), BLOCK, width), BF16),
        in_specs=[pl.BlockSpec(memory_space=pltpu.VMEM)] * (len(vectors) + 1),
        out_specs=pl.BlockSpec(memory_space=pltpu.VMEM),
        name="pack_sums",
    )(*vectors, wide)


def gather_start(shards):
    parts = jnp.concatenate(list(shards), axis=0) if len(shards) > 1 else shards[0]
    return parts.reshape(1, -1, BLOCK, parts.shape[1]) if staged() else parts


def gather_step(value, plan, stage):
    return jnp.concatenate([value, stage_swap(value, plan, stage)], axis=0) if staged() else value


def gather_last(value, plan):
    return (value, stage_swap(value, plan, len(plan[0]) - 1)) if staged() else (value,)


def gather_finish(halves):
    return halves + tuple(core_swap(h) for h in halves) if staged() else (lax.all_gather(halves[0], ALL, axis=0, tiled=False),)


def unpack(pieces, plan, count, rows):
    width = pieces[0].shape[-1]
    if not staged():
        whole = pieces[0]
        weights = [whole[:, i * rows : (i + 1) * rows].reshape(-1, width) for i in range(count)]
        return weights + [whole[:, count * rows :]]
    found = place(pieces, slot_owners(plan), count, rows // BLOCK)
    return [w.reshape(-1, width) for w in found[:count]] + [t.reshape(-1, BLOCK, width) for t in found[count:]]


def reduce_start(terms, plan, tail=None):
    devices = owners()
    width = terms[0].shape[1]
    parts = [t.astype(BF16).reshape(devices, -1, width) for t in terms]
    if tail is not None:
        parts.append(tail)
    if not staged():
        return (jnp.concatenate(parts, axis=1),) * 2
    return tuple(spread([p.reshape(devices, -1, BLOCK, width) for p in parts], slot_owners(plan)))


def add_halves(mine, got):
    half = mine.shape[0] // 2
    add = lambda a, b: (a.astype(F32) + b.astype(F32)).astype(BF16)
    return add(mine[:half], got[:half]), add(mine[half:], got[half:])


def reduce_core(halves):
    own, other = halves
    return add_halves(own, core_swap(other)) if staged() else (own, own)


def reduce_step(pair, plan, stage):
    if not staged():
        return pair
    got = stage_swap(pair[1], plan, stage)
    if stage:
        return add_halves(pair[0], got)
    return (pair[0].astype(F32) + got.astype(F32),) * 2


def reduce_finish(pair):
    if staged():
        return pair[0].reshape(-1, pair[0].shape[-1])
    return lax.psum_scatter(pair[0], ALL, scatter_dimension=0, tiled=False).astype(F32)


def per_device(target, memory, cotangent, target_segments, memory_segments, *shards):
    p = Params(*shards)
    target = target[0]
    memory = memory[0]
    local, width = target.shape
    seq = lax.axis_size("seq")
    place_in_row = lax.axis_index("seq")
    offsets = seq_offsets(seq)
    bits = seq_bits()
    block = local
    rows = p.query_weight.shape[0]
    wide = p.expand_weight.shape[1]
    last = NEAR_LAST

    expand_weight = lax.all_gather(p.expand_weight, ALL, axis=0, tiled=True)
    shrink_weight = lax.all_gather(p.shrink_weight, ALL, axis=0, tiled=True)
    vectors = pack_vectors(vectors_of(p) + (p.expand_bias,), width)
    one = gather_start([p.query_weight, p.key_weight, p.value_weight, p.output_weight, vectors])
    two = gather_start([p.probe_weight, p.lookup_weight, p.content_weight, p.merge_weight])
    marks = jnp.stack([target_segments[0], memory_segments[0]]).astype(BF16)
    marks = jnp.pad(marks, ((0, BLOCK - 2), (0, width - local)))
    target_pack = jnp.concatenate([target, marks], axis=0)[None]
    memory_row = memory[None]
    one = gather_step(one, last, 0)
    target_pack = seq_gather(target_pack, bits[:1])
    one, target_pack, two = tie(one, target_pack, two)
    one = gather_step(one, last, 1)
    target_pack = seq_gather(target_pack, bits[1:])
    one, target_pack, two = tie(one, target_pack, two)
    one = gather_step(one, last, 2)
    two = gather_step(two, last, 0)
    target_row = target_pack[:, :local].reshape(-1, width)
    key_places = jnp.concatenate([(place_in_row ^ o) * local + jnp.arange(local, dtype=jnp.int32) for o in offsets])[None]
    target_marks = target_pack[:, local, :local].reshape(1, -1).astype(jnp.int32)
    memory_marks = target_pack[:, local + 1, :local].reshape(1, -1).astype(jnp.int32)
    own_marks = target_segments.reshape(local, 1)
    start = (place_in_row * local).astype(jnp.int32).reshape(1)
    self_masks = (start, own_marks, target_marks, key_places)
    cross_masks = (start, own_marks, memory_marks, jnp.zeros_like(key_places))
    one, two = tie(one, two)
    one = gather_last(one, last)
    two = gather_step(two, last, 1)
    one, two, memory_row = tie(one, two, memory_row)

    wq, wk, wv, wo, blocks = unpack(gather_finish(one), last, 4, rows)
    two = gather_step(two, last, 2)
    memory_row = seq_gather(memory_row, bits[:1])
    named, expand_bias = unpack_vectors(blocks, width, wide)
    (
        query_bias,
        value_bias,
        output_bias,
        first_gain,
        first_shift,
        probe_bias,
        content_bias,
        merge_bias,
        second_gain,
        second_shift,
        shrink_bias,
        third_gain,
        third_shift,
    ) = (named[i : i + 1] for i in range(VECTORS))
    query_one = ((dot(target, wq) + query_bias) * 0.125).astype(BF16)
    key_one = dot(target_row, wk).astype(BF16)
    value_one = (dot(target_row, wv) + value_bias).astype(BF16)
    query_one, key_one, value_one, two, memory_row = tie(query_one, key_one, value_one, two, memory_row)
    mixed_one, log_one = attend_forward(query_one, key_one, value_one, self_masks, block)
    two = gather_last(two, last)
    memory_row = seq_gather(memory_row, bits[1:]).reshape(-1, width)
    mixed_one, log_one, two, memory_row = tie(mixed_one, log_one, two, memory_row)
    first_sum = target.astype(F32) + dot(mixed_one, wo) + output_bias
    first_full, normed_one, inverse_one = norm_forward(first_sum, first_gain, first_shift)
    first_out = first_full.astype(BF16)
    wp, wl, wc, wm, *_ = unpack(gather_finish(two), last, 4, rows)
    query_two = ((dot(first_out, wp) + probe_bias) * 0.125).astype(BF16)
    key_two = dot(memory_row, wl).astype(BF16)
    value_two = (dot(memory_row, wc) + content_bias).astype(BF16)
    mixed_two, log_two = attend_forward(query_two, key_two, value_two, cross_masks, block)
    second_sum = first_out.astype(F32) + dot(mixed_two, wm) + merge_bias
    second_full, normed_two, inverse_two = norm_forward(second_sum, second_gain, second_shift)
    second_out = second_full.astype(BF16)
    pre_act = dot(second_out, expand_weight) + expand_bias
    hidden = exact_gelu(pre_act).astype(BF16)
    third_sum = second_out.astype(F32) + dot(hidden, shrink_weight) + shrink_bias
    third_full, normed_three, inverse_three = norm_forward(third_sum, third_gain, third_shift)
    layer_output = third_full.astype(BF16)

    upstream = cotangent[0].astype(F32)
    third_grad, third_gain_grad, third_shift_grad = norm_backward(upstream, normed_three, inverse_three, third_gain)
    shrink_in = third_grad.astype(BF16)
    shrink_bias_grad = token_sum(shrink_in)
    shrink_grad = t_dot(hidden, shrink_in).astype(BF16)
    shrink_grad, shrink_in, third_grad = tie(shrink_grad, shrink_in, third_grad)
    four = lax.psum_scatter(shrink_grad, ALL, scatter_dimension=0, tiled=True).astype(F32)
    hidden_grad = dot_t(shrink_in, shrink_weight)
    act_grad = jax.vjp(exact_gelu, pre_act)[1](hidden_grad)[0].astype(BF16)
    expand_bias_grad = token_sum(act_grad)
    three = reduce_start([t_dot(second_out, act_grad)], last)
    three, act_grad, third_grad = tie(three, act_grad, third_grad)
    three = reduce_core(three)
    second_grad = third_grad + dot_t(act_grad, expand_weight)
    second_sum_grad, second_gain_grad, second_shift_grad = norm_backward(second_grad, normed_two, inverse_two, second_gain)
    merge_in = second_sum_grad.astype(BF16)
    merge_bias_grad = token_sum(merge_in)
    mixed_two_grad = dot_t(merge_in, wm).astype(BF16)
    mixed_two_grad, three = tie(mixed_two_grad, three)
    three = reduce_step(three, last, 3)
    probe_in, lookup_part, content_part = attend_backward(query_two, key_two, value_two, mixed_two_grad, log_two, cross_masks, block)
    probe_in, lookup_part, content_part, three = tie(probe_in, lookup_part, content_part, three)
    three = reduce_step(three, last, 2)
    probe_bias_grad = token_sum(probe_in)
    content_bias_grad = token_sum(content_part)
    cross_grads = [t_dot(first_out, probe_in), t_dot(memory_row, lookup_part), t_dot(memory_row, content_part), t_dot(mixed_two, merge_in)]
    two = reduce_start(cross_grads, last)
    first_grad = second_sum_grad + dot_t(probe_in, wp)
    first_sum_grad, first_gain_grad, first_shift_grad = norm_backward(first_grad, normed_one, inverse_one, first_gain)
    output_in = first_sum_grad.astype(BF16)
    output_bias_grad = token_sum(output_in)
    mixed_one_grad = dot_t(output_in, wo).astype(BF16)
    two, three, lookup_part, content_part = tie(two, three, lookup_part, content_part)
    two = reduce_core(two)
    three = reduce_step(three, last, 1)
    memory_part = (dot_t(lookup_part, wl) + dot_t(content_part, wc)).reshape(seq, local, width)
    mixed_one_grad, two, three, memory_part = tie(mixed_one_grad, two, three, memory_part)
    two = reduce_step(two, last, 3)
    three = reduce_step(three, last, 0)
    query_in, key_part, value_part = attend_backward(query_one, key_one, value_one, mixed_one_grad, log_one, self_masks, block)
    query_in, key_part, value_part, two, three, memory_part = tie(query_in, key_part, value_part, two, three, memory_part)
    two = reduce_step(two, last, 2)
    memory_part = seq_reduce(memory_part, bits[:0:-1])
    query_bias_grad = token_sum(query_in)
    value_bias_grad = token_sum(value_part)
    self_grads = [t_dot(target, query_in), t_dot(target_row, key_part), t_dot(target_row, value_part), t_dot(mixed_one, output_in)]
    vector_grads = (
        query_bias_grad,
        value_bias_grad,
        output_bias_grad,
        first_gain_grad,
        first_shift_grad,
        probe_bias_grad,
        content_bias_grad,
        merge_bias_grad,
        second_gain_grad,
        second_shift_grad,
        shrink_bias_grad,
        third_gain_grad,
        third_shift_grad,
    )
    one = reduce_start(self_grads, last, pack_sums(vector_grads, expand_bias_grad, width))
    one, two, memory_part, key_part, value_part, query_in = tie(one, two, memory_part, key_part, value_part, query_in)
    one = reduce_core(one)
    two = reduce_step(two, last, 1)
    target_part = (dot_t(key_part, wk) + dot_t(value_part, wv)).reshape(seq, local, width)
    one, two, memory_part, target_part = tie(one, two, memory_part, target_part)
    one = reduce_step(one, last, 3)
    two = reduce_step(two, last, 0)
    target_part = seq_reduce(target_part, bits[:0:-1])
    target_grad = first_sum_grad + dot_t(query_in, wq)
    one, memory_part, target_part, target_grad = tie(one, memory_part, target_part, target_grad)
    one = reduce_step(one, last, 2)
    memory_grad = seq_reduce(memory_part, bits[:1])[0]
    one, target_part, memory_grad = tie(one, target_part, memory_grad)
    one = reduce_step(one, last, 1)
    target_grad = target_grad + seq_reduce(target_part, bits[:1])[0]
    one = reduce_step(one, last, 0)

    one, two, three = (reduce_finish(t) for t in (one, two, three))
    wide_sum = one[4 * rows :]
    sums = [wide_sum[seat(i)[0], seat(i)[1] : seat(i)[1] + rows] for i in range(VECTORS)]
    row, lane = seat(VECTORS)
    result = Params(
        query_weight=one[:rows],
        key_weight=one[rows : 2 * rows],
        value_weight=one[2 * rows : 3 * rows],
        output_weight=one[3 * rows : 4 * rows],
        probe_weight=two[:rows],
        lookup_weight=two[rows : 2 * rows],
        content_weight=two[2 * rows : 3 * rows],
        merge_weight=two[3 * rows :],
        expand_weight=three.reshape(rows, wide),
        shrink_weight=four,
        expand_bias=wide_sum[row, lane : lane + wide // owners()],
        query_bias=sums[0],
        value_bias=sums[1],
        output_bias=sums[2],
        first_gain=sums[3],
        first_shift=sums[4],
        probe_bias=sums[5],
        content_bias=sums[6],
        merge_bias=sums[7],
        second_gain=sums[8],
        second_shift=sums[9],
        shrink_bias=sums[10],
        third_gain=sums[11],
        third_shift=sums[12],
    )
    return (layer_output[None], target_grad[None], memory_grad[None]) + tuple(result)


def solution(mesh):
    tokens = P("dp", "seq", None)
    matrix = P(ALL, None)
    vector = P(ALL)
    params = Params(*[vector] * len(Params._fields))._replace(
        query_weight=matrix,
        key_weight=matrix,
        value_weight=matrix,
        output_weight=matrix,
        probe_weight=matrix,
        lookup_weight=matrix,
        content_weight=matrix,
        merge_weight=matrix,
        expand_weight=matrix,
        shrink_weight=matrix,
    )
    return jax.shard_map(
        per_device,
        mesh=mesh,
        in_specs=(tokens, tokens, tokens, P("dp", "seq"), P("dp", "seq")) + tuple(params),
        out_specs=(tokens, tokens, tokens) + tuple(params),
        check_vma=False,
    )
```

```python
from typing import Any, NamedTuple

import jax
import jax.numpy as jnp
from jax import lax
from jax.experimental import pallas as pl
from jax.experimental.pallas import tpu as pltpu
from jax.sharding import PartitionSpec as P

HEAD_DIM = 64
PAIR = 2 * HEAD_DIM
NEG_FILL = -1e30
EPSILON = 1e-05
BF16 = jnp.bfloat16
F32 = jnp.float32
ALL = ("dp", "seq")

class Params(NamedTuple):
    query_weight: Any
    query_bias: Any
    key_weight: Any
    value_weight: Any
    value_bias: Any
    output_weight: Any
    output_bias: Any
    first_gain: Any
    first_shift: Any
    probe_weight: Any
    probe_bias: Any
    lookup_weight: Any
    content_weight: Any
    content_bias: Any
    merge_weight: Any
    merge_bias: Any
    second_gain: Any
    second_shift: Any
    expand_weight: Any
    expand_bias: Any
    shrink_weight: Any
    shrink_bias: Any
    third_gain: Any
    third_shift: Any


def vectors_of(p):
    return (
        p.query_bias,
        p.value_bias,
        p.output_bias,
        p.first_gain,
        p.first_shift,
        p.probe_bias,
        p.content_bias,
        p.merge_bias,
        p.second_gain,
        p.second_shift,
        p.shrink_bias,
        p.third_gain,
        p.third_shift,
    )


VECTORS = 13
LANES = 128


def dot(left, right):
    return jnp.dot(left, right, preferred_element_type=F32)


def dot_t(left, right):
    return lax.dot_general(left, right, (((1,), (1,)), ((), ())), preferred_element_type=F32)


def t_dot(left, right):
    return lax.dot_general(left, right, (((0,), (0,)), ((), ())), preferred_element_type=F32)


def token_sum(values):
    return jnp.sum(values.astype(F32), axis=0, keepdims=True)


def fill_mask(block, first, qseg, kseg_ref, kpos_ref, bias, base, flags, row):
    rows = qseg.shape[0]
    place = first + lax.broadcasted_iota(jnp.int32, (rows, block), 0)
    for j in range(bias.shape[1] // block):
        cols = pl.ds(j * block, block)
        allowed = (kseg_ref[:, cols] == qseg) & (kpos_ref[:, cols] <= place)
        term = jnp.where(allowed, 0.0, NEG_FILL)
        bias[pl.ds(base, rows), cols] = term
        flags[row, j] = (jnp.max(term) > -1.0).astype(jnp.int32)


def one_head(value, head):
    lane = lax.broadcasted_iota(jnp.int32, value.shape, 1)
    return jnp.where((lane < HEAD_DIM) == (head == 0), value, jnp.zeros_like(value))


def stacked(value, halves):
    return jnp.concatenate([one_head(value, head) for head in range(halves)], axis=0)


def tiles_forward(block, tiles, bias, flags, scores, peaks, sums, mixed):
    rows, total = bias.shape
    peaks[...] = jnp.full(peaks.shape, NEG_FILL, F32)
    sums[...] = jnp.zeros(sums.shape, F32)
    mixed[...] = jnp.zeros(mixed.shape, F32)
    for j in range(total // block):

        @pl.when(flags[0, j] > 0)
        def _():
            cols = pl.ds(j * block, block)
            for query, key, _, at in tiles:
                part = dot_t(query, key(cols))
                for half in range(query.shape[0] // rows):
                    own = pl.ds(at + half * rows, rows)
                    term = part[half * rows : (half + 1) * rows] + bias[:, cols]
                    scores[own, cols] = term
                    high = peaks[own]
                    for c in range(block // LANES):
                        high = jnp.maximum(high, term[:, c * LANES : (c + 1) * LANES])
                    peaks[own] = high

    peak = jnp.max(peaks[...], axis=-1, keepdims=True)
    peaks[...] = jnp.broadcast_to(peak, peaks.shape)
    for j in range(total // block):

        @pl.when(flags[0, j] > 0)
        def _():
            cols = pl.ds(j * block, block)
            for query, _, value, at in tiles:
                own = pl.ds(at, query.shape[0])
                part = jnp.exp(scores[own, cols] - peaks[own, 0:1])
                add = sums[own]
                for c in range(block // LANES):
                    add = add + part[:, c * LANES : (c + 1) * LANES]
                sums[own] = add
                mixed[own] += dot(part.astype(BF16), value(cols))

    whole = jnp.sum(sums[...], axis=-1, keepdims=True)
    return mixed[...] * (1.0 / whole), peak + jnp.log(whole)


def tiles_backward(block, tiles, bias, flags, query_sum, key_sum, value_sum):
    rows, total = bias.shape
    query_sum[...] = jnp.zeros(query_sum.shape, F32)
    for j in range(total // block):

        @pl.when(flags[0, j] > 0)
        def _():
            cols = pl.ds(j * block, block)
            for query, grad, log, inner, key_of, value, at, lanes in tiles:
                key = key_of(cols)
                scores = dot_t(query, key)
                slope = dot_t(grad, value(cols))
                terms = [scores[i : i + rows] + bias[:, cols] for i in range(0, query.shape[0], rows)]
                part = jnp.exp((jnp.concatenate(terms, axis=0) if len(terms) > 1 else terms[0]) - log)
                score_grad = (part * (slope - inner)).astype(BF16)
                query_sum[pl.ds(at, query.shape[0])] += dot(score_grad, key)
                key_sum[cols, lanes] += t_dot(score_grad, query)
                value_sum[cols, lanes] += t_dot(part.astype(BF16), grad)


def lower_lanes(shape):
    return lax.broadcasted_iota(jnp.int32, shape, 1) < HEAD_DIM


def eighth(value):
    return (value.astype(BF16) * 0.125).astype(BF16)


def attend_kernel(block, q0_ref, q_ref, k_ref, v_ref, qseg_ref, kseg_ref, kpos_ref, o_ref, log_ref, bias, flags, *scratch):
    @pl.when(pl.program_id(0) == 0)
    def _():
        fill_mask(block, q0_ref[0], qseg_ref[...], kseg_ref, kpos_ref, bias, 0, flags, 0)

    rows = o_ref.shape[0]
    tile = (stacked(q_ref[...], 2), lambda cols: k_ref[cols, :], lambda cols: v_ref[cols, :], 0)
    out, log = tiles_forward(block, [tile], bias, flags, *scratch)
    low = lower_lanes(o_ref.shape)
    o_ref[...] = jnp.where(low, out[:rows], out[rows:]).astype(BF16)
    log_ref[...] = jnp.where(low, log[:rows], log[rows:])


def attend_back_kernel(block, q0_ref, q_ref, k_ref, v_ref, o_ref, g_ref, log_ref, qseg_ref, kseg_ref, kpos_ref, dq_ref, dk_ref, dv_ref, bias, flags, query_sum, key_sum, value_sum):
    @pl.when(pl.program_id(0) == 0)
    def _():
        fill_mask(block, q0_ref[0], qseg_ref[...], kseg_ref, kpos_ref, bias, 0, flags, 0)

    key_sum[...] = jnp.zeros(key_sum.shape, F32)
    value_sum[...] = jnp.zeros(value_sum.shape, F32)
    rows = q_ref.shape[0]
    grad = stacked(g_ref[...], 2)
    mixed = o_ref[...].astype(F32)
    inner = jnp.sum(grad.astype(F32) * jnp.concatenate([mixed, mixed], axis=0), axis=-1, keepdims=True)
    log = jnp.concatenate([log_ref[:, 0:1], log_ref[:, HEAD_DIM : HEAD_DIM + 1]], axis=0)
    tile = (stacked(q_ref[...], 2), grad, log, inner, lambda cols: k_ref[cols, :], lambda cols: v_ref[cols, :], 0, pl.ds(0, PAIR))
    tiles_backward(block, [tile], bias, flags, query_sum, key_sum, value_sum)
    dq_ref[...] = eighth(jnp.where(lower_lanes(dq_ref.shape), query_sum[:rows], query_sum[rows:]))
    dk_ref[...] = key_sum[...].astype(BF16)
    dv_ref[...] = value_sum[...].astype(BF16)


def attend_specs(rows, total):
    whole = lambda shape: pl.BlockSpec(shape, lambda i: (0, 0))
    strip = lambda count: pl.BlockSpec((count, PAIR), lambda i: (0, i))
    return (
        pl.BlockSpec(memory_space=pltpu.SMEM),
        strip(rows),
        strip(total),
        [whole((rows, 1)), whole((1, total)), whole((1, total))],
    )


def forward_scratch(rows, total, heads):
    return [pltpu.VMEM((heads * rows, total), F32)] + [pltpu.VMEM((heads * rows, LANES), F32)] * 3


def attend_forward(query, key, value, masks, block):
    rows, width = query.shape
    total = key.shape[0]
    scalar, narrow, tall, marks = attend_specs(rows, total)
    q0, qseg, kseg, kpos = masks
    return pl.pallas_call(
        lambda *refs: attend_kernel(block, *refs),
        grid=(width // PAIR,),
        in_specs=[scalar, narrow, tall, tall] + marks,
        out_specs=[narrow, narrow],
        out_shape=[jax.ShapeDtypeStruct((rows, width), BF16), jax.ShapeDtypeStruct((rows, width), F32)],
        scratch_shapes=[pltpu.VMEM((rows, total), F32), pltpu.SMEM((1, total // block), jnp.int32)] + forward_scratch(rows, total, 2),
        cost_estimate=pl.CostEstimate(flops=8 * rows * total * width, bytes_accessed=8 * total * width, transcendentals=rows * total * 12),
        compiler_params=pltpu.CompilerParams(dimension_semantics=("arbitrary",)),
        name="attend_forward",
    )(q0, query, key, value, qseg, kseg, kpos)


def attend_backward(query, key, value, mixed, grad, log, masks, block):
    rows, width = query.shape
    total = key.shape[0]
    scalar, narrow, tall, marks = attend_specs(rows, total)
    q0, qseg, kseg, kpos = masks
    return pl.pallas_call(
        lambda *refs: attend_back_kernel(block, *refs),
        grid=(width // PAIR,),
        in_specs=[scalar, narrow, tall, tall, narrow, narrow, narrow] + marks,
        out_specs=[narrow, tall, tall],
        out_shape=[
            jax.ShapeDtypeStruct((rows, width), BF16),
            jax.ShapeDtypeStruct((total, width), BF16),
            jax.ShapeDtypeStruct((total, width), BF16),
        ],
        scratch_shapes=[
            pltpu.VMEM((rows, total), F32),
            pltpu.SMEM((1, total // block), jnp.int32),
            pltpu.VMEM((2 * rows, PAIR), F32),
            pltpu.VMEM((total, PAIR), F32),
            pltpu.VMEM((total, PAIR), F32),
        ],
        cost_estimate=pl.CostEstimate(flops=20 * rows * total * width, bytes_accessed=16 * total * width, transcendentals=rows * total * 12),
        compiler_params=pltpu.CompilerParams(dimension_semantics=("arbitrary",)),
        name="attend_backward",
    )(q0, query, key, value, mixed, grad, log, qseg, kseg, kpos)


def seats_of(heads, space):
    return [(pl.ds(t, PAIR), pl.ds(space + t, PAIR), pl.ds(2 * space + t, PAIR), min(2, heads - 2 * (t // PAIR))) for t in range(0, space, PAIR)]


def row_kernel(block, heads, q0_ref, qkv_ref, qseg_ref, kseg_ref, kpos_ref, o_ref, log_ref, bias, flags, *scratch):
    rows, space = o_ref.shape
    step = pl.program_id(0)
    own = pl.ds(pl.multiple_of(step * rows, rows), rows)
    fill_mask(block, q0_ref[step], qseg_ref[...], kseg_ref, kpos_ref, bias, 0, flags, 0)
    tiles = []
    for tile, (query_lanes, key_lanes, value_lanes, halves) in enumerate(seats_of(heads, space)):
        key = lambda cols, lanes=key_lanes: qkv_ref[cols, lanes]
        value = lambda cols, lanes=value_lanes: qkv_ref[cols, lanes]
        tiles.append((stacked(qkv_ref[own, query_lanes], halves), key, value, 2 * tile * rows))
    out, log = tiles_forward(block, tiles, bias, flags, *scratch)
    low = lower_lanes((rows, PAIR))
    blank = jnp.zeros((rows, PAIR), F32)
    for query, _, _, at in tiles:
        lanes = pl.ds(at // (2 * rows) * PAIR, PAIR)
        pair = query.shape[0] > rows
        o_ref[:, lanes] = jnp.where(low, out[at : at + rows], out[at + rows : at + 2 * rows] if pair else blank).astype(BF16)
        log_ref[:, lanes] = jnp.where(low, log[at : at + rows], log[at + rows : at + 2 * rows] if pair else blank)


def row_back_kernel(block, heads, q0_ref, qkv_ref, o_ref, g_ref, log_ref, qseg_ref, kseg_ref, kpos_ref, grads_ref, bias, flags, query_sum, key_sum, value_sum):
    rows, space = o_ref.shape
    step = pl.program_id(0)
    own = pl.ds(pl.multiple_of(step * rows, rows), rows)
    fill_mask(block, q0_ref[step], qseg_ref[...], kseg_ref, kpos_ref, bias, 0, flags, 0)

    @pl.when(step == 0)
    def _():
        key_sum[...] = jnp.zeros(key_sum.shape, F32)
        value_sum[...] = jnp.zeros(value_sum.shape, F32)

    tiles = []
    for tile, (query_lanes, key_lanes, value_lanes, halves) in enumerate(seats_of(heads, space)):
        key = lambda cols, lanes=key_lanes: qkv_ref[cols, lanes]
        value = lambda cols, lanes=value_lanes: qkv_ref[cols, lanes]
        grad = stacked(g_ref[:, query_lanes], halves)
        mixed = o_ref[:, query_lanes].astype(F32)
        inner = jnp.sum(grad.astype(F32) * jnp.concatenate([mixed] * halves, axis=0), axis=-1, keepdims=True)
        lane = tile * PAIR
        log = jnp.concatenate([log_ref[:, lane + i * HEAD_DIM : lane + i * HEAD_DIM + 1] for i in range(halves)], axis=0)
        tiles.append((stacked(qkv_ref[own, query_lanes], halves), grad, log, inner, key, value, 2 * tile * rows, query_lanes))
    tiles_backward(block, tiles, bias, flags, query_sum, key_sum, value_sum)
    low = lower_lanes((rows, PAIR))
    for query, _, _, _, _, _, at, lanes in tiles:
        upper = query_sum[at + rows : at + 2 * rows] if query.shape[0] > rows else jnp.zeros((rows, PAIR), F32)
        grads_ref[own, lanes] = eighth(jnp.where(low, query_sum[at : at + rows], upper))

    @pl.when(step == pl.num_programs(0) - 1)
    def _():
        grads_ref[:, space : 2 * space] = key_sum[...].astype(BF16)
        grads_ref[:, 2 * space :] = value_sum[...].astype(BF16)


def row_specs(rows, total, space):
    whole = lambda shape: pl.BlockSpec(shape, lambda i: (0, 0))
    strip = lambda width: pl.BlockSpec((rows, width), lambda i: (i, 0))
    return (
        pl.BlockSpec(memory_space=pltpu.SMEM),
        whole((total, 3 * space)),
        strip(space),
        [strip(1), whole((1, total)), whole((1, total))],
    )


def row_forward(qkv, masks, heads, rows, block):
    total, space = qkv.shape[0], qkv.shape[1] // 3
    scalar, full, narrow, marks = row_specs(rows, total, space)
    q0, qseg, kseg, kpos = masks
    return pl.pallas_call(
        lambda *refs: row_kernel(block, heads, *refs),
        grid=(total // rows,),
        in_specs=[scalar, full] + marks,
        out_specs=[narrow, narrow],
        out_shape=[jax.ShapeDtypeStruct((total, space), BF16), jax.ShapeDtypeStruct((total, space), F32)],
        scratch_shapes=[pltpu.VMEM((rows, total), F32), pltpu.SMEM((1, total // block), jnp.int32)] + forward_scratch(rows, total, heads),
        cost_estimate=pl.CostEstimate(flops=4 * total * total * space, bytes_accessed=10 * total * space, transcendentals=total * total * heads),
        compiler_params=pltpu.CompilerParams(dimension_semantics=("arbitrary",)),
        name="row_forward",
    )(q0, qkv, qseg, kseg, kpos)


def row_backward(qkv, mixed, grad, log, masks, heads, rows, block):
    total, space = mixed.shape
    scalar, full, narrow, marks = row_specs(rows, total, space)
    q0, qseg, kseg, kpos = masks
    return pl.pallas_call(
        lambda *refs: row_back_kernel(block, heads, *refs),
        grid=(total // rows,),
        in_specs=[scalar, full, narrow, narrow, narrow] + marks,
        out_specs=full,
        out_shape=jax.ShapeDtypeStruct((total, 3 * space), BF16),
        scratch_shapes=[
            pltpu.VMEM((rows, total), F32),
            pltpu.SMEM((1, total // block), jnp.int32),
            pltpu.VMEM((heads * rows, PAIR), F32),
            pltpu.VMEM((total, space), F32),
            pltpu.VMEM((total, space), F32),
        ],
        cost_estimate=pl.CostEstimate(flops=10 * total * total * space, bytes_accessed=20 * total * space, transcendentals=total * total * heads),
        compiler_params=pltpu.CompilerParams(dimension_semantics=("arbitrary",)),
        name="row_backward",
    )(q0, qkv, mixed, grad, log, qseg, kseg, kpos)


def split_kernel(span, me_ref, value_ref, out_ref):
    rows, space = out_ref.shape[1:]
    for group in range(out_ref.shape[0]):
        part = value_ref[:, group * span : (group + 1) * span].astype(F32)
        out_ref[me_ref[0] ^ group] = jnp.concatenate([part, jnp.zeros((rows, space - span), F32)], axis=1).astype(BF16)


def split_heads(value, me, groups, space):
    rows, width = value.shape
    return pl.pallas_call(
        lambda *refs: split_kernel(width // groups, *refs),
        out_shape=jax.ShapeDtypeStruct((groups, rows, space), BF16),
        in_specs=[pl.BlockSpec(memory_space=pltpu.SMEM), pl.BlockSpec(memory_space=pltpu.VMEM)],
        out_specs=pl.BlockSpec(memory_space=pltpu.VMEM),
        name="split_heads",
    )(me, value)


def join_kernel(span, me_ref, *refs):
    pieces, (out_ref, held) = refs[:-2], refs[-2:]
    for d, piece in enumerate(pieces):
        held[d] = piece[...]
    parts = [held[me_ref[0] ^ group].astype(F32)[:, :span] for group in range(len(pieces))]
    out_ref[...] = jnp.concatenate(parts, axis=1).astype(BF16)


def join_heads(pieces, me, span):
    rows, space = pieces[0].shape
    groups = len(pieces)
    vmem = pl.BlockSpec(memory_space=pltpu.VMEM)
    return pl.pallas_call(
        lambda *refs: join_kernel(span, *refs),
        out_shape=jax.ShapeDtypeStruct((rows, groups * span), BF16),
        in_specs=[pl.BlockSpec(memory_space=pltpu.SMEM)] + [vmem] * groups,
        out_specs=vmem,
        scratch_shapes=[pltpu.VMEM((groups, rows, space), BF16)],
        name="join_heads",
    )(me, *pieces)


def pack_heads_kernel(weights, span, me_ref, *refs):
    out_ref = refs[-1]
    vectors = refs[weights][...]
    rows = refs[0].shape[0]
    space = out_ref.shape[2] // weights
    for group in range(out_ref.shape[0]):
        parts = []
        for ref in refs[:weights]:
            parts += [ref[:, group * span : (group + 1) * span].astype(F32), jnp.zeros((rows, space - span), F32)]
        out_ref[me_ref[0] ^ group, :rows] = jnp.concatenate(parts, axis=1).astype(BF16)
        out_ref[me_ref[0] ^ group, rows:] = vectors


def pack_heads(weights, vectors, me, groups):
    rows, width = weights[0].shape
    vmem = pl.BlockSpec(memory_space=pltpu.VMEM)
    return pl.pallas_call(
        lambda *refs: pack_heads_kernel(len(weights), width // groups, *refs),
        out_shape=jax.ShapeDtypeStruct((groups, rows + vectors.shape[0], width), BF16),
        in_specs=[pl.BlockSpec(memory_space=pltpu.SMEM)] + [vmem] * (len(weights) + 1),
        out_specs=vmem,
        name="pack_heads",
    )(me, *weights, vectors)


def unpack_heads_kernel(weights, span, me_ref, *refs):
    groups = len(refs) - weights - 2
    pieces, outs, tail_ref, held = refs[:groups], refs[groups:-2], refs[-2], refs[-1]
    rows = outs[0].shape[0]
    space = pieces[0].shape[1] // weights
    for d, piece in enumerate(pieces):
        held[d] = piece[...].astype(F32)
    for i, out in enumerate(outs):
        out[...] = jnp.concatenate([held[me_ref[0] ^ group, :rows, i * space : i * space + span] for group in range(groups)], axis=1)
    tail_ref[...] = sum(held[d, rows:] for d in range(groups))


def unpack_heads(pieces, me, weights, rows):
    groups = len(pieces)
    width = pieces[0].shape[1]
    vmem = pl.BlockSpec(memory_space=pltpu.VMEM)
    return pl.pallas_call(
        lambda *refs: unpack_heads_kernel(weights, width // groups, *refs),
        out_shape=[jax.ShapeDtypeStruct((rows, width), F32)] * weights + [jax.ShapeDtypeStruct((pieces[0].shape[0] - rows, width), F32)],
        in_specs=[pl.BlockSpec(memory_space=pltpu.SMEM)] + [vmem] * groups,
        out_specs=[vmem] * (weights + 1),
        scratch_shapes=[pltpu.VMEM((groups,) + pieces[0].shape, F32)],
        name="unpack_heads",
    )(me, *pieces)


def norm_forward(hidden, gain, shift):
    centred = hidden - jnp.mean(hidden, axis=-1, keepdims=True)
    inverse = lax.rsqrt(jnp.mean(centred * centred, axis=-1, keepdims=True) + EPSILON)
    normed = centred * inverse
    return normed * gain + shift, normed, inverse


def norm_backward(upstream, normed, inverse, gain):
    scaled = upstream * gain
    inner = jnp.mean(scaled, axis=-1, keepdims=True)
    along = jnp.mean(scaled * normed, axis=-1, keepdims=True)
    return inverse * (scaled - inner - normed * along), token_sum(upstream * normed), token_sum(upstream)


def exact_gelu(values):
    return jax.nn.gelu(values, approximate=False)


def expand_kernel(value_ref, weight_ref, bias_ref, hidden_ref, slope_ref):
    act = dot(value_ref[...], weight_ref[...]) + bias_ref[...]
    share = 0.5 + 0.5 * lax.erf(act * ROOT_HALF)
    hidden_ref[...] = (act * share).astype(BF16)
    slope_ref[...] = share + act * (jnp.exp(-0.5 * act * act) * DENSITY)


ROOT_HALF = 0.7071067811865476
DENSITY = 0.3989422804014327


def expand_gelu(value, weight, bias):
    rows, width = value.shape
    wide = weight.shape[1]
    step = 4 * LANES
    strip = lambda count: pl.BlockSpec((count, step), lambda i: (0, i))
    return pl.pallas_call(
        expand_kernel,
        grid=(wide // step,),
        in_specs=[pl.BlockSpec((rows, width), lambda i: (0, 0)), strip(width), strip(1)],
        out_specs=[strip(rows), strip(rows)],
        out_shape=[jax.ShapeDtypeStruct((rows, wide), BF16), jax.ShapeDtypeStruct((rows, wide), F32)],
        cost_estimate=pl.CostEstimate(flops=2 * rows * width * wide, bytes_accessed=2 * width * wide + 6 * rows * wide, transcendentals=2 * rows * wide),
        compiler_params=pltpu.CompilerParams(dimension_semantics=("arbitrary",)),
        name="expand_gelu",
    )(value, weight, bias)


def seq_offsets(count):
    offsets = [0]
    bit = count // 2
    while bit:
        offsets = offsets + [o ^ bit for o in offsets]
        bit //= 2
    return offsets


def swap(value, axis, bit):
    count = lax.axis_size(axis)
    return lax.ppermute(value, axis, [(i, i ^ bit) for i in range(count)])


def seq_bits():
    bit = lax.axis_size("seq") // 2
    bits = []
    while bit:
        bits.append(bit)
        bit //= 2
    return bits


def seq_gather(rows, bits):
    for bit in bits:
        rows = jnp.concatenate([rows, swap(rows, "seq", bit)], axis=0)
    return rows


def seq_reduce(total, bits):
    for bit in bits:
        half = total.shape[0] // 2
        got = swap(total[half:].astype(BF16), "seq", bit)
        total = total[:half].astype(F32) + got.astype(F32)
    return total


def tie(*values):
    return lax.optimization_barrier(values)


NEAR_LAST = ((16, 8, 2, 4), (8, 16, 4, 2))
NEAR_FIRST = ((2, 4, 8, 16), (4, 2, 16, 8))
DP_LAST = ((16, 8, 4), (4, 16, 8))
NEAR_BACK = ((16, 2, 8, 4), (16, 2, 4, 8))
BLOCK = 8


FLAT = 2 ** (len(NEAR_LAST[0]) + 1)


def owners():
    return lax.axis_size("dp") * lax.axis_size("seq")


def staged():
    return owners() == 2 ** (len(NEAR_LAST[0]) + 1)


def slot_owners(plan):
    def masks(core):
        found = [0]
        for bit in plan[core]:
            found = found + [o ^ bit for o in found]
        return found

    me = lax.axis_index(ALL)
    even = jnp.array(masks(0) + [1 ^ m for m in masks(1)], jnp.int32)
    odd = jnp.array(masks(1) + [1 ^ m for m in masks(0)], jnp.int32)
    return me ^ jnp.where((me & 1) == 0, even, odd)


def group_owners(plan):
    def masks(core):
        found = list(range(lax.axis_size("seq")))
        for bit in plan[core]:
            found = found + [o ^ bit for o in found]
        return found

    me = lax.axis_index(ALL)
    return me ^ jnp.where((me & 1) == 0, jnp.array(masks(0), jnp.int32), jnp.array(masks(1), jnp.int32))


def exchange(pieces):
    return [pieces[0]] + [swap(pieces[d], "seq", d) for d in range(1, len(pieces))]


def stage_swap(value, plan, stage):
    return lax.ppermute(value, ALL, [(d, d ^ plan[d & 1][stage]) for d in range(owners())])


def core_swap(value):
    return lax.ppermute(value, ALL, [(d, d ^ 1) for d in range(owners())])


def place_kernel(groups, rows, counts, order, *refs):
    pieces, refs = refs[: len(counts)], refs[len(counts) :]
    outs, (held, came, left) = refs[:-3], refs[-3:]
    blocks = held.shape[1]
    sizes = [rows] * groups + [blocks - groups * rows] * (len(outs) - groups)
    base = 0
    for piece, count in zip(pieces, counts):

        def fetch(slot, carry):
            pltpu.make_async_copy(piece.at[slot], held.at[base + slot], came.at[base + slot]).start()
            return carry

        lax.fori_loop(0, count, fetch, 0)
        base += count

    def put(slot, carry):
        pltpu.make_async_copy(pieces[0].at[0], held.at[slot], came.at[slot]).wait()
        at = 0
        for out, size in zip(outs, sizes):
            pltpu.make_async_copy(held.at[slot, pl.ds(at, size)], out.at[order[slot]], left).start()
            at += size
        return carry

    lax.fori_loop(0, base, put, 0)

    def finish(slot, carry):
        at = 0
        for out, size in zip(outs, sizes):
            pltpu.make_async_copy(held.at[slot, pl.ds(at, size)], out.at[slot], left).wait()
            at += size
        return carry

    lax.fori_loop(0, base, finish, 0)


def place(pieces, order, groups, rows):
    counts = tuple(p.shape[0] for p in pieces)
    _, blocks, _, width = pieces[0].shape
    devices = sum(counts)
    sizes = [rows] * groups + [blocks - groups * rows] * (blocks > groups * rows)
    anywhere = pl.BlockSpec(memory_space=pl.ANY)
    return pl.pallas_call(
        lambda *refs: place_kernel(groups, rows, counts, *refs),
        out_shape=[jax.ShapeDtypeStruct((devices, size, BLOCK, width), BF16) for size in sizes],
        in_specs=[pl.BlockSpec(memory_space=pltpu.SMEM)] + [anywhere] * len(pieces),
        out_specs=[anywhere] * len(sizes),
        scratch_shapes=[
            pltpu.VMEM((devices, blocks, BLOCK, width), BF16),
            pltpu.SemaphoreType.DMA((devices,)),
            pltpu.SemaphoreType.DMA,
        ],
        cost_estimate=pl.CostEstimate(flops=0, bytes_accessed=4 * devices * blocks * BLOCK * width, transcendentals=0),
        name="place",
    )(order, *pieces)


def spread_kernel(sizes, order, *refs):
    terms, refs = refs[: len(sizes)], refs[len(sizes) :]
    outs, (held, came, left) = refs[:2], refs[2:]
    half = outs[0].shape[0]
    spans = [pl.ds(sum(sizes[:i]), size) for i, size in enumerate(sizes)]
    for i, term in enumerate(terms):
        pltpu.make_async_copy(term, held.at[:, spans[i]], came.at[i]).start()
    for i, term in enumerate(terms):
        pltpu.make_async_copy(term, held.at[:, spans[i]], came.at[i]).wait()
        for index, out in enumerate(outs):

            def put(slot, carry):
                pltpu.make_async_copy(held.at[order[index * half + slot], spans[i]], out.at[slot, spans[i]], left).start()
                return carry

            lax.fori_loop(0, half, put, 0)

    def finish(slot, carry):
        for out in outs:
            for span in spans:
                pltpu.make_async_copy(held.at[slot, span], out.at[slot, span], left).wait()
        return carry

    lax.fori_loop(0, half, finish, 0)


def spread(terms, order):
    devices, _, _, width = terms[0].shape
    sizes = tuple(t.shape[1] for t in terms)
    blocks = sum(sizes)
    shape = jax.ShapeDtypeStruct((devices // 2, blocks, BLOCK, width), BF16)
    anywhere = pl.BlockSpec(memory_space=pl.ANY)
    return pl.pallas_call(
        lambda *refs: spread_kernel(sizes, *refs),
        out_shape=[shape, shape],
        in_specs=[pl.BlockSpec(memory_space=pltpu.SMEM)] + [anywhere] * len(terms),
        out_specs=[anywhere] * 2,
        scratch_shapes=[
            pltpu.VMEM((devices, blocks, BLOCK, width), BF16),
            pltpu.SemaphoreType.DMA((len(sizes),)),
            pltpu.SemaphoreType.DMA,
        ],
        cost_estimate=pl.CostEstimate(flops=0, bytes_accessed=4 * devices * blocks * BLOCK * width, transcendentals=0),
        name="spread",
    )(order, *terms)


def seat(index):
    return index % BLOCK, LANES * (index // BLOCK)


def pack_vectors_kernel(*refs):
    out, held = refs[-2:]
    held[...] = jnp.zeros(held.shape, F32)
    for i, ref in enumerate(refs[:-2]):
        row, lane = seat(i)
        held[row : row + 1, lane : lane + ref.shape[1]] = ref[...].astype(F32)
    out[...] = held[...].astype(BF16)


def pack_vectors(vectors, width):
    return pl.pallas_call(
        pack_vectors_kernel,
        out_shape=jax.ShapeDtypeStruct((BLOCK, width), BF16),
        in_specs=[pl.BlockSpec(memory_space=pltpu.VMEM)] * len(vectors),
        out_specs=pl.BlockSpec(memory_space=pltpu.VMEM),
        scratch_shapes=[pltpu.VMEM((BLOCK, width), F32)],
        name="pack_vectors",
    )(*[v.reshape(1, -1) for v in vectors])


def unpack_vectors_kernel(blocks, out, wide):
    rows = out.shape[1] // blocks.shape[0]
    span = wide.shape[1] // blocks.shape[0]
    row, lane = seat(VECTORS)
    for d in range(blocks.shape[0]):
        for half in range(2):
            part = blocks[d, :, LANES * half : LANES * (half + 1)].astype(F32)
            out[half * BLOCK : (half + 1) * BLOCK, d * rows : (d + 1) * rows] = part[:, :rows]
            if half == lane // LANES:
                wide[:, d * span : (d + 1) * span] = part[row : row + 1, :span]


def unpack_vectors(blocks, width, wide):
    return pl.pallas_call(
        unpack_vectors_kernel,
        grid=(1,),
        in_specs=[pl.BlockSpec((blocks.shape[0], BLOCK, 2 * LANES), lambda i: (0, 0, 0))],
        out_specs=[pl.BlockSpec((2 * BLOCK, width), lambda i: (0, 0)), pl.BlockSpec((1, wide), lambda i: (0, 0))],
        out_shape=[jax.ShapeDtypeStruct((2 * BLOCK, width), F32), jax.ShapeDtypeStruct((1, wide), F32)],
        name="unpack_vectors",
    )(blocks)


def pack_sums_kernel(*refs):
    out = refs[-1]
    vectors, wide = refs[:-2], refs[-2]
    devices = out.shape[0]
    rows = vectors[0].shape[1] // devices
    span = wide.shape[1] // devices
    table = jnp.concatenate([v[...] for v in vectors] + [jnp.zeros((2 * BLOCK - len(vectors), vectors[0].shape[1]), F32)], axis=0)
    row, lane = seat(VECTORS)
    blank = jnp.zeros((BLOCK, LANES - rows), F32)
    empty = jnp.zeros((BLOCK, out.shape[2] - 2 * LANES), F32)
    line = lax.broadcasted_iota(jnp.int32, (BLOCK, LANES), 0)
    for d in range(devices):
        parts = [table[half * BLOCK : (half + 1) * BLOCK, d * rows : (d + 1) * rows] for half in range(2)]
        parts = [jnp.concatenate([part, blank], axis=1) for part in parts]
        strip = jnp.concatenate([wide[:, d * span : (d + 1) * span], jnp.zeros((1, LANES - span), F32)], axis=1)
        parts[lane // LANES] = jnp.where(line == row, strip, parts[lane // LANES])
        out[d] = jnp.concatenate(parts + [empty], axis=1).astype(BF16)


def pack_sums(vectors, wide, width):
    return pl.pallas_call(
        pack_sums_kernel,
        out_shape=jax.ShapeDtypeStruct((owners(), BLOCK, width), BF16),
        in_specs=[pl.BlockSpec(memory_space=pltpu.VMEM)] * (len(vectors) + 1),
        out_specs=pl.BlockSpec(memory_space=pltpu.VMEM),
        name="pack_sums",
    )(*vectors, wide)


def gather_start(shards):
    parts = jnp.concatenate(list(shards), axis=0) if len(shards) > 1 else shards[0]
    return parts.reshape(1, -1, BLOCK, parts.shape[1]) if staged() else parts


def gather_step(value, plan, stage):
    return jnp.concatenate([value, stage_swap(value, plan, stage)], axis=0) if staged() else value


def gather_last(value, plan):
    return (value, stage_swap(value, plan, len(plan[0]) - 1)) if staged() else (value,)


def gather_finish(halves):
    return halves + tuple(core_swap(h) for h in halves) if staged() else (lax.all_gather(halves[0], ALL, axis=0, tiled=False),)


def unpack(pieces, plan, count, rows):
    width = pieces[0].shape[-1]
    if not staged():
        whole = pieces[0]
        weights = [whole[:, i * rows : (i + 1) * rows].reshape(-1, width) for i in range(count)]
        return weights + [whole[:, count * rows :]]
    found = place(pieces, slot_owners(plan), count, rows // BLOCK)
    return [w.reshape(-1, width) for w in found[:count]] + [t.reshape(-1, BLOCK, width) for t in found[count:]]


def reduce_start(terms, plan, tail=None):
    devices = owners()
    width = terms[0].shape[1]
    parts = [t.astype(BF16).reshape(devices, -1, width) for t in terms]
    if tail is not None:
        parts.append(tail)
    if not staged():
        return (jnp.concatenate(parts, axis=1),) * 2
    return tuple(spread([p.reshape(devices, -1, BLOCK, width) for p in parts], slot_owners(plan)))


def add_halves(mine, got):
    half = mine.shape[0] // 2
    add = lambda a, b: (a.astype(F32) + b.astype(F32)).astype(BF16)
    return add(mine[:half], got[:half]), add(mine[half:], got[half:])


def reduce_core(halves):
    own, other = halves
    return add_halves(own, core_swap(other)) if staged() else (own, own)


def reduce_step(pair, plan, stage):
    if not staged():
        return pair
    got = stage_swap(pair[1], plan, stage)
    if stage:
        return add_halves(pair[0], got)
    return (pair[0].astype(F32) + got.astype(F32),) * 2


def reduce_finish(pair):
    if staged():
        return pair[0].reshape(-1, pair[0].shape[-1])
    return lax.psum_scatter(pair[0], ALL, scatter_dimension=0, tiled=False).astype(F32)


def per_device_by_rows(target, memory, cotangent, target_segments, memory_segments, *shards):
    p = Params(*shards)
    target = target[0]
    memory = memory[0]
    local, width = target.shape
    seq = lax.axis_size("seq")
    place_in_row = lax.axis_index("seq")
    offsets = seq_offsets(seq)
    bits = seq_bits()
    block = local
    rows = p.query_weight.shape[0]
    wide = p.expand_weight.shape[1]
    last = NEAR_LAST

    expand_weight = lax.all_gather(p.expand_weight, ALL, axis=0, tiled=True)
    shrink_weight = lax.all_gather(p.shrink_weight, ALL, axis=0, tiled=True)
    vectors = pack_vectors(vectors_of(p) + (p.expand_bias,), width)
    one = gather_start([p.query_weight, p.key_weight, p.value_weight, p.output_weight, vectors])
    two = gather_start([p.probe_weight, p.lookup_weight, p.content_weight, p.merge_weight])
    marks = jnp.stack([target_segments[0], memory_segments[0]]).astype(BF16)
    marks = jnp.pad(marks, ((0, BLOCK - 2), (0, width - local)))
    target_pack = jnp.concatenate([target, marks], axis=0)[None]
    memory_row = memory[None]
    one = gather_step(one, last, 0)
    target_pack = seq_gather(target_pack, bits[:1])
    one, target_pack, two = tie(one, target_pack, two)
    one = gather_step(one, last, 1)
    target_pack = seq_gather(target_pack, bits[1:])
    one, target_pack, two = tie(one, target_pack, two)
    one = gather_step(one, last, 2)
    two = gather_step(two, last, 0)
    target_row = target_pack[:, :local].reshape(-1, width)
    key_places = jnp.concatenate([(place_in_row ^ o) * local + jnp.arange(local, dtype=jnp.int32) for o in offsets])[None]
    target_marks = target_pack[:, local, :local].reshape(1, -1).astype(jnp.int32)
    memory_marks = target_pack[:, local + 1, :local].reshape(1, -1).astype(jnp.int32)
    own_marks = target_segments.reshape(local, 1)
    start = (place_in_row * local).astype(jnp.int32).reshape(1)
    self_masks = (start, own_marks, target_marks, key_places)
    cross_masks = (start, own_marks, memory_marks, jnp.zeros_like(key_places))
    one, two = tie(one, two)
    one = gather_last(one, last)
    two = gather_step(two, last, 1)
    one, two, memory_row = tie(one, two, memory_row)

    wq, wk, wv, wo, blocks = unpack(gather_finish(one), last, 4, rows)
    two = gather_step(two, last, 2)
    memory_row = seq_gather(memory_row, bits[:1])
    named, expand_bias = unpack_vectors(blocks, width, wide)
    (
        query_bias,
        value_bias,
        output_bias,
        first_gain,
        first_shift,
        probe_bias,
        content_bias,
        merge_bias,
        second_gain,
        second_shift,
        shrink_bias,
        third_gain,
        third_shift,
    ) = (named[i : i + 1] for i in range(VECTORS))
    query_one = ((dot(target, wq) + query_bias) * 0.125).astype(BF16)
    key_one = dot(target_row, wk).astype(BF16)
    value_one = (dot(target_row, wv) + value_bias).astype(BF16)
    query_one, key_one, value_one, two, memory_row = tie(query_one, key_one, value_one, two, memory_row)
    mixed_one, log_one = attend_forward(query_one, key_one, value_one, self_masks, block)
    two = gather_last(two, last)
    memory_row = seq_gather(memory_row, bits[1:]).reshape(-1, width)
    mixed_one, log_one, two, memory_row = tie(mixed_one, log_one, two, memory_row)
    first_sum = target.astype(F32) + dot(mixed_one, wo) + output_bias
    first_full, normed_one, inverse_one = norm_forward(first_sum, first_gain, first_shift)
    first_out = first_full.astype(BF16)
    wp, wl, wc, wm, *_ = unpack(gather_finish(two), last, 4, rows)
    query_two = ((dot(first_out, wp) + probe_bias) * 0.125).astype(BF16)
    key_two = dot(memory_row, wl).astype(BF16)
    value_two = (dot(memory_row, wc) + content_bias).astype(BF16)
    mixed_two, log_two = attend_forward(query_two, key_two, value_two, cross_masks, block)
    second_sum = first_out.astype(F32) + dot(mixed_two, wm) + merge_bias
    second_full, normed_two, inverse_two = norm_forward(second_sum, second_gain, second_shift)
    second_out = second_full.astype(BF16)
    pre_act = dot(second_out, expand_weight) + expand_bias
    hidden = exact_gelu(pre_act).astype(BF16)
    third_sum = second_out.astype(F32) + dot(hidden, shrink_weight) + shrink_bias
    third_full, normed_three, inverse_three = norm_forward(third_sum, third_gain, third_shift)
    layer_output = third_full.astype(BF16)

    upstream = cotangent[0].astype(F32)
    third_grad, third_gain_grad, third_shift_grad = norm_backward(upstream, normed_three, inverse_three, third_gain)
    shrink_in = third_grad.astype(BF16)
    shrink_bias_grad = token_sum(shrink_in)
    shrink_grad = t_dot(hidden, shrink_in).astype(BF16)
    shrink_grad, shrink_in, third_grad = tie(shrink_grad, shrink_in, third_grad)
    four = lax.psum_scatter(shrink_grad, ALL, scatter_dimension=0, tiled=True).astype(F32)
    hidden_grad = dot_t(shrink_in, shrink_weight)
    act_grad = jax.vjp(exact_gelu, pre_act)[1](hidden_grad)[0].astype(BF16)
    expand_bias_grad = token_sum(act_grad)
    three = reduce_start([t_dot(second_out, act_grad)], last)
    three, act_grad, third_grad = tie(three, act_grad, third_grad)
    three = reduce_core(three)
    second_grad = third_grad + dot_t(act_grad, expand_weight)
    second_sum_grad, second_gain_grad, second_shift_grad = norm_backward(second_grad, normed_two, inverse_two, second_gain)
    merge_in = second_sum_grad.astype(BF16)
    merge_bias_grad = token_sum(merge_in)
    mixed_two_grad = dot_t(merge_in, wm).astype(BF16)
    mixed_two_grad, three = tie(mixed_two_grad, three)
    three = reduce_step(three, last, 3)
    probe_in, lookup_part, content_part = attend_backward(query_two, key_two, value_two, mixed_two, mixed_two_grad, log_two, cross_masks, block)
    probe_in, lookup_part, content_part, three = tie(probe_in, lookup_part, content_part, three)
    three = reduce_step(three, last, 2)
    probe_bias_grad = token_sum(probe_in)
    content_bias_grad = token_sum(content_part)
    cross_grads = [t_dot(first_out, probe_in), t_dot(memory_row, lookup_part), t_dot(memory_row, content_part), t_dot(mixed_two, merge_in)]
    two = reduce_start(cross_grads, last)
    first_grad = second_sum_grad + dot_t(probe_in, wp)
    first_sum_grad, first_gain_grad, first_shift_grad = norm_backward(first_grad, normed_one, inverse_one, first_gain)
    output_in = first_sum_grad.astype(BF16)
    output_bias_grad = token_sum(output_in)
    mixed_one_grad = dot_t(output_in, wo).astype(BF16)
    two, three, lookup_part, content_part = tie(two, three, lookup_part, content_part)
    two = reduce_core(two)
    three = reduce_step(three, last, 1)
    memory_part = (dot_t(lookup_part, wl) + dot_t(content_part, wc)).reshape(seq, local, width)
    mixed_one_grad, two, three, memory_part = tie(mixed_one_grad, two, three, memory_part)
    two = reduce_step(two, last, 3)
    three = reduce_step(three, last, 0)
    query_in, key_part, value_part = attend_backward(query_one, key_one, value_one, mixed_one, mixed_one_grad, log_one, self_masks, block)
    query_in, key_part, value_part, two, three, memory_part = tie(query_in, key_part, value_part, two, three, memory_part)
    two = reduce_step(two, last, 2)
    memory_part = seq_reduce(memory_part, bits[:0:-1])
    query_bias_grad = token_sum(query_in)
    value_bias_grad = token_sum(value_part)
    self_grads = [t_dot(target, query_in), t_dot(target_row, key_part), t_dot(target_row, value_part), t_dot(mixed_one, output_in)]
    vector_grads = (
        query_bias_grad,
        value_bias_grad,
        output_bias_grad,
        first_gain_grad,
        first_shift_grad,
        probe_bias_grad,
        content_bias_grad,
        merge_bias_grad,
        second_gain_grad,
        second_shift_grad,
        shrink_bias_grad,
        third_gain_grad,
        third_shift_grad,
    )
    one = reduce_start(self_grads, last, pack_sums(vector_grads, expand_bias_grad, width))
    one, two, memory_part, key_part, value_part, query_in = tie(one, two, memory_part, key_part, value_part, query_in)
    one = reduce_core(one)
    two = reduce_step(two, last, 1)
    target_part = (dot_t(key_part, wk) + dot_t(value_part, wv)).reshape(seq, local, width)
    one, two, memory_part, target_part = tie(one, two, memory_part, target_part)
    one = reduce_step(one, last, 3)
    two = reduce_step(two, last, 0)
    target_part = seq_reduce(target_part, bits[:0:-1])
    target_grad = first_sum_grad + dot_t(query_in, wq)
    one, memory_part, target_part, target_grad = tie(one, memory_part, target_part, target_grad)
    one = reduce_step(one, last, 2)
    memory_grad = seq_reduce(memory_part, bits[:1])[0]
    one, target_part, memory_grad = tie(one, target_part, memory_grad)
    one = reduce_step(one, last, 1)
    target_grad = target_grad + seq_reduce(target_part, bits[:1])[0]
    one = reduce_step(one, last, 0)

    one, two, three = (reduce_finish(t) for t in (one, two, three))
    wide_sum = one[4 * rows :]
    sums = [wide_sum[seat(i)[0], seat(i)[1] : seat(i)[1] + rows] for i in range(VECTORS)]
    row, lane = seat(VECTORS)
    result = Params(
        query_weight=one[:rows],
        key_weight=one[rows : 2 * rows],
        value_weight=one[2 * rows : 3 * rows],
        output_weight=one[3 * rows : 4 * rows],
        probe_weight=two[:rows],
        lookup_weight=two[rows : 2 * rows],
        content_weight=two[2 * rows : 3 * rows],
        merge_weight=two[3 * rows :],
        expand_weight=three.reshape(rows, wide),
        shrink_weight=four,
        expand_bias=wide_sum[row, lane : lane + wide // owners()],
        query_bias=sums[0],
        value_bias=sums[1],
        output_bias=sums[2],
        first_gain=sums[3],
        first_shift=sums[4],
        probe_bias=sums[5],
        content_bias=sums[6],
        merge_bias=sums[7],
        second_gain=sums[8],
        second_shift=sums[9],
        shrink_bias=sums[10],
        third_gain=sums[11],
        third_shift=sums[12],
    )
    return (layer_output[None], target_grad[None], memory_grad[None]) + tuple(result)


def per_device(target, memory, cotangent, target_segments, memory_segments, *shards):
    p = Params(*shards)
    target = target[0]
    memory = memory[0]
    local, width = target.shape
    seq = lax.axis_size("seq")
    place_in_row = lax.axis_index("seq")
    me = place_in_row.astype(jnp.int32).reshape(1)
    offsets = seq_offsets(seq)
    bits = seq_bits()
    block = local
    rows = p.query_weight.shape[0]
    wide = p.expand_weight.shape[1]
    last, near, back = NEAR_LAST, DP_LAST, NEAR_BACK
    heads = width // HEAD_DIM // seq
    span = heads * HEAD_DIM
    space = -(-span // PAIR) * PAIR

    vectors = pack_vectors(vectors_of(p) + (p.expand_bias,), width)
    packed = pack_heads([p.query_weight, p.key_weight, p.value_weight], vectors, me, seq)
    two = gather_start([p.output_weight, p.probe_weight, p.lookup_weight, p.content_weight, p.merge_weight])
    three, four = gather_start([p.expand_weight]), gather_start([p.shrink_weight])
    marks = jnp.stack([target_segments[0], memory_segments[0]]).astype(BF16)
    marks = jnp.pad(marks, ((0, BLOCK - 2), (0, width - local)))
    target_pack = jnp.concatenate([target, marks], axis=0)[None]
    one = jnp.stack(exchange([packed[d] for d in range(seq)]))
    target_pack = seq_gather(target_pack, bits[:1])
    one, target_pack, two, three, four = tie(one, target_pack, two, three, four)
    one = gather_step(one, near, 0)
    target_pack = seq_gather(target_pack, bits[1:])
    two = gather_step(two, last, 0)
    one, target_pack, two, memory_row = tie(one, target_pack, two, memory[None])
    one = gather_step(one, near, 1)
    memory_row = seq_gather(memory_row, bits[:1])
    target_row = target_pack[:, :local].reshape(-1, width)
    block_places = jnp.stack([(place_in_row ^ o) * local for o in offsets]).astype(jnp.int32)
    key_places = (block_places[:, None] + jnp.arange(local, dtype=jnp.int32)).reshape(1, -1)
    target_marks = target_pack[:, local, :local].reshape(1, -1).astype(jnp.int32)
    memory_marks = target_pack[:, local + 1, :local].reshape(1, -1).astype(jnp.int32)
    own_marks = target_segments.reshape(local, 1)
    self_masks = (block_places, target_marks.reshape(-1, 1), target_marks, key_places)
    cross_masks = (block_places[:1], own_marks, memory_marks, jnp.zeros_like(key_places))
    one, two, memory_row = tie(one, two, memory_row)
    got = stage_swap(one, near, 2)
    two = gather_step(two, last, 1)
    one, got, two, three, four = tie(one, got, two, three, four)

    two = gather_step(two, last, 2)
    three = gather_step(three, last, 0)
    four = gather_step(four, last, 0)
    memory_row = seq_gather(memory_row, bits[1:]).reshape(-1, width)
    pieces = [v.reshape(v.shape[0], -1, BLOCK, width) for v in (one, got)]
    wqkv, blocks = place(pieces, group_owners(near), 1, rows // BLOCK)
    wqkv = wqkv.reshape(-1, width)
    named, expand_bias = unpack_vectors(blocks.reshape(-1, BLOCK, width), width, wide)
    (
        query_bias,
        value_bias,
        output_bias,
        first_gain,
        first_shift,
        probe_bias,
        content_bias,
        merge_bias,
        second_gain,
        second_shift,
        shrink_bias,
        third_gain,
        third_shift,
    ) = (named[i : i + 1] for i in range(VECTORS))
    mine = lambda v: jnp.pad(lax.dynamic_slice(v, (0, place_in_row * span), (1, span)), ((0, 0), (0, space - span)))
    row_bias = jnp.concatenate([mine(query_bias), jnp.zeros((1, space), F32), mine(value_bias)], axis=1)
    scale = jnp.where(jnp.arange(3 * space) < space, 0.125, 1.0)[None]
    qkv = ((dot(target_row, wqkv) + row_bias) * scale).astype(BF16)
    qkv, two, three, four, memory_row = tie(qkv, two, three, four, memory_row)
    two = gather_last(two, last)
    three = gather_step(three, last, 1)
    four = gather_step(four, last, 1)
    mixed_row, log_one = row_forward(qkv, self_masks, heads, local, block)
    mixed_row, two, three, four = tie(mixed_row, two, three, four)
    sent = [mixed_row[i * local : (i + 1) * local] for i in range(seq)]
    mixed_one = join_heads(exchange([sent[offsets.index(d)] for d in range(seq)]), me, span)
    two_pieces = gather_finish(two)
    mixed_one, two_pieces, three, four = tie(mixed_one, two_pieces, three, four)
    three = gather_step(three, last, 2)
    four = gather_step(four, last, 2)
    wo, wp, wl, wc, wm, *_ = unpack(two_pieces, last, 5, rows)
    first_sum = target.astype(F32) + dot(mixed_one, wo) + output_bias
    first_full, normed_one, inverse_one = norm_forward(first_sum, first_gain, first_shift)
    first_out = first_full.astype(BF16)
    query_two = ((dot(first_out, wp) + probe_bias) * 0.125).astype(BF16)
    key_two = dot(memory_row, wl).astype(BF16)
    value_two = (dot(memory_row, wc) + content_bias).astype(BF16)
    query_two, key_two, value_two, three, four = tie(query_two, key_two, value_two, three, four)
    three, four = gather_last(three, last), gather_last(four, last)
    mixed_two, log_two = attend_forward(query_two, key_two, value_two, cross_masks, block)
    mixed_two, three, four = tie(mixed_two, three, four)
    three = gather_finish(three)
    second_sum = first_out.astype(F32) + dot(mixed_two, wm) + merge_bias
    second_full, normed_two, inverse_two = norm_forward(second_sum, second_gain, second_shift)
    second_out = second_full.astype(BF16)
    second_out, three, four = tie(second_out, three, four)
    four = gather_finish(four)
    expand_weight, *_ = unpack(three, last, 1, rows)
    hidden, slope = expand_gelu(second_out, expand_weight, expand_bias)
    hidden, four = tie(hidden, four)
    shrink_weight, *_ = unpack(four, last, 1, p.shrink_weight.shape[0])
    third_sum = second_out.astype(F32) + dot(hidden, shrink_weight) + shrink_bias
    third_full, normed_three, inverse_three = norm_forward(third_sum, third_gain, third_shift)
    layer_output = third_full.astype(BF16)

    upstream = cotangent[0].astype(F32)
    third_grad, third_gain_grad, third_shift_grad = norm_backward(upstream, normed_three, inverse_three, third_gain)
    shrink_in = third_grad.astype(BF16)
    shrink_bias_grad = token_sum(shrink_in)
    shrink_grad = t_dot(hidden, shrink_in).astype(BF16)
    four = reduce_start([shrink_grad], last)
    four, shrink_in, third_grad = tie(four, shrink_in, third_grad)
    four = reduce_core(four)
    act_grad = (dot_t(shrink_in, shrink_weight) * slope).astype(BF16)
    expand_bias_grad = token_sum(act_grad)
    three = reduce_start([t_dot(second_out, act_grad)], last)
    three, four, act_grad, third_grad = tie(three, four, act_grad, third_grad)
    three = reduce_core(three)
    four = reduce_step(four, last, 3)
    second_grad = third_grad + dot_t(act_grad, expand_weight)
    second_sum_grad, second_gain_grad, second_shift_grad = norm_backward(second_grad, normed_two, inverse_two, second_gain)
    merge_in = second_sum_grad.astype(BF16)
    merge_bias_grad = token_sum(merge_in)
    mixed_two_grad = dot_t(merge_in, wm).astype(BF16)
    mixed_two_grad, three, four = tie(mixed_two_grad, three, four)
    three = reduce_step(three, last, 3)
    four = reduce_step(four, last, 2)
    probe_in, lookup_part, content_part = attend_backward(query_two, key_two, value_two, mixed_two, mixed_two_grad, log_two, cross_masks, block)
    probe_in, lookup_part, content_part, three, four = tie(probe_in, lookup_part, content_part, three, four)
    three = reduce_step(three, last, 2)
    four = reduce_step(four, last, 1)
    first_grad = second_sum_grad + dot_t(probe_in, wp)
    first_sum_grad, first_gain_grad, first_shift_grad = norm_backward(first_grad, normed_one, inverse_one, first_gain)
    output_in = first_sum_grad.astype(BF16)
    mixed_one_grad = dot_t(output_in, wo).astype(BF16)
    split = split_heads(mixed_one_grad, me, seq, space)
    split, three, four, probe_in, lookup_part, content_part, output_in = tie(split, three, four, probe_in, lookup_part, content_part, output_in)
    came = exchange([split[d] for d in range(seq)])
    mixed_row_grad = jnp.concatenate([came[o] for o in offsets], axis=0)
    three = reduce_step(three, last, 1)
    four = reduce_step(four, last, 0)
    output_bias_grad = token_sum(output_in)
    probe_bias_grad = token_sum(probe_in)
    content_bias_grad = token_sum(content_part)
    cross_grads = [
        t_dot(mixed_one, output_in),
        t_dot(first_out, probe_in),
        t_dot(memory_row, lookup_part),
        t_dot(memory_row, content_part),
        t_dot(mixed_two, merge_in),
    ]
    two = reduce_start(cross_grads, back)
    mixed_row_grad, two, three, four, lookup_part, content_part = tie(mixed_row_grad, two, three, four, lookup_part, content_part)
    two = reduce_core(two)
    three = reduce_step(three, last, 0)
    memory_part = (dot_t(lookup_part, wl) + dot_t(content_part, wc)).reshape(seq, local, width)
    mixed_row_grad, two, three, memory_part = tie(mixed_row_grad, two, three, memory_part)
    two = reduce_step(two, back, 3)
    memory_part = seq_reduce(memory_part, bits[:0:-1])
    qkv_grad = row_backward(qkv, mixed_row, mixed_row_grad, log_one, self_masks, heads, local, block)
    qkv_grad, two, memory_part = tie(qkv_grad, two, memory_part)
    two = reduce_step(two, back, 2)
    memory_grad = seq_reduce(memory_part, bits[:1])[0]
    row_grad = t_dot(target_row, qkv_grad)
    sums = token_sum(qkv_grad)
    spot = lambda v: lax.dynamic_update_slice(jnp.zeros((1, width), F32), v, (0, place_in_row * span))
    vector_grads = (
        spot(sums[:, :span]),
        spot(sums[:, 2 * space : 2 * space + span]),
        output_bias_grad,
        first_gain_grad,
        first_shift_grad,
        probe_bias_grad,
        content_bias_grad,
        merge_bias_grad,
        second_gain_grad,
        second_shift_grad,
        shrink_bias_grad,
        third_gain_grad,
        third_shift_grad,
    )
    tail = pack_sums(vector_grads, expand_bias_grad, width)
    terms = [row_grad.astype(BF16).reshape(owners(), -1, BLOCK, width), tail.reshape(owners(), -1, BLOCK, width)]
    one = tuple(spread(terms, group_owners(near)))
    one, qkv_grad, two, memory_grad = tie(one, qkv_grad, two, memory_grad)
    one = reduce_step(one, near, 2)
    two = reduce_step(two, back, 1)
    target_part = dot_t(qkv_grad, wqkv).reshape(seq, local, width)
    one, two, target_part = tie(one, two, target_part)
    one = reduce_step(one, near, 1)
    target_part = seq_reduce(target_part, bits[:0:-1])
    one, two, target_part = tie(one, two, target_part)
    one = reduce_step(one, near, 0)
    target_grad = first_sum_grad + seq_reduce(target_part, bits[:1])[0]
    slots = one[0].astype(BF16).reshape(seq, -1, width)
    slots, two = tie(slots, two)
    one = exchange([slots[d] for d in range(seq)])
    two = reduce_step(two, back, 0)

    query_grad, key_grad, value_grad, wide_sum = unpack_heads(one, me, 3, rows)
    two, three, four = (reduce_finish(t) for t in (two, three, four))
    sums = [wide_sum[seat(i)[0], seat(i)[1] : seat(i)[1] + rows] for i in range(VECTORS)]
    row, lane = seat(VECTORS)
    result = Params(
        query_weight=query_grad,
        key_weight=key_grad,
        value_weight=value_grad,
        output_weight=two[:rows],
        probe_weight=two[rows : 2 * rows],
        lookup_weight=two[2 * rows : 3 * rows],
        content_weight=two[3 * rows : 4 * rows],
        merge_weight=two[4 * rows :],
        expand_weight=three.reshape(rows, wide),
        shrink_weight=four,
        expand_bias=wide_sum[row, lane : lane + wide // owners()],
        query_bias=sums[0],
        value_bias=sums[1],
        output_bias=sums[2],
        first_gain=sums[3],
        first_shift=sums[4],
        probe_bias=sums[5],
        content_bias=sums[6],
        merge_bias=sums[7],
        second_gain=sums[8],
        second_shift=sums[9],
        shrink_bias=sums[10],
        third_gain=sums[11],
        third_shift=sums[12],
    )
    return (layer_output[None], target_grad[None], memory_grad[None]) + tuple(result)


def solution(mesh):
    tokens = P("dp", "seq", None)
    matrix = P(ALL, None)
    vector = P(ALL)
    params = Params(*[vector] * len(Params._fields))._replace(
        query_weight=matrix,
        key_weight=matrix,
        value_weight=matrix,
        output_weight=matrix,
        probe_weight=matrix,
        lookup_weight=matrix,
        content_weight=matrix,
        merge_weight=matrix,
        expand_weight=matrix,
        shrink_weight=matrix,
    )
    split = mesh.size == FLAT and mesh.shape["seq"] == 4
    return jax.shard_map(
        per_device if split else per_device_by_rows,
        mesh=mesh,
        in_specs=(tokens, tokens, tokens, P("dp", "seq"), P("dp", "seq")) + tuple(params),
        out_specs=(tokens, tokens, tokens) + tuple(params),
        check_vma=False,
    )
```

```python
from typing import Any, NamedTuple

import jax
import jax.numpy as jnp
from jax import lax
from jax.experimental import pallas as pl
from jax.experimental.pallas import tpu as pltpu
from jax.sharding import PartitionSpec as P

HEAD_DIM = 64
PAIR = 2 * HEAD_DIM
NEG_FILL = -1e30
EPSILON = 1e-05
BF16 = jnp.bfloat16
F32 = jnp.float32
ALL = ("dp", "seq")

class Params(NamedTuple):
    query_weight: Any
    query_bias: Any
    key_weight: Any
    value_weight: Any
    value_bias: Any
    output_weight: Any
    output_bias: Any
    first_gain: Any
    first_shift: Any
    probe_weight: Any
    probe_bias: Any
    lookup_weight: Any
    content_weight: Any
    content_bias: Any
    merge_weight: Any
    merge_bias: Any
    second_gain: Any
    second_shift: Any
    expand_weight: Any
    expand_bias: Any
    shrink_weight: Any
    shrink_bias: Any
    third_gain: Any
    third_shift: Any


def vectors_of(p):
    return (
        p.query_bias,
        p.value_bias,
        p.output_bias,
        p.first_gain,
        p.first_shift,
        p.probe_bias,
        p.content_bias,
        p.merge_bias,
        p.second_gain,
        p.second_shift,
        p.shrink_bias,
        p.third_gain,
        p.third_shift,
    )


VECTORS = 13
LANES = 128


def dot(left, right):
    return jnp.dot(left, right, preferred_element_type=F32)


def dot_t(left, right):
    return lax.dot_general(left, right, (((1,), (1,)), ((), ())), preferred_element_type=F32)


def t_dot(left, right):
    return lax.dot_general(left, right, (((0,), (0,)), ((), ())), preferred_element_type=F32)


def token_sum(values):
    return jnp.sum(values.astype(F32), axis=0, keepdims=True)


def fill_mask(block, first, qseg, kseg_ref, kpos_ref, bias, base, flags, row):
    rows = qseg.shape[0]
    place = first + lax.broadcasted_iota(jnp.int32, (rows, block), 0)
    for j in range(bias.shape[1] // block):
        cols = pl.ds(j * block, block)
        allowed = (kseg_ref[:, cols] == qseg) & (kpos_ref[:, cols] <= place)
        term = jnp.where(allowed, 0.0, NEG_FILL)
        bias[pl.ds(base, rows), cols] = term
        flags[row, j] = (jnp.max(term) > -1.0).astype(jnp.int32)


def one_head(value, head):
    lane = lax.broadcasted_iota(jnp.int32, value.shape, 1)
    return jnp.where((lane < HEAD_DIM) == (head == 0), value, jnp.zeros_like(value))


def stacked(value, halves):
    return jnp.concatenate([one_head(value, head) for head in range(halves)], axis=0)


def tiles_forward(block, tiles, bias, flags, scores, peaks, sums, mixed):
    rows, total = bias.shape
    peaks[...] = jnp.full(peaks.shape, NEG_FILL, F32)
    sums[...] = jnp.zeros(sums.shape, F32)
    mixed[...] = jnp.zeros(mixed.shape, F32)
    for j in range(total // block):

        @pl.when(flags[0, j] > 0)
        def _():
            cols = pl.ds(j * block, block)
            for query, key, _, at in tiles:
                part = dot_t(query, key(cols))
                for half in range(query.shape[0] // rows):
                    own = pl.ds(at + half * rows, rows)
                    term = part[half * rows : (half + 1) * rows] + bias[:, cols]
                    scores[own, cols] = term
                    high = peaks[own]
                    for c in range(block // LANES):
                        high = jnp.maximum(high, term[:, c * LANES : (c + 1) * LANES])
                    peaks[own] = high

    peak = jnp.max(peaks[...], axis=-1, keepdims=True)
    peaks[...] = jnp.broadcast_to(peak, peaks.shape)
    for j in range(total // block):

        @pl.when(flags[0, j] > 0)
        def _():
            cols = pl.ds(j * block, block)
            for query, _, value, at in tiles:
                own = pl.ds(at, query.shape[0])
                part = jnp.exp(scores[own, cols] - peaks[own, 0:1])
                add = sums[own]
                for c in range(block // LANES):
                    add = add + part[:, c * LANES : (c + 1) * LANES]
                sums[own] = add
                mixed[own] += dot(part.astype(BF16), value(cols))

    whole = jnp.sum(sums[...], axis=-1, keepdims=True)
    return mixed[...] * (1.0 / whole), peak + jnp.log(whole)


def tiles_backward(block, tiles, bias, flags, query_sum, key_sum, value_sum):
    rows, total = bias.shape
    query_sum[...] = jnp.zeros(query_sum.shape, F32)
    for j in range(total // block):

        @pl.when(flags[0, j] > 0)
        def _():
            cols = pl.ds(j * block, block)
            for query, grad, log, inner, key_of, value, at, lanes in tiles:
                key = key_of(cols)
                scores = dot_t(query, key)
                slope = dot_t(grad, value(cols))
                terms = [scores[i : i + rows] + bias[:, cols] for i in range(0, query.shape[0], rows)]
                part = jnp.exp((jnp.concatenate(terms, axis=0) if len(terms) > 1 else terms[0]) - log)
                score_grad = (part * (slope - inner)).astype(BF16)
                query_sum[pl.ds(at, query.shape[0])] += dot(score_grad, key)
                key_sum[cols, lanes] += t_dot(score_grad, query)
                value_sum[cols, lanes] += t_dot(part.astype(BF16), grad)


def lower_lanes(shape):
    return lax.broadcasted_iota(jnp.int32, shape, 1) < HEAD_DIM


def eighth(value):
    return (value.astype(BF16) * 0.125).astype(BF16)


def attend_kernel(block, q0_ref, q_ref, k_ref, v_ref, qseg_ref, kseg_ref, kpos_ref, o_ref, log_ref, bias, flags, *scratch):
    @pl.when(pl.program_id(0) == 0)
    def _():
        fill_mask(block, q0_ref[0], qseg_ref[...], kseg_ref, kpos_ref, bias, 0, flags, 0)

    rows = o_ref.shape[0]
    tile = (stacked(q_ref[...], 2), lambda cols: k_ref[cols, :], lambda cols: v_ref[cols, :], 0)
    out, log = tiles_forward(block, [tile], bias, flags, *scratch)
    low = lower_lanes(o_ref.shape)
    o_ref[...] = jnp.where(low, out[:rows], out[rows:]).astype(BF16)
    log_ref[...] = jnp.where(low, log[:rows], log[rows:])


def attend_back_kernel(block, q0_ref, q_ref, k_ref, v_ref, o_ref, g_ref, log_ref, qseg_ref, kseg_ref, kpos_ref, dq_ref, dk_ref, dv_ref, bias, flags, query_sum, key_sum, value_sum):
    @pl.when(pl.program_id(0) == 0)
    def _():
        fill_mask(block, q0_ref[0], qseg_ref[...], kseg_ref, kpos_ref, bias, 0, flags, 0)

    key_sum[...] = jnp.zeros(key_sum.shape, F32)
    value_sum[...] = jnp.zeros(value_sum.shape, F32)
    rows = q_ref.shape[0]
    grad = stacked(g_ref[...], 2)
    mixed = o_ref[...].astype(F32)
    inner = jnp.sum(grad.astype(F32) * jnp.concatenate([mixed, mixed], axis=0), axis=-1, keepdims=True)
    log = jnp.concatenate([log_ref[:, 0:1], log_ref[:, HEAD_DIM : HEAD_DIM + 1]], axis=0)
    tile = (stacked(q_ref[...], 2), grad, log, inner, lambda cols: k_ref[cols, :], lambda cols: v_ref[cols, :], 0, pl.ds(0, PAIR))
    tiles_backward(block, [tile], bias, flags, query_sum, key_sum, value_sum)
    dq_ref[...] = eighth(jnp.where(lower_lanes(dq_ref.shape), query_sum[:rows], query_sum[rows:]))
    dk_ref[...] = key_sum[...].astype(BF16)
    dv_ref[...] = value_sum[...].astype(BF16)


def attend_specs(rows, total):
    whole = lambda shape: pl.BlockSpec(shape, lambda i: (0, 0))
    strip = lambda count: pl.BlockSpec((count, PAIR), lambda i: (0, i))
    return (
        pl.BlockSpec(memory_space=pltpu.SMEM),
        strip(rows),
        strip(total),
        [whole((rows, 1)), whole((1, total)), whole((1, total))],
    )


def forward_scratch(rows, total, heads):
    return [pltpu.VMEM((heads * rows, total), F32)] + [pltpu.VMEM((heads * rows, LANES), F32)] * 3


def attend_forward(query, key, value, masks, block):
    rows, width = query.shape
    total = key.shape[0]
    scalar, narrow, tall, marks = attend_specs(rows, total)
    q0, qseg, kseg, kpos = masks
    return pl.pallas_call(
        lambda *refs: attend_kernel(block, *refs),
        grid=(width // PAIR,),
        in_specs=[scalar, narrow, tall, tall] + marks,
        out_specs=[narrow, narrow],
        out_shape=[jax.ShapeDtypeStruct((rows, width), BF16), jax.ShapeDtypeStruct((rows, width), F32)],
        scratch_shapes=[pltpu.VMEM((rows, total), F32), pltpu.SMEM((1, total // block), jnp.int32)] + forward_scratch(rows, total, 2),
        cost_estimate=pl.CostEstimate(flops=8 * rows * total * width, bytes_accessed=8 * total * width, transcendentals=rows * total * 12),
        compiler_params=pltpu.CompilerParams(dimension_semantics=("arbitrary",)),
        name="attend_forward",
    )(q0, query, key, value, qseg, kseg, kpos)


def attend_backward(query, key, value, mixed, grad, log, masks, block):
    rows, width = query.shape
    total = key.shape[0]
    scalar, narrow, tall, marks = attend_specs(rows, total)
    q0, qseg, kseg, kpos = masks
    return pl.pallas_call(
        lambda *refs: attend_back_kernel(block, *refs),
        grid=(width // PAIR,),
        in_specs=[scalar, narrow, tall, tall, narrow, narrow, narrow] + marks,
        out_specs=[narrow, tall, tall],
        out_shape=[
            jax.ShapeDtypeStruct((rows, width), BF16),
            jax.ShapeDtypeStruct((total, width), BF16),
            jax.ShapeDtypeStruct((total, width), BF16),
        ],
        scratch_shapes=[
            pltpu.VMEM((rows, total), F32),
            pltpu.SMEM((1, total // block), jnp.int32),
            pltpu.VMEM((2 * rows, PAIR), F32),
            pltpu.VMEM((total, PAIR), F32),
            pltpu.VMEM((total, PAIR), F32),
        ],
        cost_estimate=pl.CostEstimate(flops=20 * rows * total * width, bytes_accessed=16 * total * width, transcendentals=rows * total * 12),
        compiler_params=pltpu.CompilerParams(dimension_semantics=("arbitrary",)),
        name="attend_backward",
    )(q0, query, key, value, mixed, grad, log, qseg, kseg, kpos)


def seats_of(heads, space):
    return [(pl.ds(t, PAIR), pl.ds(space + t, PAIR), pl.ds(2 * space + t, PAIR), min(2, heads - 2 * (t // PAIR))) for t in range(0, space, PAIR)]


def row_kernel(block, heads, q0_ref, qkv_ref, qseg_ref, kseg_ref, kpos_ref, o_ref, log_ref, bias, flags, *scratch):
    rows, space = o_ref.shape
    step = pl.program_id(0)
    own = pl.ds(pl.multiple_of(step * rows, rows), rows)
    fill_mask(block, q0_ref[step], qseg_ref[...], kseg_ref, kpos_ref, bias, 0, flags, 0)
    tiles = []
    for tile, (query_lanes, key_lanes, value_lanes, halves) in enumerate(seats_of(heads, space)):
        key = lambda cols, lanes=key_lanes: qkv_ref[cols, lanes]
        value = lambda cols, lanes=value_lanes: qkv_ref[cols, lanes]
        tiles.append((stacked(qkv_ref[own, query_lanes], halves), key, value, 2 * tile * rows))
    out, log = tiles_forward(block, tiles, bias, flags, *scratch)
    low = lower_lanes((rows, PAIR))
    blank = jnp.zeros((rows, PAIR), F32)
    for query, _, _, at in tiles:
        lanes = pl.ds(at // (2 * rows) * PAIR, PAIR)
        pair = query.shape[0] > rows
        o_ref[:, lanes] = jnp.where(low, out[at : at + rows], out[at + rows : at + 2 * rows] if pair else blank).astype(BF16)
        log_ref[:, lanes] = jnp.where(low, log[at : at + rows], log[at + rows : at + 2 * rows] if pair else blank)


def row_back_kernel(block, heads, q0_ref, qkv_ref, o_ref, g_ref, log_ref, qseg_ref, kseg_ref, kpos_ref, grads_ref, bias, flags, query_sum, key_sum, value_sum):
    rows, space = o_ref.shape
    step = pl.program_id(0)
    own = pl.ds(pl.multiple_of(step * rows, rows), rows)
    fill_mask(block, q0_ref[step], qseg_ref[...], kseg_ref, kpos_ref, bias, 0, flags, 0)

    @pl.when(step == 0)
    def _():
        key_sum[...] = jnp.zeros(key_sum.shape, F32)
        value_sum[...] = jnp.zeros(value_sum.shape, F32)

    tiles = []
    for tile, (query_lanes, key_lanes, value_lanes, halves) in enumerate(seats_of(heads, space)):
        key = lambda cols, lanes=key_lanes: qkv_ref[cols, lanes]
        value = lambda cols, lanes=value_lanes: qkv_ref[cols, lanes]
        grad = stacked(g_ref[:, query_lanes], halves)
        mixed = o_ref[:, query_lanes].astype(F32)
        inner = jnp.sum(grad.astype(F32) * jnp.concatenate([mixed] * halves, axis=0), axis=-1, keepdims=True)
        lane = tile * PAIR
        log = jnp.concatenate([log_ref[:, lane + i * HEAD_DIM : lane + i * HEAD_DIM + 1] for i in range(halves)], axis=0)
        tiles.append((stacked(qkv_ref[own, query_lanes], halves), grad, log, inner, key, value, 2 * tile * rows, query_lanes))
    tiles_backward(block, tiles, bias, flags, query_sum, key_sum, value_sum)
    low = lower_lanes((rows, PAIR))
    for query, _, _, _, _, _, at, lanes in tiles:
        upper = query_sum[at + rows : at + 2 * rows] if query.shape[0] > rows else jnp.zeros((rows, PAIR), F32)
        grads_ref[own, lanes] = eighth(jnp.where(low, query_sum[at : at + rows], upper))

    @pl.when(step == pl.num_programs(0) - 1)
    def _():
        grads_ref[:, space : 2 * space] = key_sum[...].astype(BF16)
        grads_ref[:, 2 * space :] = value_sum[...].astype(BF16)


def row_specs(rows, total, space):
    whole = lambda shape: pl.BlockSpec(shape, lambda i: (0, 0))
    strip = lambda width: pl.BlockSpec((rows, width), lambda i: (i, 0))
    return (
        pl.BlockSpec(memory_space=pltpu.SMEM),
        whole((total, 3 * space)),
        strip(space),
        [strip(1), whole((1, total)), whole((1, total))],
    )


def row_forward(qkv, masks, heads, rows, block):
    total, space = qkv.shape[0], qkv.shape[1] // 3
    scalar, full, narrow, marks = row_specs(rows, total, space)
    q0, qseg, kseg, kpos = masks
    return pl.pallas_call(
        lambda *refs: row_kernel(block, heads, *refs),
        grid=(total // rows,),
        in_specs=[scalar, full] + marks,
        out_specs=[narrow, narrow],
        out_shape=[jax.ShapeDtypeStruct((total, space), BF16), jax.ShapeDtypeStruct((total, space), F32)],
        scratch_shapes=[pltpu.VMEM((rows, total), F32), pltpu.SMEM((1, total // block), jnp.int32)] + forward_scratch(rows, total, heads),
        cost_estimate=pl.CostEstimate(flops=4 * total * total * space, bytes_accessed=10 * total * space, transcendentals=total * total * heads),
        compiler_params=pltpu.CompilerParams(dimension_semantics=("arbitrary",)),
        name="row_forward",
    )(q0, qkv, qseg, kseg, kpos)


def row_backward(qkv, mixed, grad, log, masks, heads, rows, block):
    total, space = mixed.shape
    scalar, full, narrow, marks = row_specs(rows, total, space)
    q0, qseg, kseg, kpos = masks
    return pl.pallas_call(
        lambda *refs: row_back_kernel(block, heads, *refs),
        grid=(total // rows,),
        in_specs=[scalar, full, narrow, narrow, narrow] + marks,
        out_specs=full,
        out_shape=jax.ShapeDtypeStruct((total, 3 * space), BF16),
        scratch_shapes=[
            pltpu.VMEM((rows, total), F32),
            pltpu.SMEM((1, total // block), jnp.int32),
            pltpu.VMEM((heads * rows, PAIR), F32),
            pltpu.VMEM((total, space), F32),
            pltpu.VMEM((total, space), F32),
        ],
        cost_estimate=pl.CostEstimate(flops=10 * total * total * space, bytes_accessed=20 * total * space, transcendentals=total * total * heads),
        compiler_params=pltpu.CompilerParams(dimension_semantics=("arbitrary",)),
        name="row_backward",
    )(q0, qkv, mixed, grad, log, qseg, kseg, kpos)


def split_kernel(span, me_ref, value_ref, out_ref):
    rows, space = out_ref.shape[1:]
    for group in range(out_ref.shape[0]):
        part = value_ref[:, group * span : (group + 1) * span].astype(F32)
        out_ref[me_ref[0] ^ group] = jnp.concatenate([part, jnp.zeros((rows, space - span), F32)], axis=1).astype(BF16)


def split_heads(value, me, groups, space):
    rows, width = value.shape
    return pl.pallas_call(
        lambda *refs: split_kernel(width // groups, *refs),
        out_shape=jax.ShapeDtypeStruct((groups, rows, space), BF16),
        in_specs=[pl.BlockSpec(memory_space=pltpu.SMEM), pl.BlockSpec(memory_space=pltpu.VMEM)],
        out_specs=pl.BlockSpec(memory_space=pltpu.VMEM),
        name="split_heads",
    )(me, value)


def join_kernel(span, me_ref, *refs):
    pieces, (out_ref, held) = refs[:-2], refs[-2:]
    for d, piece in enumerate(pieces):
        held[d] = piece[...]
    parts = [held[me_ref[0] ^ group].astype(F32)[:, :span] for group in range(len(pieces))]
    out_ref[...] = jnp.concatenate(parts, axis=1).astype(BF16)


def join_heads(pieces, me, span):
    rows, space = pieces[0].shape
    groups = len(pieces)
    vmem = pl.BlockSpec(memory_space=pltpu.VMEM)
    return pl.pallas_call(
        lambda *refs: join_kernel(span, *refs),
        out_shape=jax.ShapeDtypeStruct((rows, groups * span), BF16),
        in_specs=[pl.BlockSpec(memory_space=pltpu.SMEM)] + [vmem] * groups,
        out_specs=vmem,
        scratch_shapes=[pltpu.VMEM((groups, rows, space), BF16)],
        name="join_heads",
    )(me, *pieces)


def pack_heads_kernel(weights, span, me_ref, *refs):
    out_ref = refs[-1]
    vectors = refs[weights][...]
    rows = refs[0].shape[0]
    space = out_ref.shape[2] // weights
    for group in range(out_ref.shape[0]):
        parts = []
        for ref in refs[:weights]:
            parts += [ref[:, group * span : (group + 1) * span].astype(F32), jnp.zeros((rows, space - span), F32)]
        out_ref[me_ref[0] ^ group, :rows] = jnp.concatenate(parts, axis=1).astype(BF16)
        out_ref[me_ref[0] ^ group, rows:] = vectors


def pack_heads(weights, vectors, me, groups):
    rows, width = weights[0].shape
    vmem = pl.BlockSpec(memory_space=pltpu.VMEM)
    return pl.pallas_call(
        lambda *refs: pack_heads_kernel(len(weights), width // groups, *refs),
        out_shape=jax.ShapeDtypeStruct((groups, rows + vectors.shape[0], width), BF16),
        in_specs=[pl.BlockSpec(memory_space=pltpu.SMEM)] + [vmem] * (len(weights) + 1),
        out_specs=vmem,
        name="pack_heads",
    )(me, *weights, vectors)


def unpack_heads_kernel(weights, span, me_ref, *refs):
    groups = len(refs) - weights - 2
    pieces, outs, tail_ref, held = refs[:groups], refs[groups:-2], refs[-2], refs[-1]
    rows = outs[0].shape[0]
    space = pieces[0].shape[1] // weights
    for d, piece in enumerate(pieces):
        held[d] = piece[...].astype(F32)
    for i, out in enumerate(outs):
        out[...] = jnp.concatenate([held[me_ref[0] ^ group, :rows, i * space : i * space + span] for group in range(groups)], axis=1)
    tail_ref[...] = sum(held[d, rows:] for d in range(groups))


def unpack_heads(pieces, me, weights, rows):
    groups = len(pieces)
    width = pieces[0].shape[1]
    vmem = pl.BlockSpec(memory_space=pltpu.VMEM)
    return pl.pallas_call(
        lambda *refs: unpack_heads_kernel(weights, width // groups, *refs),
        out_shape=[jax.ShapeDtypeStruct((rows, width), F32)] * weights + [jax.ShapeDtypeStruct((pieces[0].shape[0] - rows, width), F32)],
        in_specs=[pl.BlockSpec(memory_space=pltpu.SMEM)] + [vmem] * groups,
        out_specs=[vmem] * (weights + 1),
        scratch_shapes=[pltpu.VMEM((groups,) + pieces[0].shape, F32)],
        name="unpack_heads",
    )(me, *pieces)


def norm_forward(hidden, gain, shift):
    centred = hidden - jnp.mean(hidden, axis=-1, keepdims=True)
    inverse = lax.rsqrt(jnp.mean(centred * centred, axis=-1, keepdims=True) + EPSILON)
    normed = centred * inverse
    return normed * gain + shift, normed, inverse


def norm_backward(upstream, normed, inverse, gain):
    scaled = upstream * gain
    inner = jnp.mean(scaled, axis=-1, keepdims=True)
    along = jnp.mean(scaled * normed, axis=-1, keepdims=True)
    return inverse * (scaled - inner - normed * along), token_sum(upstream * normed), token_sum(upstream)


def exact_gelu(values):
    return jax.nn.gelu(values, approximate=False)


def expand_kernel(value_ref, weight_ref, bias_ref, hidden_ref, slope_ref):
    act = dot(value_ref[...], weight_ref[...]) + bias_ref[...]
    share = 0.5 + 0.5 * lax.erf(act * ROOT_HALF)
    hidden_ref[...] = (act * share).astype(BF16)
    slope_ref[...] = share + act * (jnp.exp(-0.5 * act * act) * DENSITY)


ROOT_HALF = 0.7071067811865476
DENSITY = 0.3989422804014327


def expand_gelu(value, weight, bias):
    rows, width = value.shape
    wide = weight.shape[1]
    step = 4 * LANES
    strip = lambda count: pl.BlockSpec((count, step), lambda i: (0, i))
    return pl.pallas_call(
        expand_kernel,
        grid=(wide // step,),
        in_specs=[pl.BlockSpec((rows, width), lambda i: (0, 0)), strip(width), strip(1)],
        out_specs=[strip(rows), strip(rows)],
        out_shape=[jax.ShapeDtypeStruct((rows, wide), BF16), jax.ShapeDtypeStruct((rows, wide), F32)],
        cost_estimate=pl.CostEstimate(flops=2 * rows * width * wide, bytes_accessed=2 * width * wide + 6 * rows * wide, transcendentals=2 * rows * wide),
        compiler_params=pltpu.CompilerParams(dimension_semantics=("arbitrary",)),
        name="expand_gelu",
    )(value, weight, bias)


def seq_offsets(count):
    offsets = [0]
    bit = count // 2
    while bit:
        offsets = offsets + [o ^ bit for o in offsets]
        bit //= 2
    return offsets


def swap(value, axis, bit):
    count = lax.axis_size(axis)
    return lax.ppermute(value, axis, [(i, i ^ bit) for i in range(count)])


def seq_bits():
    bit = lax.axis_size("seq") // 2
    bits = []
    while bit:
        bits.append(bit)
        bit //= 2
    return bits


def seq_gather(rows, bits):
    for bit in bits:
        rows = jnp.concatenate([rows, swap(rows, "seq", bit)], axis=0)
    return rows


def seq_reduce(total, bits):
    for bit in bits:
        half = total.shape[0] // 2
        got = swap(total[half:].astype(BF16), "seq", bit)
        total = total[:half].astype(F32) + got.astype(F32)
    return total


def tie(*values):
    return lax.optimization_barrier(values)


NEAR_LAST = ((16, 8, 2, 4), (8, 16, 4, 2))
NEAR_FIRST = ((2, 4, 8, 16), (4, 2, 16, 8))
DP_LAST = ((16, 8, 4), (4, 16, 8))
NEAR_BACK = ((16, 2, 8, 4), (16, 2, 4, 8))
BLOCK = 8


FLAT = 2 ** (len(NEAR_LAST[0]) + 1)


def owners():
    return lax.axis_size("dp") * lax.axis_size("seq")


def staged():
    return owners() == 2 ** (len(NEAR_LAST[0]) + 1)


def slot_owners(plan):
    def masks(core):
        found = [0]
        for bit in plan[core]:
            found = found + [o ^ bit for o in found]
        return found

    me = lax.axis_index(ALL)
    even = jnp.array(masks(0) + [1 ^ m for m in masks(1)], jnp.int32)
    odd = jnp.array(masks(1) + [1 ^ m for m in masks(0)], jnp.int32)
    return me ^ jnp.where((me & 1) == 0, even, odd)


def group_owners(plan):
    def masks(core):
        found = list(range(lax.axis_size("seq")))
        for bit in plan[core]:
            found = found + [o ^ bit for o in found]
        return found

    me = lax.axis_index(ALL)
    return me ^ jnp.where((me & 1) == 0, jnp.array(masks(0), jnp.int32), jnp.array(masks(1), jnp.int32))


def exchange(pieces):
    return [pieces[0]] + [swap(pieces[d], "seq", d) for d in range(1, len(pieces))]


def stage_swap(value, plan, stage):
    return lax.ppermute(value, ALL, [(d, d ^ plan[d & 1][stage]) for d in range(owners())])


def core_swap(value):
    return lax.ppermute(value, ALL, [(d, d ^ 1) for d in range(owners())])


def place_kernel(groups, rows, counts, order, *refs):
    pieces, refs = refs[: len(counts)], refs[len(counts) :]
    outs, (held, came, left) = refs[:-3], refs[-3:]
    blocks = held.shape[1]
    sizes = [rows] * groups + [blocks - groups * rows] * (len(outs) - groups)
    base = 0
    for piece, count in zip(pieces, counts):

        def fetch(slot, carry):
            pltpu.make_async_copy(piece.at[slot], held.at[base + slot], came.at[base + slot]).start()
            return carry

        lax.fori_loop(0, count, fetch, 0)
        base += count

    def put(slot, carry):
        pltpu.make_async_copy(pieces[0].at[0], held.at[slot], came.at[slot]).wait()
        at = 0
        for out, size in zip(outs, sizes):
            pltpu.make_async_copy(held.at[slot, pl.ds(at, size)], out.at[order[slot]], left).start()
            at += size
        return carry

    lax.fori_loop(0, base, put, 0)

    def finish(slot, carry):
        at = 0
        for out, size in zip(outs, sizes):
            pltpu.make_async_copy(held.at[slot, pl.ds(at, size)], out.at[slot], left).wait()
            at += size
        return carry

    lax.fori_loop(0, base, finish, 0)


def place(pieces, order, groups, rows):
    counts = tuple(p.shape[0] for p in pieces)
    _, blocks, _, width = pieces[0].shape
    devices = sum(counts)
    sizes = [rows] * groups + [blocks - groups * rows] * (blocks > groups * rows)
    anywhere = pl.BlockSpec(memory_space=pl.ANY)
    return pl.pallas_call(
        lambda *refs: place_kernel(groups, rows, counts, *refs),
        out_shape=[jax.ShapeDtypeStruct((devices, size, BLOCK, width), BF16) for size in sizes],
        in_specs=[pl.BlockSpec(memory_space=pltpu.SMEM)] + [anywhere] * len(pieces),
        out_specs=[anywhere] * len(sizes),
        scratch_shapes=[
            pltpu.VMEM((devices, blocks, BLOCK, width), BF16),
            pltpu.SemaphoreType.DMA((devices,)),
            pltpu.SemaphoreType.DMA,
        ],
        cost_estimate=pl.CostEstimate(flops=0, bytes_accessed=4 * devices * blocks * BLOCK * width, transcendentals=0),
        name="place",
    )(order, *pieces)


def spread_kernel(sizes, order, *refs):
    terms, refs = refs[: len(sizes)], refs[len(sizes) :]
    outs, (held, came, left) = refs[:2], refs[2:]
    half = outs[0].shape[0]
    spans = [pl.ds(sum(sizes[:i]), size) for i, size in enumerate(sizes)]
    for i, term in enumerate(terms):
        pltpu.make_async_copy(term, held.at[:, spans[i]], came.at[i]).start()
    for i, term in enumerate(terms):
        pltpu.make_async_copy(term, held.at[:, spans[i]], came.at[i]).wait()
        for index, out in enumerate(outs):

            def put(slot, carry):
                pltpu.make_async_copy(held.at[order[index * half + slot], spans[i]], out.at[slot, spans[i]], left).start()
                return carry

            lax.fori_loop(0, half, put, 0)

    def finish(slot, carry):
        for out in outs:
            for span in spans:
                pltpu.make_async_copy(held.at[slot, span], out.at[slot, span], left).wait()
        return carry

    lax.fori_loop(0, half, finish, 0)


def spread(terms, order):
    devices, _, _, width = terms[0].shape
    sizes = tuple(t.shape[1] for t in terms)
    blocks = sum(sizes)
    shape = jax.ShapeDtypeStruct((devices // 2, blocks, BLOCK, width), BF16)
    anywhere = pl.BlockSpec(memory_space=pl.ANY)
    return pl.pallas_call(
        lambda *refs: spread_kernel(sizes, *refs),
        out_shape=[shape, shape],
        in_specs=[pl.BlockSpec(memory_space=pltpu.SMEM)] + [anywhere] * len(terms),
        out_specs=[anywhere] * 2,
        scratch_shapes=[
            pltpu.VMEM((devices, blocks, BLOCK, width), BF16),
            pltpu.SemaphoreType.DMA((len(sizes),)),
            pltpu.SemaphoreType.DMA,
        ],
        cost_estimate=pl.CostEstimate(flops=0, bytes_accessed=4 * devices * blocks * BLOCK * width, transcendentals=0),
        name="spread",
    )(order, *terms)


def seat(index):
    return index % BLOCK, LANES * (index // BLOCK)


def pack_vectors_kernel(*refs):
    out, held = refs[-2:]
    held[...] = jnp.zeros(held.shape, F32)
    for i, ref in enumerate(refs[:-2]):
        row, lane = seat(i)
        held[row : row + 1, lane : lane + ref.shape[1]] = ref[...].astype(F32)
    out[...] = held[...].astype(BF16)


def pack_vectors(vectors, width):
    return pl.pallas_call(
        pack_vectors_kernel,
        out_shape=jax.ShapeDtypeStruct((BLOCK, width), BF16),
        in_specs=[pl.BlockSpec(memory_space=pltpu.VMEM)] * len(vectors),
        out_specs=pl.BlockSpec(memory_space=pltpu.VMEM),
        scratch_shapes=[pltpu.VMEM((BLOCK, width), F32)],
        name="pack_vectors",
    )(*[v.reshape(1, -1) for v in vectors])


def unpack_vectors_kernel(blocks, out, wide):
    rows = out.shape[1] // blocks.shape[0]
    span = wide.shape[1] // blocks.shape[0]
    row, lane = seat(VECTORS)
    for d in range(blocks.shape[0]):
        for half in range(2):
            part = blocks[d, :, LANES * half : LANES * (half + 1)].astype(F32)
            out[half * BLOCK : (half + 1) * BLOCK, d * rows : (d + 1) * rows] = part[:, :rows]
            if half == lane // LANES:
                wide[:, d * span : (d + 1) * span] = part[row : row + 1, :span]


def unpack_vectors(blocks, width, wide):
    return pl.pallas_call(
        unpack_vectors_kernel,
        grid=(1,),
        in_specs=[pl.BlockSpec((blocks.shape[0], BLOCK, 2 * LANES), lambda i: (0, 0, 0))],
        out_specs=[pl.BlockSpec((2 * BLOCK, width), lambda i: (0, 0)), pl.BlockSpec((1, wide), lambda i: (0, 0))],
        out_shape=[jax.ShapeDtypeStruct((2 * BLOCK, width), F32), jax.ShapeDtypeStruct((1, wide), F32)],
        name="unpack_vectors",
    )(blocks)


def pack_sums_kernel(*refs):
    out = refs[-1]
    vectors, wide = refs[:-2], refs[-2]
    devices = out.shape[0]
    rows = vectors[0].shape[0] // devices
    span = wide.shape[1] // devices
    table = jnp.concatenate([v[...].reshape(1, -1) for v in vectors] + [jnp.zeros((2 * BLOCK - len(vectors), vectors[0].shape[0]), F32)], axis=0)
    row, lane = seat(VECTORS)
    blank = jnp.zeros((BLOCK, LANES - rows), F32)
    empty = jnp.zeros((BLOCK, out.shape[2] - 2 * LANES), F32)
    line = lax.broadcasted_iota(jnp.int32, (BLOCK, LANES), 0)
    for d in range(devices):
        parts = [table[half * BLOCK : (half + 1) * BLOCK, d * rows : (d + 1) * rows] for half in range(2)]
        parts = [jnp.concatenate([part, blank], axis=1) for part in parts]
        strip = jnp.concatenate([wide[:, d * span : (d + 1) * span], jnp.zeros((1, LANES - span), F32)], axis=1)
        parts[lane // LANES] = jnp.where(line == row, strip, parts[lane // LANES])
        out[d] = jnp.concatenate(parts + [empty], axis=1).astype(BF16)


def pack_sums(vectors, wide, width):
    return pl.pallas_call(
        pack_sums_kernel,
        out_shape=jax.ShapeDtypeStruct((owners(), BLOCK, width), BF16),
        in_specs=[pl.BlockSpec(memory_space=pltpu.VMEM)] * (len(vectors) + 1),
        out_specs=pl.BlockSpec(memory_space=pltpu.VMEM),
        name="pack_sums",
    )(*[v.reshape(-1) for v in vectors], wide)


def gather_start(shards):
    parts = jnp.concatenate(list(shards), axis=0) if len(shards) > 1 else shards[0]
    return parts.reshape(1, -1, BLOCK, parts.shape[1]) if staged() else parts


def gather_step(value, plan, stage):
    return jnp.concatenate([value, stage_swap(value, plan, stage)], axis=0) if staged() else value


def gather_last(value, plan):
    return (value, stage_swap(value, plan, len(plan[0]) - 1), core_swap(value)) if staged() else (value,)


def gather_finish(halves):
    return halves + (core_swap(halves[1]),) if staged() else (lax.all_gather(halves[0], ALL, axis=0, tiled=False),)


def unpack(pieces, plan, count, rows):
    width = pieces[0].shape[-1]
    if not staged():
        whole = pieces[0]
        weights = [whole[:, i * rows : (i + 1) * rows].reshape(-1, width) for i in range(count)]
        return weights + [whole[:, count * rows :]]
    found = place(pieces, slot_owners(plan), count, rows // BLOCK)
    return [w.reshape(-1, width) for w in found[:count]] + [t.reshape(-1, BLOCK, width) for t in found[count:]]


def reduce_start(terms, plan, tail=None):
    devices = owners()
    width = terms[0].shape[1]
    parts = [t.astype(BF16).reshape(devices, -1, width) for t in terms]
    if tail is not None:
        parts.append(tail)
    if not staged():
        return (jnp.concatenate(parts, axis=1),) * 2
    return tuple(spread([p.reshape(devices, -1, BLOCK, width) for p in parts], slot_owners(plan)))


def add_halves(mine, got):
    half = mine.shape[0] // 2
    add = lambda a, b: (a.astype(F32) + b.astype(F32)).astype(BF16)
    return add(mine[:half], got[:half]), add(mine[half:], got[half:])


def reduce_core(halves):
    own, other = halves
    return add_halves(own, core_swap(other)) if staged() else (own, own)


def reduce_step(pair, plan, stage):
    if not staged():
        return pair
    got = stage_swap(pair[1], plan, stage)
    if stage:
        return add_halves(pair[0], got)
    return (pair[0].astype(F32) + got.astype(F32),) * 2


def reduce_finish(pair):
    if staged():
        return pair[0].reshape(-1, pair[0].shape[-1])
    return lax.psum_scatter(pair[0], ALL, scatter_dimension=0, tiled=False).astype(F32)


def per_device_by_rows(target, memory, cotangent, target_segments, memory_segments, *shards):
    p = Params(*shards)
    target = target[0]
    memory = memory[0]
    local, width = target.shape
    seq = lax.axis_size("seq")
    place_in_row = lax.axis_index("seq")
    offsets = seq_offsets(seq)
    bits = seq_bits()
    block = local
    rows = p.query_weight.shape[0]
    wide = p.expand_weight.shape[1]
    last = NEAR_LAST

    expand_weight = lax.all_gather(p.expand_weight, ALL, axis=0, tiled=True)
    shrink_weight = lax.all_gather(p.shrink_weight, ALL, axis=0, tiled=True)
    vectors = pack_vectors(vectors_of(p) + (p.expand_bias,), width)
    one = gather_start([p.query_weight, p.key_weight, p.value_weight, p.output_weight, vectors])
    two = gather_start([p.probe_weight, p.lookup_weight, p.content_weight, p.merge_weight])
    marks = jnp.stack([target_segments[0], memory_segments[0]]).astype(BF16)
    marks = jnp.pad(marks, ((0, BLOCK - 2), (0, width - local)))
    target_pack = jnp.concatenate([target, marks], axis=0)[None]
    memory_row = memory[None]
    one = gather_step(one, last, 0)
    target_pack = seq_gather(target_pack, bits[:1])
    one, target_pack, two = tie(one, target_pack, two)
    one = gather_step(one, last, 1)
    target_pack = seq_gather(target_pack, bits[1:])
    one, target_pack, two = tie(one, target_pack, two)
    one = gather_step(one, last, 2)
    two = gather_step(two, last, 0)
    target_row = target_pack[:, :local].reshape(-1, width)
    key_places = jnp.concatenate([(place_in_row ^ o) * local + jnp.arange(local, dtype=jnp.int32) for o in offsets])[None]
    target_marks = target_pack[:, local, :local].reshape(1, -1).astype(jnp.int32)
    memory_marks = target_pack[:, local + 1, :local].reshape(1, -1).astype(jnp.int32)
    own_marks = target_segments.reshape(local, 1)
    start = (place_in_row * local).astype(jnp.int32).reshape(1)
    self_masks = (start, own_marks, target_marks, key_places)
    cross_masks = (start, own_marks, memory_marks, jnp.zeros_like(key_places))
    one, two = tie(one, two)
    one = gather_last(one, last)
    two = gather_step(two, last, 1)
    one, two, memory_row = tie(one, two, memory_row)

    wq, wk, wv, wo, blocks = unpack(gather_finish(one), last, 4, rows)
    two = gather_step(two, last, 2)
    memory_row = seq_gather(memory_row, bits[:1])
    named, expand_bias = unpack_vectors(blocks, width, wide)
    (
        query_bias,
        value_bias,
        output_bias,
        first_gain,
        first_shift,
        probe_bias,
        content_bias,
        merge_bias,
        second_gain,
        second_shift,
        shrink_bias,
        third_gain,
        third_shift,
    ) = (named[i : i + 1] for i in range(VECTORS))
    query_one = ((dot(target, wq) + query_bias) * 0.125).astype(BF16)
    key_one = dot(target_row, wk).astype(BF16)
    value_one = (dot(target_row, wv) + value_bias).astype(BF16)
    query_one, key_one, value_one, two, memory_row = tie(query_one, key_one, value_one, two, memory_row)
    mixed_one, log_one = attend_forward(query_one, key_one, value_one, self_masks, block)
    two = gather_last(two, last)
    memory_row = seq_gather(memory_row, bits[1:]).reshape(-1, width)
    mixed_one, log_one, two, memory_row = tie(mixed_one, log_one, two, memory_row)
    first_sum = target.astype(F32) + dot(mixed_one, wo) + output_bias
    first_full, normed_one, inverse_one = norm_forward(first_sum, first_gain, first_shift)
    first_out = first_full.astype(BF16)
    wp, wl, wc, wm, *_ = unpack(gather_finish(two), last, 4, rows)
    query_two = ((dot(first_out, wp) + probe_bias) * 0.125).astype(BF16)
    key_two = dot(memory_row, wl).astype(BF16)
    value_two = (dot(memory_row, wc) + content_bias).astype(BF16)
    mixed_two, log_two = attend_forward(query_two, key_two, value_two, cross_masks, block)
    second_sum = first_out.astype(F32) + dot(mixed_two, wm) + merge_bias
    second_full, normed_two, inverse_two = norm_forward(second_sum, second_gain, second_shift)
    second_out = second_full.astype(BF16)
    pre_act = dot(second_out, expand_weight) + expand_bias
    hidden = exact_gelu(pre_act).astype(BF16)
    third_sum = second_out.astype(F32) + dot(hidden, shrink_weight) + shrink_bias
    third_full, normed_three, inverse_three = norm_forward(third_sum, third_gain, third_shift)
    layer_output = third_full.astype(BF16)

    upstream = cotangent[0].astype(F32)
    third_grad, third_gain_grad, third_shift_grad = norm_backward(upstream, normed_three, inverse_three, third_gain)
    shrink_in = third_grad.astype(BF16)
    shrink_bias_grad = token_sum(shrink_in)
    shrink_grad = t_dot(hidden, shrink_in).astype(BF16)
    shrink_grad, shrink_in, third_grad = tie(shrink_grad, shrink_in, third_grad)
    four = lax.psum_scatter(shrink_grad, ALL, scatter_dimension=0, tiled=True).astype(F32)
    hidden_grad = dot_t(shrink_in, shrink_weight)
    act_grad = jax.vjp(exact_gelu, pre_act)[1](hidden_grad)[0].astype(BF16)
    expand_bias_grad = token_sum(act_grad)
    three = reduce_start([t_dot(second_out, act_grad)], last)
    three, act_grad, third_grad = tie(three, act_grad, third_grad)
    three = reduce_core(three)
    second_grad = third_grad + dot_t(act_grad, expand_weight)
    second_sum_grad, second_gain_grad, second_shift_grad = norm_backward(second_grad, normed_two, inverse_two, second_gain)
    merge_in = second_sum_grad.astype(BF16)
    merge_bias_grad = token_sum(merge_in)
    mixed_two_grad = dot_t(merge_in, wm).astype(BF16)
    mixed_two_grad, three = tie(mixed_two_grad, three)
    three = reduce_step(three, last, 3)
    probe_in, lookup_part, content_part = attend_backward(query_two, key_two, value_two, mixed_two, mixed_two_grad, log_two, cross_masks, block)
    probe_in, lookup_part, content_part, three = tie(probe_in, lookup_part, content_part, three)
    three = reduce_step(three, last, 2)
    probe_bias_grad = token_sum(probe_in)
    content_bias_grad = token_sum(content_part)
    cross_grads = [t_dot(first_out, probe_in), t_dot(memory_row, lookup_part), t_dot(memory_row, content_part), t_dot(mixed_two, merge_in)]
    two = reduce_start(cross_grads, last)
    first_grad = second_sum_grad + dot_t(probe_in, wp)
    first_sum_grad, first_gain_grad, first_shift_grad = norm_backward(first_grad, normed_one, inverse_one, first_gain)
    output_in = first_sum_grad.astype(BF16)
    output_bias_grad = token_sum(output_in)
    mixed_one_grad = dot_t(output_in, wo).astype(BF16)
    two, three, lookup_part, content_part = tie(two, three, lookup_part, content_part)
    two = reduce_core(two)
    three = reduce_step(three, last, 1)
    memory_part = (dot_t(lookup_part, wl) + dot_t(content_part, wc)).reshape(seq, local, width)
    mixed_one_grad, two, three, memory_part = tie(mixed_one_grad, two, three, memory_part)
    two = reduce_step(two, last, 3)
    three = reduce_step(three, last, 0)
    query_in, key_part, value_part = attend_backward(query_one, key_one, value_one, mixed_one, mixed_one_grad, log_one, self_masks, block)
    query_in, key_part, value_part, two, three, memory_part = tie(query_in, key_part, value_part, two, three, memory_part)
    two = reduce_step(two, last, 2)
    memory_part = seq_reduce(memory_part, bits[:0:-1])
    query_bias_grad = token_sum(query_in)
    value_bias_grad = token_sum(value_part)
    self_grads = [t_dot(target, query_in), t_dot(target_row, key_part), t_dot(target_row, value_part), t_dot(mixed_one, output_in)]
    vector_grads = (
        query_bias_grad,
        value_bias_grad,
        output_bias_grad,
        first_gain_grad,
        first_shift_grad,
        probe_bias_grad,
        content_bias_grad,
        merge_bias_grad,
        second_gain_grad,
        second_shift_grad,
        shrink_bias_grad,
        third_gain_grad,
        third_shift_grad,
    )
    one = reduce_start(self_grads, last, pack_sums(vector_grads, expand_bias_grad, width))
    one, two, memory_part, key_part, value_part, query_in = tie(one, two, memory_part, key_part, value_part, query_in)
    one = reduce_core(one)
    two = reduce_step(two, last, 1)
    target_part = (dot_t(key_part, wk) + dot_t(value_part, wv)).reshape(seq, local, width)
    one, two, memory_part, target_part = tie(one, two, memory_part, target_part)
    one = reduce_step(one, last, 3)
    two = reduce_step(two, last, 0)
    target_part = seq_reduce(target_part, bits[:0:-1])
    target_grad = first_sum_grad + dot_t(query_in, wq)
    one, memory_part, target_part, target_grad = tie(one, memory_part, target_part, target_grad)
    one = reduce_step(one, last, 2)
    memory_grad = seq_reduce(memory_part, bits[:1])[0]
    one, target_part, memory_grad = tie(one, target_part, memory_grad)
    one = reduce_step(one, last, 1)
    target_grad = target_grad + seq_reduce(target_part, bits[:1])[0]
    one = reduce_step(one, last, 0)

    one, two, three = (reduce_finish(t) for t in (one, two, three))
    wide_sum = one[4 * rows :]
    sums = [wide_sum[seat(i)[0], seat(i)[1] : seat(i)[1] + rows] for i in range(VECTORS)]
    row, lane = seat(VECTORS)
    result = Params(
        query_weight=one[:rows],
        key_weight=one[rows : 2 * rows],
        value_weight=one[2 * rows : 3 * rows],
        output_weight=one[3 * rows : 4 * rows],
        probe_weight=two[:rows],
        lookup_weight=two[rows : 2 * rows],
        content_weight=two[2 * rows : 3 * rows],
        merge_weight=two[3 * rows :],
        expand_weight=three.reshape(rows, wide),
        shrink_weight=four,
        expand_bias=wide_sum[row, lane : lane + wide // owners()],
        query_bias=sums[0],
        value_bias=sums[1],
        output_bias=sums[2],
        first_gain=sums[3],
        first_shift=sums[4],
        probe_bias=sums[5],
        content_bias=sums[6],
        merge_bias=sums[7],
        second_gain=sums[8],
        second_shift=sums[9],
        shrink_bias=sums[10],
        third_gain=sums[11],
        third_shift=sums[12],
    )
    return (layer_output[None], target_grad[None], memory_grad[None]) + tuple(result)


def per_device(target, memory, cotangent, target_segments, memory_segments, *shards):
    p = Params(*shards)
    target = target[0]
    memory = memory[0]
    local, width = target.shape
    seq = lax.axis_size("seq")
    place_in_row = lax.axis_index("seq")
    me = place_in_row.astype(jnp.int32).reshape(1)
    offsets = seq_offsets(seq)
    bits = seq_bits()
    block = local
    rows = p.query_weight.shape[0]
    wide = p.expand_weight.shape[1]
    last, near, back = NEAR_LAST, DP_LAST, NEAR_BACK
    heads = width // HEAD_DIM // seq
    span = heads * HEAD_DIM
    space = -(-span // PAIR) * PAIR

    vectors = pack_vectors(vectors_of(p) + (p.expand_bias,), width)
    packed = pack_heads([p.query_weight, p.key_weight, p.value_weight], vectors, me, seq)
    two = gather_start([p.output_weight, p.probe_weight, p.lookup_weight, p.content_weight, p.merge_weight])
    three, four = gather_start([p.expand_weight]), gather_start([p.shrink_weight])
    marks = jnp.stack([target_segments[0], memory_segments[0]]).astype(BF16)
    marks = jnp.pad(marks, ((0, BLOCK - 2), (0, width - local)))
    target_pack = jnp.concatenate([target, marks], axis=0)[None]
    one = jnp.stack(exchange([packed[d] for d in range(seq)]))
    target_pack = seq_gather(target_pack, bits[:1])
    two = gather_step(two, back, 0)
    one, three, four = tie(one, three, four)
    one = gather_step(one, near, 0)
    one, target_pack, two, memory_row = tie(one, target_pack, two, memory[None])
    one = gather_step(one, near, 1)
    target_pack = seq_gather(target_pack, bits[1:])
    memory_row = seq_gather(memory_row, bits[:1])
    target_row = target_pack[:, :local].reshape(-1, width)
    block_places = jnp.stack([(place_in_row ^ o) * local for o in offsets]).astype(jnp.int32)
    key_places = (block_places[:, None] + jnp.arange(local, dtype=jnp.int32)).reshape(1, -1)
    target_marks = target_pack[:, local, :local].reshape(1, -1).astype(jnp.int32)
    memory_marks = target_pack[:, local + 1, :local].reshape(1, -1).astype(jnp.int32)
    own_marks = target_segments.reshape(local, 1)
    self_masks = (block_places, target_marks.reshape(-1, 1), target_marks, key_places)
    cross_masks = (block_places[:1], own_marks, memory_marks, jnp.zeros_like(key_places))
    one, two, memory_row = tie(one, two, memory_row)
    got = stage_swap(one, near, 2)
    two = gather_step(two, back, 1)
    one, got, three, four = tie(one, got, three, four)

    two = gather_step(two, back, 2)
    three = gather_step(three, back, 0)
    four = gather_step(four, back, 0)
    memory_row = seq_gather(memory_row, bits[1:]).reshape(-1, width)
    pieces = [v.reshape(v.shape[0], -1, BLOCK, width) for v in (one, got)]
    wqkv, blocks = place(pieces, group_owners(near), 1, rows // BLOCK)
    wqkv = wqkv.reshape(-1, width)
    named, expand_bias = unpack_vectors(blocks.reshape(-1, BLOCK, width), width, wide)
    (
        query_bias,
        value_bias,
        output_bias,
        first_gain,
        first_shift,
        probe_bias,
        content_bias,
        merge_bias,
        second_gain,
        second_shift,
        shrink_bias,
        third_gain,
        third_shift,
    ) = (named[i : i + 1] for i in range(VECTORS))
    mine = lambda v: jnp.pad(lax.dynamic_slice(v, (0, place_in_row * span), (1, span)), ((0, 0), (0, space - span)))
    row_bias = jnp.concatenate([mine(query_bias), jnp.zeros((1, space), F32), mine(value_bias)], axis=1)
    scale = jnp.where(jnp.arange(3 * space) < space, 0.125, 1.0)[None]
    qkv = ((dot(target_row, wqkv) + row_bias) * scale).astype(BF16)
    qkv, two, three, four, memory_row = tie(qkv, two, three, four, memory_row)
    two = gather_last(two, back)
    three = gather_step(three, back, 1)
    four = gather_step(four, back, 1)
    mixed_row, log_one = row_forward(qkv, self_masks, heads, local, block)
    mixed_row, two, three, four = tie(mixed_row, two, three, four)
    sent = [mixed_row[i * local : (i + 1) * local] for i in range(seq)]
    mixed_one = join_heads(exchange([sent[offsets.index(d)] for d in range(seq)]), me, span)
    two_pieces = gather_finish(two)
    mixed_one, two_pieces, three, four = tie(mixed_one, two_pieces, three, four)
    three = gather_step(three, back, 2)
    four = gather_step(four, back, 2)
    wo, wp, wl, wc, wm, *_ = unpack(two_pieces, back, 5, rows)
    first_sum = target.astype(F32) + dot(mixed_one, wo) + output_bias
    first_full, normed_one, inverse_one = norm_forward(first_sum, first_gain, first_shift)
    first_out = first_full.astype(BF16)
    query_two = ((dot(first_out, wp) + probe_bias) * 0.125).astype(BF16)
    key_two = dot(memory_row, wl).astype(BF16)
    value_two = (dot(memory_row, wc) + content_bias).astype(BF16)
    query_two, key_two, value_two, three, four = tie(query_two, key_two, value_two, three, four)
    three = gather_last(three, back)
    mixed_two, log_two = attend_forward(query_two, key_two, value_two, cross_masks, block)
    mixed_two, three, four = tie(mixed_two, three, four)
    four = gather_last(four, back)
    three = gather_finish(three)
    second_sum = first_out.astype(F32) + dot(mixed_two, wm) + merge_bias
    second_full, normed_two, inverse_two = norm_forward(second_sum, second_gain, second_shift)
    second_out = second_full.astype(BF16)
    expand_weight, *_ = unpack(three, back, 1, rows)
    second_out, expand_weight, four = tie(second_out, expand_weight, four)
    four = gather_finish(four)
    hidden, slope = expand_gelu(second_out, expand_weight, expand_bias)
    hidden, four = tie(hidden, four)
    shrink_weight, *_ = unpack(four, back, 1, p.shrink_weight.shape[0])
    third_sum = second_out.astype(F32) + dot(hidden, shrink_weight) + shrink_bias
    third_full, normed_three, inverse_three = norm_forward(third_sum, third_gain, third_shift)
    layer_output = third_full.astype(BF16)

    upstream = cotangent[0].astype(F32)
    third_grad, third_gain_grad, third_shift_grad = norm_backward(upstream, normed_three, inverse_three, third_gain)
    shrink_in = third_grad.astype(BF16)
    shrink_bias_grad = token_sum(shrink_in)
    shrink_grad = t_dot(hidden, shrink_in).astype(BF16)
    four = reduce_start([shrink_grad], last)
    four, shrink_in, third_grad = tie(four, shrink_in, third_grad)
    four = reduce_core(four)
    act_grad = (dot_t(shrink_in, shrink_weight) * slope).astype(BF16)
    expand_bias_grad = token_sum(act_grad)
    three = reduce_start([t_dot(second_out, act_grad)], last)
    three, four, act_grad, third_grad = tie(three, four, act_grad, third_grad)
    three = reduce_core(three)
    four = reduce_step(four, last, 3)
    second_grad = third_grad + dot_t(act_grad, expand_weight)
    second_sum_grad, second_gain_grad, second_shift_grad = norm_backward(second_grad, normed_two, inverse_two, second_gain)
    merge_in = second_sum_grad.astype(BF16)
    merge_bias_grad = token_sum(merge_in)
    mixed_two_grad = dot_t(merge_in, wm).astype(BF16)
    mixed_two_grad, three = tie(mixed_two_grad, three)
    three = reduce_step(three, last, 3)
    probe_in, lookup_part, content_part = attend_backward(query_two, key_two, value_two, mixed_two, mixed_two_grad, log_two, cross_masks, block)
    probe_in, lookup_part, content_part, three, four = tie(probe_in, lookup_part, content_part, three, four)
    three = reduce_step(three, last, 2)
    four = reduce_step(four, last, 2)
    first_grad = second_sum_grad + dot_t(probe_in, wp)
    first_sum_grad, first_gain_grad, first_shift_grad = norm_backward(first_grad, normed_one, inverse_one, first_gain)
    output_in = first_sum_grad.astype(BF16)
    mixed_one_grad = dot_t(output_in, wo).astype(BF16)
    split = split_heads(mixed_one_grad, me, seq, space)
    split, three, four, probe_in, lookup_part, content_part, output_in = tie(split, three, four, probe_in, lookup_part, content_part, output_in)
    came = exchange([split[d] for d in range(seq)])
    mixed_row_grad = jnp.concatenate([came[o] for o in offsets], axis=0)
    three = reduce_step(three, last, 1)
    four = reduce_step(four, last, 1)
    output_bias_grad = token_sum(output_in)
    probe_bias_grad = token_sum(probe_in)
    content_bias_grad = token_sum(content_part)
    cross_grads = [
        t_dot(mixed_one, output_in),
        t_dot(first_out, probe_in),
        t_dot(memory_row, lookup_part),
        t_dot(memory_row, content_part),
        t_dot(mixed_two, merge_in),
    ]
    two = reduce_start(cross_grads, back)
    mixed_row_grad, two, three, four, lookup_part, content_part = tie(mixed_row_grad, two, three, four, lookup_part, content_part)
    two = reduce_core(two)
    three = reduce_step(three, last, 0)
    four = reduce_step(four, last, 0)
    memory_part = (dot_t(lookup_part, wl) + dot_t(content_part, wc)).reshape(seq, local, width)
    mixed_row_grad, two, three, memory_part = tie(mixed_row_grad, two, three, memory_part)
    two = reduce_step(two, back, 3)
    memory_part = seq_reduce(memory_part, bits[:0:-1])
    qkv_grad = row_backward(qkv, mixed_row, mixed_row_grad, log_one, self_masks, heads, local, block)
    qkv_grad, two, memory_part = tie(qkv_grad, two, memory_part)
    two = reduce_step(two, back, 2)
    memory_grad = seq_reduce(memory_part, bits[:1])[0]
    row_grad = t_dot(target_row, qkv_grad)
    sums = token_sum(qkv_grad)
    spot = lambda v: lax.dynamic_update_slice(jnp.zeros((1, width), F32), v, (0, place_in_row * span))
    vector_grads = (
        spot(sums[:, :span]),
        spot(sums[:, 2 * space : 2 * space + span]),
        output_bias_grad,
        first_gain_grad,
        first_shift_grad,
        probe_bias_grad,
        content_bias_grad,
        merge_bias_grad,
        second_gain_grad,
        second_shift_grad,
        shrink_bias_grad,
        third_gain_grad,
        third_shift_grad,
    )
    tail = pack_sums(vector_grads, expand_bias_grad, width)
    terms = [row_grad.astype(BF16).reshape(owners(), -1, BLOCK, width), tail.reshape(owners(), -1, BLOCK, width)]
    one = tuple(spread(terms, group_owners(near)))
    one, qkv_grad = tie(one, qkv_grad)
    one = reduce_step(one, near, 2)
    two = reduce_step(two, back, 1)
    target_part = dot_t(qkv_grad, wqkv).reshape(seq, local, width)
    one, two, target_part = tie(one, two, target_part)
    one = reduce_step(one, near, 1)
    target_part = seq_reduce(target_part, bits[:0:-1])
    one, two, target_part = tie(one, two, target_part)
    one = reduce_step(one, near, 0)
    target_grad = first_sum_grad + seq_reduce(target_part, bits[:1])[0]
    slots = one[0].astype(BF16).reshape(seq, -1, width)
    slots, two = tie(slots, two)
    one = exchange([slots[d] for d in range(seq)])
    two = reduce_step(two, back, 0)

    query_grad, key_grad, value_grad, wide_sum = unpack_heads(one, me, 3, rows)
    two, three, four = (reduce_finish(t) for t in (two, three, four))
    sums = [wide_sum[seat(i)[0], seat(i)[1] : seat(i)[1] + rows] for i in range(VECTORS)]
    row, lane = seat(VECTORS)
    result = Params(
        query_weight=query_grad,
        key_weight=key_grad,
        value_weight=value_grad,
        output_weight=two[:rows],
        probe_weight=two[rows : 2 * rows],
        lookup_weight=two[2 * rows : 3 * rows],
        content_weight=two[3 * rows : 4 * rows],
        merge_weight=two[4 * rows :],
        expand_weight=three.reshape(rows, wide),
        shrink_weight=four,
        expand_bias=wide_sum[row, lane : lane + wide // owners()],
        query_bias=sums[0],
        value_bias=sums[1],
        output_bias=sums[2],
        first_gain=sums[3],
        first_shift=sums[4],
        probe_bias=sums[5],
        content_bias=sums[6],
        merge_bias=sums[7],
        second_gain=sums[8],
        second_shift=sums[9],
        shrink_bias=sums[10],
        third_gain=sums[11],
        third_shift=sums[12],
    )
    return (layer_output[None], target_grad[None], memory_grad[None]) + tuple(result)


def solution(mesh):
    tokens = P("dp", "seq", None)
    matrix = P(ALL, None)
    vector = P(ALL)
    params = Params(*[vector] * len(Params._fields))._replace(
        query_weight=matrix,
        key_weight=matrix,
        value_weight=matrix,
        output_weight=matrix,
        probe_weight=matrix,
        lookup_weight=matrix,
        content_weight=matrix,
        merge_weight=matrix,
        expand_weight=matrix,
        shrink_weight=matrix,
    )
    split = mesh.size == FLAT and mesh.shape["seq"] == 4
    return jax.shard_map(
        per_device if split else per_device_by_rows,
        mesh=mesh,
        in_specs=(tokens, tokens, tokens, P("dp", "seq"), P("dp", "seq")) + tuple(params),
        out_specs=(tokens, tokens, tokens) + tuple(params),
        check_vma=False,
    )
```

```python
from typing import Any, NamedTuple

import jax
import jax.numpy as jnp
from jax import lax
from jax.experimental import pallas as pl
from jax.experimental.pallas import tpu as pltpu
from jax.sharding import PartitionSpec as P

HEAD_DIM = 64
PAIR = 2 * HEAD_DIM
NEG_FILL = -1e30
EPSILON = 1e-05
BF16 = jnp.bfloat16
F32 = jnp.float32
ALL = ("dp", "seq")

class Params(NamedTuple):
    query_weight: Any
    query_bias: Any
    key_weight: Any
    value_weight: Any
    value_bias: Any
    output_weight: Any
    output_bias: Any
    first_gain: Any
    first_shift: Any
    probe_weight: Any
    probe_bias: Any
    lookup_weight: Any
    content_weight: Any
    content_bias: Any
    merge_weight: Any
    merge_bias: Any
    second_gain: Any
    second_shift: Any
    expand_weight: Any
    expand_bias: Any
    shrink_weight: Any
    shrink_bias: Any
    third_gain: Any
    third_shift: Any


def vectors_of(p):
    return (
        p.query_bias,
        p.value_bias,
        p.output_bias,
        p.first_gain,
        p.first_shift,
        p.probe_bias,
        p.content_bias,
        p.merge_bias,
        p.second_gain,
        p.second_shift,
        p.shrink_bias,
        p.third_gain,
        p.third_shift,
    )


VECTORS = 13
LANES = 128


def dot(left, right):
    return jnp.dot(left, right, preferred_element_type=F32)


def dot_t(left, right):
    return lax.dot_general(left, right, (((1,), (1,)), ((), ())), preferred_element_type=F32)


def t_dot(left, right):
    return lax.dot_general(left, right, (((0,), (0,)), ((), ())), preferred_element_type=F32)


def token_sum(values):
    return jnp.sum(values.astype(F32), axis=0, keepdims=True)


TILES = 2


def fill_mask(block, first, qseg, kseg_ref, kpos_ref, bias, base, flags, row):
    rows = qseg.shape[0]
    place = first + lax.broadcasted_iota(jnp.int32, (rows, block), 0)
    for j in range(bias.shape[1] // block):
        cols = pl.ds(j * block, block)
        allowed = (kseg_ref[:, cols] == qseg) & (kpos_ref[:, cols] <= place)
        term = jnp.where(allowed, 0.0, NEG_FILL)
        bias[pl.ds(base, rows), cols] = term
        flags[row, j] = (jnp.max(term) > -1.0).astype(jnp.int32)


def one_head(value, head):
    lane = lax.broadcasted_iota(jnp.int32, value.shape, 1)
    return jnp.where((lane < HEAD_DIM) == (head == 0), value, jnp.zeros_like(value))


def stacked(value, halves):
    return jnp.concatenate([one_head(value, head) for head in range(halves)], axis=0)


def tiles_forward(block, tiles, bias, flags, scores, peaks, sums, mixed):
    rows, total = bias.shape
    peaks[...] = jnp.full(peaks.shape, NEG_FILL, F32)
    sums[...] = jnp.zeros(sums.shape, F32)
    mixed[...] = jnp.zeros(mixed.shape, F32)
    for j in range(total // block):

        @pl.when(flags[0, j] > 0)
        def _():
            cols = pl.ds(j * block, block)
            for query, key, _, at in tiles:
                part = dot_t(query, key(cols))
                for half in range(query.shape[0] // rows):
                    own = pl.ds(at + half * rows, rows)
                    term = part[half * rows : (half + 1) * rows] + bias[:, cols]
                    scores[own, cols] = term
                    high = peaks[own]
                    for c in range(block // LANES):
                        high = jnp.maximum(high, term[:, c * LANES : (c + 1) * LANES])
                    peaks[own] = high

    peak = jnp.max(peaks[...], axis=-1, keepdims=True)
    peaks[...] = jnp.broadcast_to(peak, peaks.shape)
    for j in range(total // block):

        @pl.when(flags[0, j] > 0)
        def _():
            cols = pl.ds(j * block, block)
            for query, _, value, at in tiles:
                own = pl.ds(at, query.shape[0])
                part = jnp.exp(scores[own, cols] - peaks[own, 0:1])
                add = sums[own]
                for c in range(block // LANES):
                    add = add + part[:, c * LANES : (c + 1) * LANES]
                sums[own] = add
                mixed[own] += dot(part.astype(BF16), value(cols))

    whole = jnp.sum(sums[...], axis=-1, keepdims=True)
    return mixed[...] * (1.0 / whole), peak + jnp.log(whole)


def tiles_backward(block, tiles, bias, flags, query_sum, key_sum, value_sum):
    rows, total = bias.shape
    query_sum[...] = jnp.zeros(query_sum.shape, F32)
    for j in range(total // block):

        @pl.when(flags[0, j] > 0)
        def _():
            cols = pl.ds(j * block, block)
            for query, grad, log, inner, key_of, value, at, lanes in tiles:
                key = key_of(cols)
                scores = dot_t(query, key)
                slope = dot_t(grad, value(cols))
                terms = [scores[i : i + rows] + bias[:, cols] for i in range(0, query.shape[0], rows)]
                part = jnp.exp((jnp.concatenate(terms, axis=0) if len(terms) > 1 else terms[0]) - log)
                score_grad = (part * (slope - inner)).astype(BF16)
                query_sum[pl.ds(at, query.shape[0])] += dot(score_grad, key)
                key_sum[cols, lanes] += t_dot(score_grad, query)
                value_sum[cols, lanes] += t_dot(part.astype(BF16), grad)


def lower_lanes(shape):
    return lax.broadcasted_iota(jnp.int32, shape, 1) < HEAD_DIM


def eighth(value):
    return (value.astype(BF16) * 0.125).astype(BF16)


def attend_kernel(block, q0_ref, q_ref, k_ref, v_ref, qseg_ref, kseg_ref, kpos_ref, o_ref, log_ref, bias, flags, *scratch):
    @pl.when(pl.program_id(0) == 0)
    def _():
        fill_mask(block, q0_ref[0], qseg_ref[...], kseg_ref, kpos_ref, bias, 0, flags, 0)

    rows = o_ref.shape[0]
    tiles = []
    for t in range(TILES):
        lanes = pl.ds(t * PAIR, PAIR)
        key = lambda cols, lanes=lanes: k_ref[cols, lanes]
        value = lambda cols, lanes=lanes: v_ref[cols, lanes]
        tiles.append((stacked(q_ref[:, lanes], 2), key, value, 2 * t * rows))
    out, log = tiles_forward(block, tiles, bias, flags, *scratch)
    low = lower_lanes((rows, PAIR))
    for t in range(TILES):
        lanes = pl.ds(t * PAIR, PAIR)
        upper, lower = slice(2 * t * rows, (2 * t + 1) * rows), slice((2 * t + 1) * rows, (2 * t + 2) * rows)
        o_ref[:, lanes] = jnp.where(low, out[upper], out[lower]).astype(BF16)
        log_ref[:, lanes] = jnp.where(low, log[upper], log[lower])


def attend_back_kernel(block, q0_ref, q_ref, k_ref, v_ref, o_ref, g_ref, log_ref, qseg_ref, kseg_ref, kpos_ref, dq_ref, dk_ref, dv_ref, bias, flags, query_sum, key_sum, value_sum):
    @pl.when(pl.program_id(0) == 0)
    def _():
        fill_mask(block, q0_ref[0], qseg_ref[...], kseg_ref, kpos_ref, bias, 0, flags, 0)

    key_sum[...] = jnp.zeros(key_sum.shape, F32)
    value_sum[...] = jnp.zeros(value_sum.shape, F32)
    rows = q_ref.shape[0]
    tiles = []
    for t in range(TILES):
        lanes = pl.ds(t * PAIR, PAIR)
        key = lambda cols, lanes=lanes: k_ref[cols, lanes]
        value = lambda cols, lanes=lanes: v_ref[cols, lanes]
        grad = stacked(g_ref[:, lanes], 2)
        mixed = o_ref[:, lanes].astype(F32)
        inner = jnp.sum(grad.astype(F32) * jnp.concatenate([mixed, mixed], axis=0), axis=-1, keepdims=True)
        log = jnp.concatenate([log_ref[:, t * PAIR + i * HEAD_DIM : t * PAIR + i * HEAD_DIM + 1] for i in range(2)], axis=0)
        tiles.append((stacked(q_ref[:, lanes], 2), grad, log, inner, key, value, 2 * t * rows, lanes))
    tiles_backward(block, tiles, bias, flags, query_sum, key_sum, value_sum)
    for t in range(TILES):
        at = 2 * t * rows
        dq_ref[:, pl.ds(t * PAIR, PAIR)] = eighth(jnp.where(lower_lanes((rows, PAIR)), query_sum[at : at + rows], query_sum[at + rows : at + 2 * rows]))
    dk_ref[...] = key_sum[...].astype(BF16)
    dv_ref[...] = value_sum[...].astype(BF16)


def attend_specs(rows, total):
    whole = lambda shape: pl.BlockSpec(shape, lambda i: (0, 0))
    strip = lambda count: pl.BlockSpec((count, TILES * PAIR), lambda i: (0, i))
    return (
        pl.BlockSpec(memory_space=pltpu.SMEM),
        strip(rows),
        strip(total),
        [whole((rows, 1)), whole((1, total)), whole((1, total))],
    )


def forward_scratch(rows, total, heads):
    return [pltpu.VMEM((heads * rows, total), F32)] + [pltpu.VMEM((heads * rows, LANES), F32)] * 3


def attend_forward(query, key, value, masks, block):
    rows, width = query.shape
    total = key.shape[0]
    scalar, narrow, tall, marks = attend_specs(rows, total)
    q0, qseg, kseg, kpos = masks
    return pl.pallas_call(
        lambda *refs: attend_kernel(block, *refs),
        grid=(width // (TILES * PAIR),),
        in_specs=[scalar, narrow, tall, tall] + marks,
        out_specs=[narrow, narrow],
        out_shape=[jax.ShapeDtypeStruct((rows, width), BF16), jax.ShapeDtypeStruct((rows, width), F32)],
        scratch_shapes=[pltpu.VMEM((rows, total), F32), pltpu.SMEM((1, total // block), jnp.int32)] + forward_scratch(rows, total, 2 * TILES),
        cost_estimate=pl.CostEstimate(flops=8 * rows * total * width, bytes_accessed=8 * total * width, transcendentals=rows * total * 12),
        compiler_params=pltpu.CompilerParams(dimension_semantics=("arbitrary",)),
        name="attend_forward",
    )(q0, query, key, value, qseg, kseg, kpos)


def attend_backward(query, key, value, mixed, grad, log, masks, block):
    rows, width = query.shape
    total = key.shape[0]
    scalar, narrow, tall, marks = attend_specs(rows, total)
    q0, qseg, kseg, kpos = masks
    return pl.pallas_call(
        lambda *refs: attend_back_kernel(block, *refs),
        grid=(width // (TILES * PAIR),),
        in_specs=[scalar, narrow, tall, tall, narrow, narrow, narrow] + marks,
        out_specs=[narrow, tall, tall],
        out_shape=[
            jax.ShapeDtypeStruct((rows, width), BF16),
            jax.ShapeDtypeStruct((total, width), BF16),
            jax.ShapeDtypeStruct((total, width), BF16),
        ],
        scratch_shapes=[
            pltpu.VMEM((rows, total), F32),
            pltpu.SMEM((1, total // block), jnp.int32),
            pltpu.VMEM((2 * TILES * rows, PAIR), F32),
            pltpu.VMEM((total, TILES * PAIR), F32),
            pltpu.VMEM((total, TILES * PAIR), F32),
        ],
        cost_estimate=pl.CostEstimate(flops=20 * rows * total * width, bytes_accessed=16 * total * width, transcendentals=rows * total * 12),
        compiler_params=pltpu.CompilerParams(dimension_semantics=("arbitrary",)),
        name="attend_backward",
    )(q0, query, key, value, mixed, grad, log, qseg, kseg, kpos)


def seats_of(heads, space):
    return [(pl.ds(t, PAIR), pl.ds(space + t, PAIR), pl.ds(2 * space + t, PAIR), min(2, heads - 2 * (t // PAIR))) for t in range(0, space, PAIR)]


def row_kernel(block, heads, q0_ref, qkv_ref, qseg_ref, kseg_ref, kpos_ref, o_ref, log_ref, bias, flags, *scratch):
    rows, space = o_ref.shape
    step = pl.program_id(0)
    own = pl.ds(pl.multiple_of(step * rows, rows), rows)
    fill_mask(block, q0_ref[step], qseg_ref[...], kseg_ref, kpos_ref, bias, 0, flags, 0)
    tiles = []
    for tile, (query_lanes, key_lanes, value_lanes, halves) in enumerate(seats_of(heads, space)):
        key = lambda cols, lanes=key_lanes: qkv_ref[cols, lanes]
        value = lambda cols, lanes=value_lanes: qkv_ref[cols, lanes]
        tiles.append((stacked(qkv_ref[own, query_lanes], halves), key, value, 2 * tile * rows))
    out, log = tiles_forward(block, tiles, bias, flags, *scratch)
    low = lower_lanes((rows, PAIR))
    blank = jnp.zeros((rows, PAIR), F32)
    for query, _, _, at in tiles:
        lanes = pl.ds(at // (2 * rows) * PAIR, PAIR)
        pair = query.shape[0] > rows
        o_ref[:, lanes] = jnp.where(low, out[at : at + rows], out[at + rows : at + 2 * rows] if pair else blank).astype(BF16)
        log_ref[:, lanes] = jnp.where(low, log[at : at + rows], log[at + rows : at + 2 * rows] if pair else blank)


def row_back_kernel(block, heads, q0_ref, qkv_ref, o_ref, g_ref, log_ref, qseg_ref, kseg_ref, kpos_ref, grads_ref, bias, flags, query_sum, key_sum, value_sum):
    rows, space = o_ref.shape
    step = pl.program_id(0)
    own = pl.ds(pl.multiple_of(step * rows, rows), rows)
    fill_mask(block, q0_ref[step], qseg_ref[...], kseg_ref, kpos_ref, bias, 0, flags, 0)

    @pl.when(step == 0)
    def _():
        key_sum[...] = jnp.zeros(key_sum.shape, F32)
        value_sum[...] = jnp.zeros(value_sum.shape, F32)

    tiles = []
    for tile, (query_lanes, key_lanes, value_lanes, halves) in enumerate(seats_of(heads, space)):
        key = lambda cols, lanes=key_lanes: qkv_ref[cols, lanes]
        value = lambda cols, lanes=value_lanes: qkv_ref[cols, lanes]
        grad = stacked(g_ref[:, query_lanes], halves)
        mixed = o_ref[:, query_lanes].astype(F32)
        inner = jnp.sum(grad.astype(F32) * jnp.concatenate([mixed] * halves, axis=0), axis=-1, keepdims=True)
        lane = tile * PAIR
        log = jnp.concatenate([log_ref[:, lane + i * HEAD_DIM : lane + i * HEAD_DIM + 1] for i in range(halves)], axis=0)
        tiles.append((stacked(qkv_ref[own, query_lanes], halves), grad, log, inner, key, value, 2 * tile * rows, query_lanes))
    tiles_backward(block, tiles, bias, flags, query_sum, key_sum, value_sum)
    low = lower_lanes((rows, PAIR))
    for query, _, _, _, _, _, at, lanes in tiles:
        upper = query_sum[at + rows : at + 2 * rows] if query.shape[0] > rows else jnp.zeros((rows, PAIR), F32)
        grads_ref[own, lanes] = eighth(jnp.where(low, query_sum[at : at + rows], upper))

    @pl.when(step == pl.num_programs(0) - 1)
    def _():
        grads_ref[:, space : 2 * space] = key_sum[...].astype(BF16)
        grads_ref[:, 2 * space :] = value_sum[...].astype(BF16)


def row_specs(rows, total, space):
    whole = lambda shape: pl.BlockSpec(shape, lambda i: (0, 0))
    strip = lambda width: pl.BlockSpec((rows, width), lambda i: (i, 0))
    return (
        pl.BlockSpec(memory_space=pltpu.SMEM),
        whole((total, 3 * space)),
        strip(space),
        [strip(1), whole((1, total)), whole((1, total))],
    )


def row_forward(qkv, masks, heads, rows, block):
    total, space = qkv.shape[0], qkv.shape[1] // 3
    scalar, full, narrow, marks = row_specs(rows, total, space)
    q0, qseg, kseg, kpos = masks
    return pl.pallas_call(
        lambda *refs: row_kernel(block, heads, *refs),
        grid=(total // rows,),
        in_specs=[scalar, full] + marks,
        out_specs=[narrow, narrow],
        out_shape=[jax.ShapeDtypeStruct((total, space), BF16), jax.ShapeDtypeStruct((total, space), F32)],
        scratch_shapes=[pltpu.VMEM((rows, total), F32), pltpu.SMEM((1, total // block), jnp.int32)] + forward_scratch(rows, total, heads),
        cost_estimate=pl.CostEstimate(flops=4 * total * total * space, bytes_accessed=10 * total * space, transcendentals=total * total * heads),
        compiler_params=pltpu.CompilerParams(dimension_semantics=("arbitrary",)),
        name="row_forward",
    )(q0, qkv, qseg, kseg, kpos)


def row_backward(qkv, mixed, grad, log, masks, heads, rows, block):
    total, space = mixed.shape
    scalar, full, narrow, marks = row_specs(rows, total, space)
    q0, qseg, kseg, kpos = masks
    return pl.pallas_call(
        lambda *refs: row_back_kernel(block, heads, *refs),
        grid=(total // rows,),
        in_specs=[scalar, full, narrow, narrow, narrow] + marks,
        out_specs=full,
        out_shape=jax.ShapeDtypeStruct((total, 3 * space), BF16),
        scratch_shapes=[
            pltpu.VMEM((rows, total), F32),
            pltpu.SMEM((1, total // block), jnp.int32),
            pltpu.VMEM((heads * rows, PAIR), F32),
            pltpu.VMEM((total, space), F32),
            pltpu.VMEM((total, space), F32),
        ],
        cost_estimate=pl.CostEstimate(flops=10 * total * total * space, bytes_accessed=20 * total * space, transcendentals=total * total * heads),
        compiler_params=pltpu.CompilerParams(dimension_semantics=("arbitrary",)),
        name="row_backward",
    )(q0, qkv, mixed, grad, log, qseg, kseg, kpos)


def split_kernel(span, me_ref, value_ref, out_ref):
    rows, space = out_ref.shape[1:]
    for group in range(out_ref.shape[0]):
        part = value_ref[:, group * span : (group + 1) * span].astype(F32)
        out_ref[me_ref[0] ^ group] = jnp.concatenate([part, jnp.zeros((rows, space - span), F32)], axis=1).astype(BF16)


def split_heads(value, me, groups, space):
    rows, width = value.shape
    return pl.pallas_call(
        lambda *refs: split_kernel(width // groups, *refs),
        out_shape=jax.ShapeDtypeStruct((groups, rows, space), BF16),
        in_specs=[pl.BlockSpec(memory_space=pltpu.SMEM), pl.BlockSpec(memory_space=pltpu.VMEM)],
        out_specs=pl.BlockSpec(memory_space=pltpu.VMEM),
        name="split_heads",
    )(me, value)


def join_kernel(span, me_ref, *refs):
    pieces, (out_ref, held) = refs[:-2], refs[-2:]
    for d, piece in enumerate(pieces):
        held[d] = piece[...]
    parts = [held[me_ref[0] ^ group].astype(F32)[:, :span] for group in range(len(pieces))]
    out_ref[...] = jnp.concatenate(parts, axis=1).astype(BF16)


def join_heads(pieces, me, span):
    rows, space = pieces[0].shape
    groups = len(pieces)
    vmem = pl.BlockSpec(memory_space=pltpu.VMEM)
    return pl.pallas_call(
        lambda *refs: join_kernel(span, *refs),
        out_shape=jax.ShapeDtypeStruct((rows, groups * span), BF16),
        in_specs=[pl.BlockSpec(memory_space=pltpu.SMEM)] + [vmem] * groups,
        out_specs=vmem,
        scratch_shapes=[pltpu.VMEM((groups, rows, space), BF16)],
        name="join_heads",
    )(me, *pieces)


def pack_heads_kernel(weights, span, me_ref, *refs):
    out_ref = refs[-1]
    vectors = refs[weights][...]
    rows = refs[0].shape[0]
    space = out_ref.shape[2] // weights
    for group in range(out_ref.shape[0]):
        parts = []
        for ref in refs[:weights]:
            parts += [ref[:, group * span : (group + 1) * span].astype(F32), jnp.zeros((rows, space - span), F32)]
        out_ref[me_ref[0] ^ group, :rows] = jnp.concatenate(parts, axis=1).astype(BF16)
        out_ref[me_ref[0] ^ group, rows:] = vectors


def pack_heads(weights, vectors, me, groups):
    rows, width = weights[0].shape
    vmem = pl.BlockSpec(memory_space=pltpu.VMEM)
    return pl.pallas_call(
        lambda *refs: pack_heads_kernel(len(weights), width // groups, *refs),
        out_shape=jax.ShapeDtypeStruct((groups, rows + vectors.shape[0], width), BF16),
        in_specs=[pl.BlockSpec(memory_space=pltpu.SMEM)] + [vmem] * (len(weights) + 1),
        out_specs=vmem,
        name="pack_heads",
    )(me, *weights, vectors)


def unpack_heads_kernel(weights, span, me_ref, *refs):
    groups = len(refs) - weights - 2
    pieces, outs, tail_ref, held = refs[:groups], refs[groups:-2], refs[-2], refs[-1]
    rows = outs[0].shape[0]
    space = pieces[0].shape[1] // weights
    for d, piece in enumerate(pieces):
        held[d] = piece[...].astype(F32)
    for i, out in enumerate(outs):
        out[...] = jnp.concatenate([held[me_ref[0] ^ group, :rows, i * space : i * space + span] for group in range(groups)], axis=1)
    tail_ref[...] = sum(held[d, rows:] for d in range(groups))


def unpack_heads(pieces, me, weights, rows):
    groups = len(pieces)
    width = pieces[0].shape[1]
    vmem = pl.BlockSpec(memory_space=pltpu.VMEM)
    return pl.pallas_call(
        lambda *refs: unpack_heads_kernel(weights, width // groups, *refs),
        out_shape=[jax.ShapeDtypeStruct((rows, width), F32)] * weights + [jax.ShapeDtypeStruct((pieces[0].shape[0] - rows, width), F32)],
        in_specs=[pl.BlockSpec(memory_space=pltpu.SMEM)] + [vmem] * groups,
        out_specs=[vmem] * (weights + 1),
        scratch_shapes=[pltpu.VMEM((groups,) + pieces[0].shape, F32)],
        name="unpack_heads",
    )(me, *pieces)


def norm_forward(hidden, gain, shift):
    centred = hidden - jnp.mean(hidden, axis=-1, keepdims=True)
    inverse = lax.rsqrt(jnp.mean(centred * centred, axis=-1, keepdims=True) + EPSILON)
    normed = centred * inverse
    return normed * gain + shift, normed, inverse


def norm_backward(upstream, normed, inverse, gain):
    scaled = upstream * gain
    inner = jnp.mean(scaled, axis=-1, keepdims=True)
    along = jnp.mean(scaled * normed, axis=-1, keepdims=True)
    return inverse * (scaled - inner - normed * along), token_sum(upstream * normed), token_sum(upstream)


def exact_gelu(values):
    return jax.nn.gelu(values, approximate=False)


def expand_kernel(value_ref, weight_ref, bias_ref, hidden_ref, slope_ref):
    act = dot(value_ref[...], weight_ref[...]) + bias_ref[...]
    share = 0.5 + 0.5 * lax.erf(act * ROOT_HALF)
    hidden_ref[...] = (act * share).astype(BF16)
    slope_ref[...] = share + act * (jnp.exp(-0.5 * act * act) * DENSITY)


ROOT_HALF = 0.7071067811865476
DENSITY = 0.3989422804014327


def expand_gelu(value, weight, bias):
    rows, width = value.shape
    wide = weight.shape[1]
    step = 4 * LANES
    strip = lambda count: pl.BlockSpec((count, step), lambda i: (0, i))
    return pl.pallas_call(
        expand_kernel,
        grid=(wide // step,),
        in_specs=[pl.BlockSpec((rows, width), lambda i: (0, 0)), strip(width), strip(1)],
        out_specs=[strip(rows), strip(rows)],
        out_shape=[jax.ShapeDtypeStruct((rows, wide), BF16), jax.ShapeDtypeStruct((rows, wide), F32)],
        cost_estimate=pl.CostEstimate(flops=2 * rows * width * wide, bytes_accessed=2 * width * wide + 6 * rows * wide, transcendentals=2 * rows * wide),
        compiler_params=pltpu.CompilerParams(dimension_semantics=("arbitrary",)),
        name="expand_gelu",
    )(value, weight, bias)


def seq_offsets(count):
    offsets = [0]
    bit = count // 2
    while bit:
        offsets = offsets + [o ^ bit for o in offsets]
        bit //= 2
    return offsets


def swap(value, axis, bit):
    count = lax.axis_size(axis)
    return lax.ppermute(value, axis, [(i, i ^ bit) for i in range(count)])


def seq_bits():
    bit = lax.axis_size("seq") // 2
    bits = []
    while bit:
        bits.append(bit)
        bit //= 2
    return bits


def seq_gather(rows, bits):
    for bit in bits:
        rows = jnp.concatenate([rows, swap(rows, "seq", bit)], axis=0)
    return rows


def seq_reduce(total, bits):
    for bit in bits:
        half = total.shape[0] // 2
        got = swap(total[half:].astype(BF16), "seq", bit)
        total = total[:half].astype(F32) + got.astype(F32)
    return total


def tie(*values):
    return lax.optimization_barrier(values)


NEAR_LAST = ((16, 8, 2, 4), (8, 16, 4, 2))
NEAR_FIRST = ((2, 4, 8, 16), (4, 2, 16, 8))
DP_LAST = ((16, 8, 4), (4, 16, 8))
NEAR_BACK = ((16, 2, 8, 4), (16, 2, 4, 8))
BLOCK = 8


FLAT = 2 ** (len(NEAR_LAST[0]) + 1)


def owners():
    return lax.axis_size("dp") * lax.axis_size("seq")


def staged():
    return owners() == 2 ** (len(NEAR_LAST[0]) + 1)


def slot_owners(plan):
    def masks(core):
        found = [0]
        for bit in plan[core]:
            found = found + [o ^ bit for o in found]
        return found

    me = lax.axis_index(ALL)
    even = jnp.array(masks(0) + [1 ^ m for m in masks(1)], jnp.int32)
    odd = jnp.array(masks(1) + [1 ^ m for m in masks(0)], jnp.int32)
    return me ^ jnp.where((me & 1) == 0, even, odd)


def group_owners(plan):
    def masks(core):
        found = list(range(lax.axis_size("seq")))
        for bit in plan[core]:
            found = found + [o ^ bit for o in found]
        return found

    me = lax.axis_index(ALL)
    return me ^ jnp.where((me & 1) == 0, jnp.array(masks(0), jnp.int32), jnp.array(masks(1), jnp.int32))


def exchange(pieces):
    return [pieces[0]] + [swap(pieces[d], "seq", d) for d in range(1, len(pieces))]


def stage_swap(value, plan, stage):
    return lax.ppermute(value, ALL, [(d, d ^ plan[d & 1][stage]) for d in range(owners())])


def core_swap(value):
    return lax.ppermute(value, ALL, [(d, d ^ 1) for d in range(owners())])


def place_kernel(groups, rows, counts, order, *refs):
    pieces, refs = refs[: len(counts)], refs[len(counts) :]
    outs, (held, came, left) = refs[:-3], refs[-3:]
    blocks = held.shape[1]
    sizes = [rows] * groups + [blocks - groups * rows] * (len(outs) - groups)
    base = 0
    for piece, count in zip(pieces, counts):

        def fetch(slot, carry):
            pltpu.make_async_copy(piece.at[slot], held.at[base + slot], came.at[base + slot]).start()
            return carry

        lax.fori_loop(0, count, fetch, 0)
        base += count

    def put(slot, carry):
        pltpu.make_async_copy(pieces[0].at[0], held.at[slot], came.at[slot]).wait()
        at = 0
        for out, size in zip(outs, sizes):
            pltpu.make_async_copy(held.at[slot, pl.ds(at, size)], out.at[order[slot]], left).start()
            at += size
        return carry

    lax.fori_loop(0, base, put, 0)

    def finish(slot, carry):
        at = 0
        for out, size in zip(outs, sizes):
            pltpu.make_async_copy(held.at[slot, pl.ds(at, size)], out.at[slot], left).wait()
            at += size
        return carry

    lax.fori_loop(0, base, finish, 0)


def place(pieces, order, groups, rows):
    counts = tuple(p.shape[0] for p in pieces)
    _, blocks, _, width = pieces[0].shape
    devices = sum(counts)
    sizes = [rows] * groups + [blocks - groups * rows] * (blocks > groups * rows)
    anywhere = pl.BlockSpec(memory_space=pl.ANY)
    return pl.pallas_call(
        lambda *refs: place_kernel(groups, rows, counts, *refs),
        out_shape=[jax.ShapeDtypeStruct((devices, size, BLOCK, width), BF16) for size in sizes],
        in_specs=[pl.BlockSpec(memory_space=pltpu.SMEM)] + [anywhere] * len(pieces),
        out_specs=[anywhere] * len(sizes),
        scratch_shapes=[
            pltpu.VMEM((devices, blocks, BLOCK, width), BF16),
            pltpu.SemaphoreType.DMA((devices,)),
            pltpu.SemaphoreType.DMA,
        ],
        cost_estimate=pl.CostEstimate(flops=0, bytes_accessed=4 * devices * blocks * BLOCK * width, transcendentals=0),
        name="place",
    )(order, *pieces)


def spread_kernel(sizes, order, *refs):
    terms, refs = refs[: len(sizes)], refs[len(sizes) :]
    outs, (held, came, left) = refs[:2], refs[2:]
    half = outs[0].shape[0]
    spans = [pl.ds(sum(sizes[:i]), size) for i, size in enumerate(sizes)]
    for i, term in enumerate(terms):
        pltpu.make_async_copy(term, held.at[:, spans[i]], came.at[i]).start()
    for i, term in enumerate(terms):
        pltpu.make_async_copy(term, held.at[:, spans[i]], came.at[i]).wait()
        for index, out in enumerate(outs):

            def put(slot, carry):
                pltpu.make_async_copy(held.at[order[index * half + slot], spans[i]], out.at[slot, spans[i]], left).start()
                return carry

            lax.fori_loop(0, half, put, 0)

    def finish(slot, carry):
        for out in outs:
            for span in spans:
                pltpu.make_async_copy(held.at[slot, span], out.at[slot, span], left).wait()
        return carry

    lax.fori_loop(0, half, finish, 0)


def spread(terms, order):
    devices, _, _, width = terms[0].shape
    sizes = tuple(t.shape[1] for t in terms)
    blocks = sum(sizes)
    shape = jax.ShapeDtypeStruct((devices // 2, blocks, BLOCK, width), BF16)
    anywhere = pl.BlockSpec(memory_space=pl.ANY)
    return pl.pallas_call(
        lambda *refs: spread_kernel(sizes, *refs),
        out_shape=[shape, shape],
        in_specs=[pl.BlockSpec(memory_space=pltpu.SMEM)] + [anywhere] * len(terms),
        out_specs=[anywhere] * 2,
        scratch_shapes=[
            pltpu.VMEM((devices, blocks, BLOCK, width), BF16),
            pltpu.SemaphoreType.DMA((len(sizes),)),
            pltpu.SemaphoreType.DMA,
        ],
        cost_estimate=pl.CostEstimate(flops=0, bytes_accessed=4 * devices * blocks * BLOCK * width, transcendentals=0),
        name="spread",
    )(order, *terms)


def seat(index):
    return index % BLOCK, LANES * (index // BLOCK)


def pack_vectors_kernel(*refs):
    out, held = refs[-2:]
    held[...] = jnp.zeros(held.shape, F32)
    for i, ref in enumerate(refs[:-2]):
        row, lane = seat(i)
        held[row : row + 1, lane : lane + ref.shape[1]] = ref[...].astype(F32)
    out[...] = held[...].astype(BF16)


def pack_vectors(vectors, width):
    return pl.pallas_call(
        pack_vectors_kernel,
        out_shape=jax.ShapeDtypeStruct((BLOCK, width), BF16),
        in_specs=[pl.BlockSpec(memory_space=pltpu.VMEM)] * len(vectors),
        out_specs=pl.BlockSpec(memory_space=pltpu.VMEM),
        scratch_shapes=[pltpu.VMEM((BLOCK, width), F32)],
        name="pack_vectors",
    )(*[v.reshape(1, -1) for v in vectors])


def unpack_vectors_kernel(blocks, out, wide):
    rows = out.shape[1] // blocks.shape[0]
    span = wide.shape[1] // blocks.shape[0]
    row, lane = seat(VECTORS)
    for d in range(blocks.shape[0]):
        for half in range(2):
            part = blocks[d, :, LANES * half : LANES * (half + 1)].astype(F32)
            out[half * BLOCK : (half + 1) * BLOCK, d * rows : (d + 1) * rows] = part[:, :rows]
            if half == lane // LANES:
                wide[:, d * span : (d + 1) * span] = part[row : row + 1, :span]


def unpack_vectors(blocks, width, wide):
    return pl.pallas_call(
        unpack_vectors_kernel,
        grid=(1,),
        in_specs=[pl.BlockSpec((blocks.shape[0], BLOCK, 2 * LANES), lambda i: (0, 0, 0))],
        out_specs=[pl.BlockSpec((2 * BLOCK, width), lambda i: (0, 0)), pl.BlockSpec((1, wide), lambda i: (0, 0))],
        out_shape=[jax.ShapeDtypeStruct((2 * BLOCK, width), F32), jax.ShapeDtypeStruct((1, wide), F32)],
        name="unpack_vectors",
    )(blocks)


def pack_sums_kernel(*refs):
    out = refs[-1]
    vectors, wide = refs[:-2], refs[-2]
    devices = out.shape[0]
    rows = vectors[0].shape[0] // devices
    span = wide.shape[1] // devices
    table = jnp.concatenate([v[...].reshape(1, -1) for v in vectors] + [jnp.zeros((2 * BLOCK - len(vectors), vectors[0].shape[0]), F32)], axis=0)
    row, lane = seat(VECTORS)
    blank = jnp.zeros((BLOCK, LANES - rows), F32)
    empty = jnp.zeros((BLOCK, out.shape[2] - 2 * LANES), F32)
    line = lax.broadcasted_iota(jnp.int32, (BLOCK, LANES), 0)
    for d in range(devices):
        parts = [table[half * BLOCK : (half + 1) * BLOCK, d * rows : (d + 1) * rows] for half in range(2)]
        parts = [jnp.concatenate([part, blank], axis=1) for part in parts]
        strip = jnp.concatenate([wide[:, d * span : (d + 1) * span], jnp.zeros((1, LANES - span), F32)], axis=1)
        parts[lane // LANES] = jnp.where(line == row, strip, parts[lane // LANES])
        out[d] = jnp.concatenate(parts + [empty], axis=1).astype(BF16)


def pack_sums(vectors, wide, width):
    return pl.pallas_call(
        pack_sums_kernel,
        out_shape=jax.ShapeDtypeStruct((owners(), BLOCK, width), BF16),
        in_specs=[pl.BlockSpec(memory_space=pltpu.VMEM)] * (len(vectors) + 1),
        out_specs=pl.BlockSpec(memory_space=pltpu.VMEM),
        name="pack_sums",
    )(*[v.reshape(-1) for v in vectors], wide)


def gather_start(shards):
    parts = jnp.concatenate(list(shards), axis=0) if len(shards) > 1 else shards[0]
    return parts.reshape(1, -1, BLOCK, parts.shape[1]) if staged() else parts


def gather_step(value, plan, stage):
    return jnp.concatenate([value, stage_swap(value, plan, stage)], axis=0) if staged() else value


def gather_last(value, plan):
    return (value, stage_swap(value, plan, len(plan[0]) - 1), core_swap(value)) if staged() else (value,)


def gather_finish(halves):
    return halves + (core_swap(halves[1]),) if staged() else (lax.all_gather(halves[0], ALL, axis=0, tiled=False),)


def unpack(pieces, plan, count, rows):
    width = pieces[0].shape[-1]
    if not staged():
        whole = pieces[0]
        weights = [whole[:, i * rows : (i + 1) * rows].reshape(-1, width) for i in range(count)]
        return weights + [whole[:, count * rows :]]
    found = place(pieces, slot_owners(plan), count, rows // BLOCK)
    return [w.reshape(-1, width) for w in found[:count]] + [t.reshape(-1, BLOCK, width) for t in found[count:]]


def reduce_start(terms, plan, tail=None):
    devices = owners()
    width = terms[0].shape[1]
    parts = [t.astype(BF16).reshape(devices, -1, width) for t in terms]
    if tail is not None:
        parts.append(tail)
    if not staged():
        return (jnp.concatenate(parts, axis=1),) * 2
    return tuple(spread([p.reshape(devices, -1, BLOCK, width) for p in parts], slot_owners(plan)))


def add_halves(mine, got):
    half = mine.shape[0] // 2
    add = lambda a, b: (a.astype(F32) + b.astype(F32)).astype(BF16)
    return add(mine[:half], got[:half]), add(mine[half:], got[half:])


def reduce_core(halves):
    own, other = halves
    return add_halves(own, core_swap(other)) if staged() else (own, own)


def reduce_step(pair, plan, stage):
    if not staged():
        return pair
    got = stage_swap(pair[1], plan, stage)
    if stage:
        return add_halves(pair[0], got)
    return (pair[0].astype(F32) + got.astype(F32),) * 2


def reduce_finish(pair):
    if staged():
        return pair[0].reshape(-1, pair[0].shape[-1])
    return lax.psum_scatter(pair[0], ALL, scatter_dimension=0, tiled=False).astype(F32)


def per_device_by_rows(target, memory, cotangent, target_segments, memory_segments, *shards):
    p = Params(*shards)
    target = target[0]
    memory = memory[0]
    local, width = target.shape
    seq = lax.axis_size("seq")
    place_in_row = lax.axis_index("seq")
    offsets = seq_offsets(seq)
    bits = seq_bits()
    block = local
    rows = p.query_weight.shape[0]
    wide = p.expand_weight.shape[1]
    last = NEAR_LAST

    expand_weight = lax.all_gather(p.expand_weight, ALL, axis=0, tiled=True)
    shrink_weight = lax.all_gather(p.shrink_weight, ALL, axis=0, tiled=True)
    vectors = pack_vectors(vectors_of(p) + (p.expand_bias,), width)
    one = gather_start([p.query_weight, p.key_weight, p.value_weight, p.output_weight, vectors])
    two = gather_start([p.probe_weight, p.lookup_weight, p.content_weight, p.merge_weight])
    marks = jnp.stack([target_segments[0], memory_segments[0]]).astype(BF16)
    marks = jnp.pad(marks, ((0, BLOCK - 2), (0, width - local)))
    target_pack = jnp.concatenate([target, marks], axis=0)[None]
    memory_row = memory[None]
    one = gather_step(one, last, 0)
    target_pack = seq_gather(target_pack, bits[:1])
    one, target_pack, two = tie(one, target_pack, two)
    one = gather_step(one, last, 1)
    target_pack = seq_gather(target_pack, bits[1:])
    one, target_pack, two = tie(one, target_pack, two)
    one = gather_step(one, last, 2)
    two = gather_step(two, last, 0)
    target_row = target_pack[:, :local].reshape(-1, width)
    key_places = jnp.concatenate([(place_in_row ^ o) * local + jnp.arange(local, dtype=jnp.int32) for o in offsets])[None]
    target_marks = target_pack[:, local, :local].reshape(1, -1).astype(jnp.int32)
    memory_marks = target_pack[:, local + 1, :local].reshape(1, -1).astype(jnp.int32)
    own_marks = target_segments.reshape(local, 1)
    start = (place_in_row * local).astype(jnp.int32).reshape(1)
    self_masks = (start, own_marks, target_marks, key_places)
    cross_masks = (start, own_marks, memory_marks, jnp.zeros_like(key_places))
    one, two = tie(one, two)
    one = gather_last(one, last)
    two = gather_step(two, last, 1)
    one, two, memory_row = tie(one, two, memory_row)

    wq, wk, wv, wo, blocks = unpack(gather_finish(one), last, 4, rows)
    two = gather_step(two, last, 2)
    memory_row = seq_gather(memory_row, bits[:1])
    named, expand_bias = unpack_vectors(blocks, width, wide)
    (
        query_bias,
        value_bias,
        output_bias,
        first_gain,
        first_shift,
        probe_bias,
        content_bias,
        merge_bias,
        second_gain,
        second_shift,
        shrink_bias,
        third_gain,
        third_shift,
    ) = (named[i : i + 1] for i in range(VECTORS))
    query_one = ((dot(target, wq) + query_bias) * 0.125).astype(BF16)
    key_one = dot(target_row, wk).astype(BF16)
    value_one = (dot(target_row, wv) + value_bias).astype(BF16)
    query_one, key_one, value_one, two, memory_row = tie(query_one, key_one, value_one, two, memory_row)
    mixed_one, log_one = attend_forward(query_one, key_one, value_one, self_masks, block)
    two = gather_last(two, last)
    memory_row = seq_gather(memory_row, bits[1:]).reshape(-1, width)
    mixed_one, log_one, two, memory_row = tie(mixed_one, log_one, two, memory_row)
    first_sum = target.astype(F32) + dot(mixed_one, wo) + output_bias
    first_full, normed_one, inverse_one = norm_forward(first_sum, first_gain, first_shift)
    first_out = first_full.astype(BF16)
    wp, wl, wc, wm, *_ = unpack(gather_finish(two), last, 4, rows)
    query_two = ((dot(first_out, wp) + probe_bias) * 0.125).astype(BF16)
    key_two = dot(memory_row, wl).astype(BF16)
    value_two = (dot(memory_row, wc) + content_bias).astype(BF16)
    mixed_two, log_two = attend_forward(query_two, key_two, value_two, cross_masks, block)
    second_sum = first_out.astype(F32) + dot(mixed_two, wm) + merge_bias
    second_full, normed_two, inverse_two = norm_forward(second_sum, second_gain, second_shift)
    second_out = second_full.astype(BF16)
    pre_act = dot(second_out, expand_weight) + expand_bias
    hidden = exact_gelu(pre_act).astype(BF16)
    third_sum = second_out.astype(F32) + dot(hidden, shrink_weight) + shrink_bias
    third_full, normed_three, inverse_three = norm_forward(third_sum, third_gain, third_shift)
    layer_output = third_full.astype(BF16)

    upstream = cotangent[0].astype(F32)
    third_grad, third_gain_grad, third_shift_grad = norm_backward(upstream, normed_three, inverse_three, third_gain)
    shrink_in = third_grad.astype(BF16)
    shrink_bias_grad = token_sum(shrink_in)
    shrink_grad = t_dot(hidden, shrink_in).astype(BF16)
    shrink_grad, shrink_in, third_grad = tie(shrink_grad, shrink_in, third_grad)
    four = lax.psum_scatter(shrink_grad, ALL, scatter_dimension=0, tiled=True).astype(F32)
    hidden_grad = dot_t(shrink_in, shrink_weight)
    act_grad = jax.vjp(exact_gelu, pre_act)[1](hidden_grad)[0].astype(BF16)
    expand_bias_grad = token_sum(act_grad)
    three = reduce_start([t_dot(second_out, act_grad)], last)
    three, act_grad, third_grad = tie(three, act_grad, third_grad)
    three = reduce_core(three)
    second_grad = third_grad + dot_t(act_grad, expand_weight)
    second_sum_grad, second_gain_grad, second_shift_grad = norm_backward(second_grad, normed_two, inverse_two, second_gain)
    merge_in = second_sum_grad.astype(BF16)
    merge_bias_grad = token_sum(merge_in)
    mixed_two_grad = dot_t(merge_in, wm).astype(BF16)
    mixed_two_grad, three = tie(mixed_two_grad, three)
    three = reduce_step(three, last, 3)
    probe_in, lookup_part, content_part = attend_backward(query_two, key_two, value_two, mixed_two, mixed_two_grad, log_two, cross_masks, block)
    probe_in, lookup_part, content_part, three = tie(probe_in, lookup_part, content_part, three)
    three = reduce_step(three, last, 2)
    probe_bias_grad = token_sum(probe_in)
    content_bias_grad = token_sum(content_part)
    cross_grads = [t_dot(first_out, probe_in), t_dot(memory_row, lookup_part), t_dot(memory_row, content_part), t_dot(mixed_two, merge_in)]
    two = reduce_start(cross_grads, last)
    first_grad = second_sum_grad + dot_t(probe_in, wp)
    first_sum_grad, first_gain_grad, first_shift_grad = norm_backward(first_grad, normed_one, inverse_one, first_gain)
    output_in = first_sum_grad.astype(BF16)
    output_bias_grad = token_sum(output_in)
    mixed_one_grad = dot_t(output_in, wo).astype(BF16)
    two, three, lookup_part, content_part = tie(two, three, lookup_part, content_part)
    two = reduce_core(two)
    three = reduce_step(three, last, 1)
    memory_part = (dot_t(lookup_part, wl) + dot_t(content_part, wc)).reshape(seq, local, width)
    mixed_one_grad, two, three, memory_part = tie(mixed_one_grad, two, three, memory_part)
    two = reduce_step(two, last, 3)
    three = reduce_step(three, last, 0)
    query_in, key_part, value_part = attend_backward(query_one, key_one, value_one, mixed_one, mixed_one_grad, log_one, self_masks, block)
    query_in, key_part, value_part, two, three, memory_part = tie(query_in, key_part, value_part, two, three, memory_part)
    two = reduce_step(two, last, 2)
    memory_part = seq_reduce(memory_part, bits[:0:-1])
    query_bias_grad = token_sum(query_in)
    value_bias_grad = token_sum(value_part)
    self_grads = [t_dot(target, query_in), t_dot(target_row, key_part), t_dot(target_row, value_part), t_dot(mixed_one, output_in)]
    vector_grads = (
        query_bias_grad,
        value_bias_grad,
        output_bias_grad,
        first_gain_grad,
        first_shift_grad,
        probe_bias_grad,
        content_bias_grad,
        merge_bias_grad,
        second_gain_grad,
        second_shift_grad,
        shrink_bias_grad,
        third_gain_grad,
        third_shift_grad,
    )
    one = reduce_start(self_grads, last, pack_sums(vector_grads, expand_bias_grad, width))
    one, two, memory_part, key_part, value_part, query_in = tie(one, two, memory_part, key_part, value_part, query_in)
    one = reduce_core(one)
    two = reduce_step(two, last, 1)
    target_part = (dot_t(key_part, wk) + dot_t(value_part, wv)).reshape(seq, local, width)
    one, two, memory_part, target_part = tie(one, two, memory_part, target_part)
    one = reduce_step(one, last, 3)
    two = reduce_step(two, last, 0)
    target_part = seq_reduce(target_part, bits[:0:-1])
    target_grad = first_sum_grad + dot_t(query_in, wq)
    one, memory_part, target_part, target_grad = tie(one, memory_part, target_part, target_grad)
    one = reduce_step(one, last, 2)
    memory_grad = seq_reduce(memory_part, bits[:1])[0]
    one, target_part, memory_grad = tie(one, target_part, memory_grad)
    one = reduce_step(one, last, 1)
    target_grad = target_grad + seq_reduce(target_part, bits[:1])[0]
    one = reduce_step(one, last, 0)

    one, two, three = (reduce_finish(t) for t in (one, two, three))
    wide_sum = one[4 * rows :]
    sums = [wide_sum[seat(i)[0], seat(i)[1] : seat(i)[1] + rows] for i in range(VECTORS)]
    row, lane = seat(VECTORS)
    result = Params(
        query_weight=one[:rows],
        key_weight=one[rows : 2 * rows],
        value_weight=one[2 * rows : 3 * rows],
        output_weight=one[3 * rows : 4 * rows],
        probe_weight=two[:rows],
        lookup_weight=two[rows : 2 * rows],
        content_weight=two[2 * rows : 3 * rows],
        merge_weight=two[3 * rows :],
        expand_weight=three.reshape(rows, wide),
        shrink_weight=four,
        expand_bias=wide_sum[row, lane : lane + wide // owners()],
        query_bias=sums[0],
        value_bias=sums[1],
        output_bias=sums[2],
        first_gain=sums[3],
        first_shift=sums[4],
        probe_bias=sums[5],
        content_bias=sums[6],
        merge_bias=sums[7],
        second_gain=sums[8],
        second_shift=sums[9],
        shrink_bias=sums[10],
        third_gain=sums[11],
        third_shift=sums[12],
    )
    return (layer_output[None], target_grad[None], memory_grad[None]) + tuple(result)


def per_device(target, memory, cotangent, target_segments, memory_segments, *shards):
    p = Params(*shards)
    target = target[0]
    memory = memory[0]
    local, width = target.shape
    seq = lax.axis_size("seq")
    place_in_row = lax.axis_index("seq")
    me = place_in_row.astype(jnp.int32).reshape(1)
    offsets = seq_offsets(seq)
    bits = seq_bits()
    block = local
    rows = p.query_weight.shape[0]
    wide = p.expand_weight.shape[1]
    last, near, back = NEAR_LAST, DP_LAST, NEAR_BACK
    heads = width // HEAD_DIM // seq
    span = heads * HEAD_DIM
    space = -(-span // PAIR) * PAIR

    vectors = pack_vectors(vectors_of(p) + (p.expand_bias,), width)
    packed = pack_heads([p.query_weight, p.key_weight, p.value_weight], vectors, me, seq)
    two = gather_start([p.output_weight, p.probe_weight, p.lookup_weight, p.content_weight, p.merge_weight])
    three, four = gather_start([p.expand_weight]), gather_start([p.shrink_weight])
    marks = jnp.stack([target_segments[0], memory_segments[0]]).astype(BF16)
    marks = jnp.pad(marks, ((0, BLOCK - 2), (0, width - local)))
    target_pack = jnp.concatenate([target, marks], axis=0)[None]
    one = jnp.stack(exchange([packed[d] for d in range(seq)]))
    target_pack = seq_gather(target_pack, bits[:1])
    two = gather_step(two, back, 0)
    one, three, four = tie(one, three, four)
    one = gather_step(one, near, 0)
    one, target_pack, two, memory_row = tie(one, target_pack, two, memory[None])
    one = gather_step(one, near, 1)
    target_pack = seq_gather(target_pack, bits[1:])
    memory_row = seq_gather(memory_row, bits[:1])
    target_row = target_pack[:, :local].reshape(-1, width)
    block_places = jnp.stack([(place_in_row ^ o) * local for o in offsets]).astype(jnp.int32)
    key_places = (block_places[:, None] + jnp.arange(local, dtype=jnp.int32)).reshape(1, -1)
    target_marks = target_pack[:, local, :local].reshape(1, -1).astype(jnp.int32)
    memory_marks = target_pack[:, local + 1, :local].reshape(1, -1).astype(jnp.int32)
    own_marks = target_segments.reshape(local, 1)
    self_masks = (block_places, target_marks.reshape(-1, 1), target_marks, key_places)
    cross_masks = (block_places[:1], own_marks, memory_marks, jnp.zeros_like(key_places))
    one, two, memory_row = tie(one, two, memory_row)
    got = stage_swap(one, near, 2)
    two = gather_step(two, back, 1)
    one, got, three, four = tie(one, got, three, four)

    two = gather_step(two, back, 2)
    three = gather_step(three, back, 0)
    four = gather_step(four, back, 0)
    memory_row = seq_gather(memory_row, bits[1:]).reshape(-1, width)
    pieces = [v.reshape(v.shape[0], -1, BLOCK, width) for v in (one, got)]
    wqkv, blocks = place(pieces, group_owners(near), 1, rows // BLOCK)
    wqkv = wqkv.reshape(-1, width)
    named, expand_bias = unpack_vectors(blocks.reshape(-1, BLOCK, width), width, wide)
    (
        query_bias,
        value_bias,
        output_bias,
        first_gain,
        first_shift,
        probe_bias,
        content_bias,
        merge_bias,
        second_gain,
        second_shift,
        shrink_bias,
        third_gain,
        third_shift,
    ) = (named[i : i + 1] for i in range(VECTORS))
    mine = lambda v: jnp.pad(lax.dynamic_slice(v, (0, place_in_row * span), (1, span)), ((0, 0), (0, space - span)))
    row_bias = jnp.concatenate([mine(query_bias), jnp.zeros((1, space), F32), mine(value_bias)], axis=1)
    scale = jnp.where(jnp.arange(3 * space) < space, 0.125, 1.0)[None]
    qkv = ((dot(target_row, wqkv) + row_bias) * scale).astype(BF16)
    qkv, two, three, four, memory_row = tie(qkv, two, three, four, memory_row)
    two = gather_last(two, back)
    three = gather_step(three, back, 1)
    four = gather_step(four, back, 1)
    mixed_row, log_one = row_forward(qkv, self_masks, heads, local, block)
    mixed_row, two, three, four = tie(mixed_row, two, three, four)
    sent = [mixed_row[i * local : (i + 1) * local] for i in range(seq)]
    mixed_one = join_heads(exchange([sent[offsets.index(d)] for d in range(seq)]), me, span)
    two_pieces = gather_finish(two)
    mixed_one, two_pieces, three, four = tie(mixed_one, two_pieces, three, four)
    three = gather_step(three, back, 2)
    four = gather_step(four, back, 2)
    wo, wp, wl, wc, wm, *_ = unpack(two_pieces, back, 5, rows)
    first_sum = target.astype(F32) + dot(mixed_one, wo) + output_bias
    first_full, normed_one, inverse_one = norm_forward(first_sum, first_gain, first_shift)
    first_out = first_full.astype(BF16)
    query_two = ((dot(first_out, wp) + probe_bias) * 0.125).astype(BF16)
    key_two = dot(memory_row, wl).astype(BF16)
    value_two = (dot(memory_row, wc) + content_bias).astype(BF16)
    query_two, key_two, value_two, three, four = tie(query_two, key_two, value_two, three, four)
    three = gather_last(three, back)
    mixed_two, log_two = attend_forward(query_two, key_two, value_two, cross_masks, block)
    mixed_two, three, four = tie(mixed_two, three, four)
    four = gather_last(four, back)
    three = gather_finish(three)
    second_sum = first_out.astype(F32) + dot(mixed_two, wm) + merge_bias
    second_full, normed_two, inverse_two = norm_forward(second_sum, second_gain, second_shift)
    second_out = second_full.astype(BF16)
    expand_weight, *_ = unpack(three, back, 1, rows)
    second_out, expand_weight, four = tie(second_out, expand_weight, four)
    four = gather_finish(four)
    hidden, slope = expand_gelu(second_out, expand_weight, expand_bias)
    hidden, four = tie(hidden, four)
    shrink_weight, *_ = unpack(four, back, 1, p.shrink_weight.shape[0])
    third_sum = second_out.astype(F32) + dot(hidden, shrink_weight) + shrink_bias
    third_full, normed_three, inverse_three = norm_forward(third_sum, third_gain, third_shift)
    layer_output = third_full.astype(BF16)

    upstream = cotangent[0].astype(F32)
    third_grad, third_gain_grad, third_shift_grad = norm_backward(upstream, normed_three, inverse_three, third_gain)
    shrink_in = third_grad.astype(BF16)
    shrink_bias_grad = token_sum(shrink_in)
    shrink_grad = t_dot(hidden, shrink_in).astype(BF16)
    four = reduce_start([shrink_grad], last)
    four, shrink_in, third_grad = tie(four, shrink_in, third_grad)
    four = reduce_core(four)
    act_grad = (dot_t(shrink_in, shrink_weight) * slope).astype(BF16)
    expand_bias_grad = token_sum(act_grad)
    three = reduce_start([t_dot(second_out, act_grad)], last)
    three, four, act_grad, third_grad = tie(three, four, act_grad, third_grad)
    three = reduce_core(three)
    four = reduce_step(four, last, 3)
    second_grad = third_grad + dot_t(act_grad, expand_weight)
    second_sum_grad, second_gain_grad, second_shift_grad = norm_backward(second_grad, normed_two, inverse_two, second_gain)
    merge_in = second_sum_grad.astype(BF16)
    merge_bias_grad = token_sum(merge_in)
    mixed_two_grad = dot_t(merge_in, wm).astype(BF16)
    mixed_two_grad, three = tie(mixed_two_grad, three)
    three = reduce_step(three, last, 3)
    probe_in, lookup_part, content_part = attend_backward(query_two, key_two, value_two, mixed_two, mixed_two_grad, log_two, cross_masks, block)
    probe_in, lookup_part, content_part, three, four = tie(probe_in, lookup_part, content_part, three, four)
    three = reduce_step(three, last, 2)
    four = reduce_step(four, last, 2)
    first_grad = second_sum_grad + dot_t(probe_in, wp)
    first_sum_grad, first_gain_grad, first_shift_grad = norm_backward(first_grad, normed_one, inverse_one, first_gain)
    output_in = first_sum_grad.astype(BF16)
    mixed_one_grad = dot_t(output_in, wo).astype(BF16)
    split = split_heads(mixed_one_grad, me, seq, space)
    split, probe_in, lookup_part, content_part, output_in = tie(split, probe_in, lookup_part, content_part, output_in)
    came = exchange([split[d] for d in range(seq)])
    mixed_row_grad = jnp.concatenate([came[o] for o in offsets], axis=0)
    output_bias_grad = token_sum(output_in)
    probe_bias_grad = token_sum(probe_in)
    content_bias_grad = token_sum(content_part)
    cross_grads = [
        t_dot(mixed_one, output_in),
        t_dot(first_out, probe_in),
        t_dot(memory_row, lookup_part),
        t_dot(memory_row, content_part),
        t_dot(mixed_two, merge_in),
    ]
    two = reduce_start(cross_grads, back)
    mixed_row_grad, two, three, four, lookup_part, content_part = tie(mixed_row_grad, two, three, four, lookup_part, content_part)
    two = reduce_core(two)
    three = reduce_step(three, last, 1)
    four = reduce_step(four, last, 1)
    memory_part = (dot_t(lookup_part, wl) + dot_t(content_part, wc)).reshape(seq, local, width)
    mixed_row_grad, two, memory_part = tie(mixed_row_grad, two, memory_part)
    two = reduce_step(two, back, 3)
    memory_part = seq_reduce(memory_part, bits[:0:-1])
    qkv_grad = row_backward(qkv, mixed_row, mixed_row_grad, log_one, self_masks, heads, local, block)
    qkv_grad, two, three, four, memory_part = tie(qkv_grad, two, three, four, memory_part)
    three = reduce_step(three, last, 0)
    four = reduce_step(four, last, 0)
    two = reduce_step(two, back, 2)
    memory_grad = seq_reduce(memory_part, bits[:1])[0]
    row_grad = t_dot(target_row, qkv_grad)
    sums = token_sum(qkv_grad)
    spot = lambda v: lax.dynamic_update_slice(jnp.zeros((1, width), F32), v, (0, place_in_row * span))
    vector_grads = (
        spot(sums[:, :span]),
        spot(sums[:, 2 * space : 2 * space + span]),
        output_bias_grad,
        first_gain_grad,
        first_shift_grad,
        probe_bias_grad,
        content_bias_grad,
        merge_bias_grad,
        second_gain_grad,
        second_shift_grad,
        shrink_bias_grad,
        third_gain_grad,
        third_shift_grad,
    )
    tail = pack_sums(vector_grads, expand_bias_grad, width)
    terms = [row_grad.astype(BF16).reshape(owners(), -1, BLOCK, width), tail.reshape(owners(), -1, BLOCK, width)]
    one = tuple(spread(terms, group_owners(near)))
    one, qkv_grad = tie(one, qkv_grad)
    one = reduce_step(one, near, 2)
    two = reduce_step(two, back, 1)
    target_part = dot_t(qkv_grad, wqkv).reshape(seq, local, width)
    one, two, target_part = tie(one, two, target_part)
    one = reduce_step(one, near, 1)
    target_part = seq_reduce(target_part, bits[:0:-1])
    one, two, target_part = tie(one, two, target_part)
    one = reduce_step(one, near, 0)
    target_grad = first_sum_grad + seq_reduce(target_part, bits[:1])[0]
    slots = one[0].astype(BF16).reshape(seq, -1, width)
    slots, two = tie(slots, two)
    one = exchange([slots[d] for d in range(seq)])
    two = reduce_step(two, back, 0)

    query_grad, key_grad, value_grad, wide_sum = unpack_heads(one, me, 3, rows)
    two, three, four = (reduce_finish(t) for t in (two, three, four))
    sums = [wide_sum[seat(i)[0], seat(i)[1] : seat(i)[1] + rows] for i in range(VECTORS)]
    row, lane = seat(VECTORS)
    result = Params(
        query_weight=query_grad,
        key_weight=key_grad,
        value_weight=value_grad,
        output_weight=two[:rows],
        probe_weight=two[rows : 2 * rows],
        lookup_weight=two[2 * rows : 3 * rows],
        content_weight=two[3 * rows : 4 * rows],
        merge_weight=two[4 * rows :],
        expand_weight=three.reshape(rows, wide),
        shrink_weight=four,
        expand_bias=wide_sum[row, lane : lane + wide // owners()],
        query_bias=sums[0],
        value_bias=sums[1],
        output_bias=sums[2],
        first_gain=sums[3],
        first_shift=sums[4],
        probe_bias=sums[5],
        content_bias=sums[6],
        merge_bias=sums[7],
        second_gain=sums[8],
        second_shift=sums[9],
        shrink_bias=sums[10],
        third_gain=sums[11],
        third_shift=sums[12],
    )
    return (layer_output[None], target_grad[None], memory_grad[None]) + tuple(result)


def solution(mesh):
    tokens = P("dp", "seq", None)
    matrix = P(ALL, None)
    vector = P(ALL)
    params = Params(*[vector] * len(Params._fields))._replace(
        query_weight=matrix,
        key_weight=matrix,
        value_weight=matrix,
        output_weight=matrix,
        probe_weight=matrix,
        lookup_weight=matrix,
        content_weight=matrix,
        merge_weight=matrix,
        expand_weight=matrix,
        shrink_weight=matrix,
    )
    split = mesh.size == FLAT and mesh.shape["seq"] == 4
    return jax.shard_map(
        per_device if split else per_device_by_rows,
        mesh=mesh,
        in_specs=(tokens, tokens, tokens, P("dp", "seq"), P("dp", "seq")) + tuple(params),
        out_specs=(tokens, tokens, tokens) + tuple(params),
        check_vma=False,
    )
```

```python
from typing import Any, NamedTuple

import jax
import jax.numpy as jnp
from jax import lax
from jax.experimental import pallas as pl
from jax.experimental.pallas import tpu as pltpu
from jax.sharding import PartitionSpec as P

HEAD_DIM = 64
PAIR = 2 * HEAD_DIM
NEG_FILL = -1e30
EPSILON = 1e-05
BF16 = jnp.bfloat16
F32 = jnp.float32
ALL = ("dp", "seq")

class Params(NamedTuple):
    query_weight: Any
    query_bias: Any
    key_weight: Any
    value_weight: Any
    value_bias: Any
    output_weight: Any
    output_bias: Any
    first_gain: Any
    first_shift: Any
    probe_weight: Any
    probe_bias: Any
    lookup_weight: Any
    content_weight: Any
    content_bias: Any
    merge_weight: Any
    merge_bias: Any
    second_gain: Any
    second_shift: Any
    expand_weight: Any
    expand_bias: Any
    shrink_weight: Any
    shrink_bias: Any
    third_gain: Any
    third_shift: Any


def vectors_of(p):
    return (
        p.query_bias,
        p.value_bias,
        p.output_bias,
        p.first_gain,
        p.first_shift,
        p.probe_bias,
        p.content_bias,
        p.merge_bias,
        p.second_gain,
        p.second_shift,
        p.shrink_bias,
        p.third_gain,
        p.third_shift,
    )


VECTORS = 13
LANES = 128


def dot(left, right):
    return jnp.dot(left, right, preferred_element_type=F32)


def dot_t(left, right):
    return lax.dot_general(left, right, (((1,), (1,)), ((), ())), preferred_element_type=F32)


def t_dot(left, right):
    return lax.dot_general(left, right, (((0,), (0,)), ((), ())), preferred_element_type=F32)


def token_sum(values):
    return jnp.sum(values.astype(F32), axis=0, keepdims=True)


TILES = 3


def fill_mask(block, first, qseg, kseg_ref, kpos_ref, bias, base, flags, row):
    rows = qseg.shape[0]
    place = first + lax.broadcasted_iota(jnp.int32, (rows, block), 0)
    for j in range(bias.shape[1] // block):
        cols = pl.ds(j * block, block)
        allowed = (kseg_ref[:, cols] == qseg) & (kpos_ref[:, cols] <= place)
        term = jnp.where(allowed, 0.0, NEG_FILL)
        bias[pl.ds(base, rows), cols] = term
        flags[row, j] = (jnp.max(term) > -1.0).astype(jnp.int32)


def one_head(value, head):
    lane = lax.broadcasted_iota(jnp.int32, value.shape, 1)
    return jnp.where((lane < HEAD_DIM) == (head == 0), value, jnp.zeros_like(value))


def stacked(value, halves):
    return jnp.concatenate([one_head(value, head) for head in range(halves)], axis=0)


def tiles_forward(block, tiles, bias, flags, scores, peaks, sums, mixed):
    rows, total = bias.shape
    peaks[...] = jnp.full(peaks.shape, NEG_FILL, F32)
    sums[...] = jnp.zeros(sums.shape, F32)
    mixed[...] = jnp.zeros(mixed.shape, F32)
    for j in range(total // block):

        @pl.when(flags[0, j] > 0)
        def _():
            cols = pl.ds(j * block, block)
            for query, key, _, at in tiles:
                part = dot_t(query, key(cols))
                for half in range(query.shape[0] // rows):
                    own = pl.ds(at + half * rows, rows)
                    term = part[half * rows : (half + 1) * rows] + bias[:, cols]
                    scores[own, cols] = term
                    high = peaks[own]
                    for c in range(block // LANES):
                        high = jnp.maximum(high, term[:, c * LANES : (c + 1) * LANES])
                    peaks[own] = high

    peak = jnp.max(peaks[...], axis=-1, keepdims=True)
    peaks[...] = jnp.broadcast_to(peak, peaks.shape)
    for j in range(total // block):

        @pl.when(flags[0, j] > 0)
        def _():
            cols = pl.ds(j * block, block)
            for query, _, value, at in tiles:
                own = pl.ds(at, query.shape[0])
                part = jnp.exp(scores[own, cols] - peaks[own, 0:1])
                add = sums[own]
                for c in range(block // LANES):
                    add = add + part[:, c * LANES : (c + 1) * LANES]
                sums[own] = add
                mixed[own] += dot(part.astype(BF16), value(cols))

    whole = jnp.sum(sums[...], axis=-1, keepdims=True)
    return mixed[...] * (1.0 / whole), peak + jnp.log(whole)


def tiles_backward(block, tiles, bias, flags, query_sum, key_sum, value_sum):
    rows, total = bias.shape
    query_sum[...] = jnp.zeros(query_sum.shape, F32)
    for j in range(total // block):

        @pl.when(flags[0, j] > 0)
        def _():
            cols = pl.ds(j * block, block)
            for query, grad, log, inner, key_of, value, at, lanes in tiles:
                key = key_of(cols)
                scores = dot_t(query, key)
                slope = dot_t(grad, value(cols))
                terms = [scores[i : i + rows] + bias[:, cols] for i in range(0, query.shape[0], rows)]
                part = jnp.exp((jnp.concatenate(terms, axis=0) if len(terms) > 1 else terms[0]) - log)
                score_grad = (part * (slope - inner)).astype(BF16)
                query_sum[pl.ds(at, query.shape[0])] += dot(score_grad, key)
                key_sum[cols, lanes] += t_dot(score_grad, query)
                value_sum[cols, lanes] += t_dot(part.astype(BF16), grad)


def lower_lanes(shape):
    return lax.broadcasted_iota(jnp.int32, shape, 1) < HEAD_DIM


def eighth(value):
    return (value.astype(BF16) * 0.125).astype(BF16)


def attend_kernel(block, q0_ref, q_ref, k_ref, v_ref, qseg_ref, kseg_ref, kpos_ref, o_ref, log_ref, bias, flags, *scratch):
    @pl.when(pl.program_id(0) == 0)
    def _():
        fill_mask(block, q0_ref[0], qseg_ref[...], kseg_ref, kpos_ref, bias, 0, flags, 0)

    rows = o_ref.shape[0]
    tiles = []
    for t in range(TILES):
        lanes = pl.ds(t * PAIR, PAIR)
        key = lambda cols, lanes=lanes: k_ref[cols, lanes]
        value = lambda cols, lanes=lanes: v_ref[cols, lanes]
        tiles.append((stacked(q_ref[:, lanes], 2), key, value, 2 * t * rows))
    out, log = tiles_forward(block, tiles, bias, flags, *scratch)
    low = lower_lanes((rows, PAIR))
    for t in range(TILES):
        lanes = pl.ds(t * PAIR, PAIR)
        upper, lower = slice(2 * t * rows, (2 * t + 1) * rows), slice((2 * t + 1) * rows, (2 * t + 2) * rows)
        o_ref[:, lanes] = jnp.where(low, out[upper], out[lower]).astype(BF16)
        log_ref[:, lanes] = jnp.where(low, log[upper], log[lower])


def attend_back_kernel(block, q0_ref, q_ref, k_ref, v_ref, o_ref, g_ref, log_ref, qseg_ref, kseg_ref, kpos_ref, dq_ref, dk_ref, dv_ref, bias, flags, query_sum, key_sum, value_sum):
    @pl.when(pl.program_id(0) == 0)
    def _():
        fill_mask(block, q0_ref[0], qseg_ref[...], kseg_ref, kpos_ref, bias, 0, flags, 0)

    key_sum[...] = jnp.zeros(key_sum.shape, F32)
    value_sum[...] = jnp.zeros(value_sum.shape, F32)
    rows = q_ref.shape[0]
    tiles = []
    for t in range(TILES):
        lanes = pl.ds(t * PAIR, PAIR)
        key = lambda cols, lanes=lanes: k_ref[cols, lanes]
        value = lambda cols, lanes=lanes: v_ref[cols, lanes]
        grad = stacked(g_ref[:, lanes], 2)
        mixed = o_ref[:, lanes].astype(F32)
        inner = jnp.sum(grad.astype(F32) * jnp.concatenate([mixed, mixed], axis=0), axis=-1, keepdims=True)
        log = jnp.concatenate([log_ref[:, t * PAIR + i * HEAD_DIM : t * PAIR + i * HEAD_DIM + 1] for i in range(2)], axis=0)
        tiles.append((stacked(q_ref[:, lanes], 2), grad, log, inner, key, value, 2 * t * rows, lanes))
    tiles_backward(block, tiles, bias, flags, query_sum, key_sum, value_sum)
    for t in range(TILES):
        at = 2 * t * rows
        dq_ref[:, pl.ds(t * PAIR, PAIR)] = eighth(jnp.where(lower_lanes((rows, PAIR)), query_sum[at : at + rows], query_sum[at + rows : at + 2 * rows]))
    dk_ref[...] = key_sum[...].astype(BF16)
    dv_ref[...] = value_sum[...].astype(BF16)


def attend_specs(rows, total):
    whole = lambda shape: pl.BlockSpec(shape, lambda i: (0, 0))
    strip = lambda count: pl.BlockSpec((count, TILES * PAIR), lambda i: (0, i))
    return (
        pl.BlockSpec(memory_space=pltpu.SMEM),
        strip(rows),
        strip(total),
        [whole((rows, 1)), whole((1, total)), whole((1, total))],
    )


def forward_scratch(rows, total, heads):
    return [pltpu.VMEM((heads * rows, total), F32)] + [pltpu.VMEM((heads * rows, LANES), F32)] * 3


def attend_forward(query, key, value, masks, block):
    rows, width = query.shape
    total = key.shape[0]
    scalar, narrow, tall, marks = attend_specs(rows, total)
    q0, qseg, kseg, kpos = masks
    return pl.pallas_call(
        lambda *refs: attend_kernel(block, *refs),
        grid=(width // (TILES * PAIR),),
        in_specs=[scalar, narrow, tall, tall] + marks,
        out_specs=[narrow, narrow],
        out_shape=[jax.ShapeDtypeStruct((rows, width), BF16), jax.ShapeDtypeStruct((rows, width), F32)],
        scratch_shapes=[pltpu.VMEM((rows, total), F32), pltpu.SMEM((1, total // block), jnp.int32)] + forward_scratch(rows, total, 2 * TILES),
        cost_estimate=pl.CostEstimate(flops=8 * rows * total * width, bytes_accessed=8 * total * width, transcendentals=rows * total * 12),
        compiler_params=pltpu.CompilerParams(dimension_semantics=("arbitrary",)),
        name="attend_forward",
    )(q0, query, key, value, qseg, kseg, kpos)


def attend_backward(query, key, value, mixed, grad, log, masks, block):
    rows, width = query.shape
    total = key.shape[0]
    scalar, narrow, tall, marks = attend_specs(rows, total)
    q0, qseg, kseg, kpos = masks
    return pl.pallas_call(
        lambda *refs: attend_back_kernel(block, *refs),
        grid=(width // (TILES * PAIR),),
        in_specs=[scalar, narrow, tall, tall, narrow, narrow, narrow] + marks,
        out_specs=[narrow, tall, tall],
        out_shape=[
            jax.ShapeDtypeStruct((rows, width), BF16),
            jax.ShapeDtypeStruct((total, width), BF16),
            jax.ShapeDtypeStruct((total, width), BF16),
        ],
        scratch_shapes=[
            pltpu.VMEM((rows, total), F32),
            pltpu.SMEM((1, total // block), jnp.int32),
            pltpu.VMEM((2 * TILES * rows, PAIR), F32),
            pltpu.VMEM((total, TILES * PAIR), F32),
            pltpu.VMEM((total, TILES * PAIR), F32),
        ],
        cost_estimate=pl.CostEstimate(flops=20 * rows * total * width, bytes_accessed=16 * total * width, transcendentals=rows * total * 12),
        compiler_params=pltpu.CompilerParams(dimension_semantics=("arbitrary",)),
        name="attend_backward",
    )(q0, query, key, value, mixed, grad, log, qseg, kseg, kpos)


def seats_of(heads, space):
    return [(pl.ds(t, PAIR), pl.ds(space + t, PAIR), pl.ds(2 * space + t, PAIR), min(2, heads - 2 * (t // PAIR))) for t in range(0, space, PAIR)]


def row_kernel(block, heads, q0_ref, qkv_ref, qseg_ref, kseg_ref, kpos_ref, o_ref, log_ref, bias, flags, *scratch):
    rows, space = o_ref.shape
    step = pl.program_id(0)
    own = pl.ds(pl.multiple_of(step * rows, rows), rows)
    fill_mask(block, q0_ref[step], qseg_ref[...], kseg_ref, kpos_ref, bias, 0, flags, 0)
    tiles = []
    for tile, (query_lanes, key_lanes, value_lanes, halves) in enumerate(seats_of(heads, space)):
        key = lambda cols, lanes=key_lanes: qkv_ref[cols, lanes]
        value = lambda cols, lanes=value_lanes: qkv_ref[cols, lanes]
        tiles.append((stacked(qkv_ref[own, query_lanes], halves), key, value, 2 * tile * rows))
    out, log = tiles_forward(block, tiles, bias, flags, *scratch)
    low = lower_lanes((rows, PAIR))
    blank = jnp.zeros((rows, PAIR), F32)
    for query, _, _, at in tiles:
        lanes = pl.ds(at // (2 * rows) * PAIR, PAIR)
        pair = query.shape[0] > rows
        o_ref[:, lanes] = jnp.where(low, out[at : at + rows], out[at + rows : at + 2 * rows] if pair else blank).astype(BF16)
        log_ref[:, lanes] = jnp.where(low, log[at : at + rows], log[at + rows : at + 2 * rows] if pair else blank)


def row_back_kernel(block, heads, q0_ref, qkv_ref, o_ref, g_ref, log_ref, qseg_ref, kseg_ref, kpos_ref, grads_ref, bias, flags, query_sum, key_sum, value_sum):
    rows, space = o_ref.shape
    step = pl.program_id(0)
    own = pl.ds(pl.multiple_of(step * rows, rows), rows)
    fill_mask(block, q0_ref[step], qseg_ref[...], kseg_ref, kpos_ref, bias, 0, flags, 0)

    @pl.when(step == 0)
    def _():
        key_sum[...] = jnp.zeros(key_sum.shape, F32)
        value_sum[...] = jnp.zeros(value_sum.shape, F32)

    tiles = []
    for tile, (query_lanes, key_lanes, value_lanes, halves) in enumerate(seats_of(heads, space)):
        key = lambda cols, lanes=key_lanes: qkv_ref[cols, lanes]
        value = lambda cols, lanes=value_lanes: qkv_ref[cols, lanes]
        grad = stacked(g_ref[:, query_lanes], halves)
        mixed = o_ref[:, query_lanes].astype(F32)
        inner = jnp.sum(grad.astype(F32) * jnp.concatenate([mixed] * halves, axis=0), axis=-1, keepdims=True)
        lane = tile * PAIR
        log = jnp.concatenate([log_ref[:, lane + i * HEAD_DIM : lane + i * HEAD_DIM + 1] for i in range(halves)], axis=0)
        tiles.append((stacked(qkv_ref[own, query_lanes], halves), grad, log, inner, key, value, 2 * tile * rows, query_lanes))
    tiles_backward(block, tiles, bias, flags, query_sum, key_sum, value_sum)
    low = lower_lanes((rows, PAIR))
    for query, _, _, _, _, _, at, lanes in tiles:
        upper = query_sum[at + rows : at + 2 * rows] if query.shape[0] > rows else jnp.zeros((rows, PAIR), F32)
        grads_ref[own, lanes] = eighth(jnp.where(low, query_sum[at : at + rows], upper))

    @pl.when(step == pl.num_programs(0) - 1)
    def _():
        grads_ref[:, space : 2 * space] = key_sum[...].astype(BF16)
        grads_ref[:, 2 * space :] = value_sum[...].astype(BF16)


def row_specs(rows, total, space):
    whole = lambda shape: pl.BlockSpec(shape, lambda i: (0, 0))
    strip = lambda width: pl.BlockSpec((rows, width), lambda i: (i, 0))
    return (
        pl.BlockSpec(memory_space=pltpu.SMEM),
        whole((total, 3 * space)),
        strip(space),
        [strip(1), whole((1, total)), whole((1, total))],
    )


def row_forward(qkv, masks, heads, rows, block):
    total, space = qkv.shape[0], qkv.shape[1] // 3
    scalar, full, narrow, marks = row_specs(rows, total, space)
    q0, qseg, kseg, kpos = masks
    return pl.pallas_call(
        lambda *refs: row_kernel(block, heads, *refs),
        grid=(total // rows,),
        in_specs=[scalar, full] + marks,
        out_specs=[narrow, narrow],
        out_shape=[jax.ShapeDtypeStruct((total, space), BF16), jax.ShapeDtypeStruct((total, space), F32)],
        scratch_shapes=[pltpu.VMEM((rows, total), F32), pltpu.SMEM((1, total // block), jnp.int32)] + forward_scratch(rows, total, heads),
        cost_estimate=pl.CostEstimate(flops=4 * total * total * space, bytes_accessed=10 * total * space, transcendentals=total * total * heads),
        compiler_params=pltpu.CompilerParams(dimension_semantics=("arbitrary",)),
        name="row_forward",
    )(q0, qkv, qseg, kseg, kpos)


def row_backward(qkv, mixed, grad, log, masks, heads, rows, block):
    total, space = mixed.shape
    scalar, full, narrow, marks = row_specs(rows, total, space)
    q0, qseg, kseg, kpos = masks
    return pl.pallas_call(
        lambda *refs: row_back_kernel(block, heads, *refs),
        grid=(total // rows,),
        in_specs=[scalar, full, narrow, narrow, narrow] + marks,
        out_specs=full,
        out_shape=jax.ShapeDtypeStruct((total, 3 * space), BF16),
        scratch_shapes=[
            pltpu.VMEM((rows, total), F32),
            pltpu.SMEM((1, total // block), jnp.int32),
            pltpu.VMEM((heads * rows, PAIR), F32),
            pltpu.VMEM((total, space), F32),
            pltpu.VMEM((total, space), F32),
        ],
        cost_estimate=pl.CostEstimate(flops=10 * total * total * space, bytes_accessed=20 * total * space, transcendentals=total * total * heads),
        compiler_params=pltpu.CompilerParams(dimension_semantics=("arbitrary",)),
        name="row_backward",
    )(q0, qkv, mixed, grad, log, qseg, kseg, kpos)


def split_kernel(span, me_ref, value_ref, out_ref):
    rows, space = out_ref.shape[1:]
    for group in range(out_ref.shape[0]):
        part = value_ref[:, group * span : (group + 1) * span].astype(F32)
        out_ref[me_ref[0] ^ group] = jnp.concatenate([part, jnp.zeros((rows, space - span), F32)], axis=1).astype(BF16)


def split_heads(value, me, groups, space):
    rows, width = value.shape
    return pl.pallas_call(
        lambda *refs: split_kernel(width // groups, *refs),
        out_shape=jax.ShapeDtypeStruct((groups, rows, space), BF16),
        in_specs=[pl.BlockSpec(memory_space=pltpu.SMEM), pl.BlockSpec(memory_space=pltpu.VMEM)],
        out_specs=pl.BlockSpec(memory_space=pltpu.VMEM),
        name="split_heads",
    )(me, value)


def join_kernel(span, me_ref, *refs):
    pieces, (out_ref, held) = refs[:-2], refs[-2:]
    for d, piece in enumerate(pieces):
        held[d] = piece[...]
    parts = [held[me_ref[0] ^ group].astype(F32)[:, :span] for group in range(len(pieces))]
    out_ref[...] = jnp.concatenate(parts, axis=1).astype(BF16)


def join_heads(pieces, me, span):
    rows, space = pieces[0].shape
    groups = len(pieces)
    vmem = pl.BlockSpec(memory_space=pltpu.VMEM)
    return pl.pallas_call(
        lambda *refs: join_kernel(span, *refs),
        out_shape=jax.ShapeDtypeStruct((rows, groups * span), BF16),
        in_specs=[pl.BlockSpec(memory_space=pltpu.SMEM)] + [vmem] * groups,
        out_specs=vmem,
        scratch_shapes=[pltpu.VMEM((groups, rows, space), BF16)],
        name="join_heads",
    )(me, *pieces)


def pack_heads_kernel(weights, span, me_ref, *refs):
    out_ref = refs[-1]
    vectors = refs[weights][...]
    rows = refs[0].shape[0]
    space = out_ref.shape[2] // weights
    for group in range(out_ref.shape[0]):
        parts = []
        for ref in refs[:weights]:
            parts += [ref[:, group * span : (group + 1) * span].astype(F32), jnp.zeros((rows, space - span), F32)]
        out_ref[me_ref[0] ^ group, :rows] = jnp.concatenate(parts, axis=1).astype(BF16)
        out_ref[me_ref[0] ^ group, rows:] = vectors


def pack_heads(weights, vectors, me, groups):
    rows, width = weights[0].shape
    vmem = pl.BlockSpec(memory_space=pltpu.VMEM)
    return pl.pallas_call(
        lambda *refs: pack_heads_kernel(len(weights), width // groups, *refs),
        out_shape=jax.ShapeDtypeStruct((groups, rows + vectors.shape[0], width), BF16),
        in_specs=[pl.BlockSpec(memory_space=pltpu.SMEM)] + [vmem] * (len(weights) + 1),
        out_specs=vmem,
        name="pack_heads",
    )(me, *weights, vectors)


def unpack_heads_kernel(weights, span, me_ref, *refs):
    groups = len(refs) - weights - 2
    pieces, outs, tail_ref, held = refs[:groups], refs[groups:-2], refs[-2], refs[-1]
    rows = outs[0].shape[0]
    space = pieces[0].shape[1] // weights
    for d, piece in enumerate(pieces):
        held[d] = piece[...].astype(F32)
    for i, out in enumerate(outs):
        out[...] = jnp.concatenate([held[me_ref[0] ^ group, :rows, i * space : i * space + span] for group in range(groups)], axis=1)
    tail_ref[...] = sum(held[d, rows:] for d in range(groups))


def unpack_heads(pieces, me, weights, rows):
    groups = len(pieces)
    width = pieces[0].shape[1]
    vmem = pl.BlockSpec(memory_space=pltpu.VMEM)
    return pl.pallas_call(
        lambda *refs: unpack_heads_kernel(weights, width // groups, *refs),
        out_shape=[jax.ShapeDtypeStruct((rows, width), F32)] * weights + [jax.ShapeDtypeStruct((pieces[0].shape[0] - rows, width), F32)],
        in_specs=[pl.BlockSpec(memory_space=pltpu.SMEM)] + [vmem] * groups,
        out_specs=[vmem] * (weights + 1),
        scratch_shapes=[pltpu.VMEM((groups,) + pieces[0].shape, F32)],
        name="unpack_heads",
    )(me, *pieces)


def norm_forward(hidden, gain, shift):
    centred = hidden - jnp.mean(hidden, axis=-1, keepdims=True)
    inverse = lax.rsqrt(jnp.mean(centred * centred, axis=-1, keepdims=True) + EPSILON)
    normed = centred * inverse
    return normed * gain + shift, normed, inverse


def norm_backward(upstream, normed, inverse, gain):
    scaled = upstream * gain
    inner = jnp.mean(scaled, axis=-1, keepdims=True)
    along = jnp.mean(scaled * normed, axis=-1, keepdims=True)
    return inverse * (scaled - inner - normed * along), token_sum(upstream * normed), token_sum(upstream)


def exact_gelu(values):
    return jax.nn.gelu(values, approximate=False)


def expand_kernel(value_ref, weight_ref, bias_ref, hidden_ref, slope_ref):
    act = dot(value_ref[...], weight_ref[...]) + bias_ref[...]
    share = 0.5 + 0.5 * lax.erf(act * ROOT_HALF)
    hidden_ref[...] = (act * share).astype(BF16)
    slope_ref[...] = share + act * (jnp.exp(-0.5 * act * act) * DENSITY)


ROOT_HALF = 0.7071067811865476
DENSITY = 0.3989422804014327


def expand_gelu(value, weight, bias):
    rows, width = value.shape
    wide = weight.shape[1]
    step = 4 * LANES
    strip = lambda count: pl.BlockSpec((count, step), lambda i: (0, i))
    return pl.pallas_call(
        expand_kernel,
        grid=(wide // step,),
        in_specs=[pl.BlockSpec((rows, width), lambda i: (0, 0)), strip(width), strip(1)],
        out_specs=[strip(rows), strip(rows)],
        out_shape=[jax.ShapeDtypeStruct((rows, wide), BF16), jax.ShapeDtypeStruct((rows, wide), F32)],
        cost_estimate=pl.CostEstimate(flops=2 * rows * width * wide, bytes_accessed=2 * width * wide + 6 * rows * wide, transcendentals=2 * rows * wide),
        compiler_params=pltpu.CompilerParams(dimension_semantics=("arbitrary",)),
        name="expand_gelu",
    )(value, weight, bias)


def seq_offsets(count):
    offsets = [0]
    bit = count // 2
    while bit:
        offsets = offsets + [o ^ bit for o in offsets]
        bit //= 2
    return offsets


def swap(value, axis, bit):
    count = lax.axis_size(axis)
    return lax.ppermute(value, axis, [(i, i ^ bit) for i in range(count)])


def seq_bits():
    bit = lax.axis_size("seq") // 2
    bits = []
    while bit:
        bits.append(bit)
        bit //= 2
    return bits


def seq_gather(rows, bits):
    for bit in bits:
        rows = jnp.concatenate([rows, swap(rows, "seq", bit)], axis=0)
    return rows


def seq_reduce(total, bits):
    for bit in bits:
        half = total.shape[0] // 2
        got = swap(total[half:].astype(BF16), "seq", bit)
        total = total[:half].astype(F32) + got.astype(F32)
    return total


def tie(*values):
    return lax.optimization_barrier(values)


NEAR_LAST = ((16, 8, 2, 4), (8, 16, 4, 2))
NEAR_FIRST = ((2, 4, 8, 16), (4, 2, 16, 8))
DP_LAST = ((16, 8, 4), (4, 16, 8))
NEAR_BACK = ((16, 2, 8, 4), (16, 2, 4, 8))
BLOCK = 8


FLAT = 2 ** (len(NEAR_LAST[0]) + 1)


def owners():
    return lax.axis_size("dp") * lax.axis_size("seq")


def staged():
    return owners() == 2 ** (len(NEAR_LAST[0]) + 1)


def slot_owners(plan):
    def masks(core):
        found = [0]
        for bit in plan[core]:
            found = found + [o ^ bit for o in found]
        return found

    me = lax.axis_index(ALL)
    even = jnp.array(masks(0) + [1 ^ m for m in masks(1)], jnp.int32)
    odd = jnp.array(masks(1) + [1 ^ m for m in masks(0)], jnp.int32)
    return me ^ jnp.where((me & 1) == 0, even, odd)


def group_owners(plan):
    def masks(core):
        found = list(range(lax.axis_size("seq")))
        for bit in plan[core]:
            found = found + [o ^ bit for o in found]
        return found

    me = lax.axis_index(ALL)
    return me ^ jnp.where((me & 1) == 0, jnp.array(masks(0), jnp.int32), jnp.array(masks(1), jnp.int32))


def exchange(pieces):
    return [pieces[0]] + [swap(pieces[d], "seq", d) for d in range(1, len(pieces))]


def stage_swap(value, plan, stage):
    return lax.ppermute(value, ALL, [(d, d ^ plan[d & 1][stage]) for d in range(owners())])


def core_swap(value):
    return lax.ppermute(value, ALL, [(d, d ^ 1) for d in range(owners())])


def place_kernel(groups, rows, counts, order, *refs):
    pieces, refs = refs[: len(counts)], refs[len(counts) :]
    outs, (held, came, left) = refs[:-3], refs[-3:]
    blocks = held.shape[1]
    sizes = [rows] * groups + [blocks - groups * rows] * (len(outs) - groups)
    base = 0
    for piece, count in zip(pieces, counts):

        def fetch(slot, carry):
            pltpu.make_async_copy(piece.at[slot], held.at[base + slot], came.at[base + slot]).start()
            return carry

        lax.fori_loop(0, count, fetch, 0)
        base += count

    def put(slot, carry):
        pltpu.make_async_copy(pieces[0].at[0], held.at[slot], came.at[slot]).wait()
        at = 0
        for out, size in zip(outs, sizes):
            pltpu.make_async_copy(held.at[slot, pl.ds(at, size)], out.at[order[slot]], left).start()
            at += size
        return carry

    lax.fori_loop(0, base, put, 0)

    def finish(slot, carry):
        at = 0
        for out, size in zip(outs, sizes):
            pltpu.make_async_copy(held.at[slot, pl.ds(at, size)], out.at[slot], left).wait()
            at += size
        return carry

    lax.fori_loop(0, base, finish, 0)


def place(pieces, order, groups, rows):
    counts = tuple(p.shape[0] for p in pieces)
    _, blocks, _, width = pieces[0].shape
    devices = sum(counts)
    sizes = [rows] * groups + [blocks - groups * rows] * (blocks > groups * rows)
    anywhere = pl.BlockSpec(memory_space=pl.ANY)
    return pl.pallas_call(
        lambda *refs: place_kernel(groups, rows, counts, *refs),
        out_shape=[jax.ShapeDtypeStruct((devices, size, BLOCK, width), BF16) for size in sizes],
        in_specs=[pl.BlockSpec(memory_space=pltpu.SMEM)] + [anywhere] * len(pieces),
        out_specs=[anywhere] * len(sizes),
        scratch_shapes=[
            pltpu.VMEM((devices, blocks, BLOCK, width), BF16),
            pltpu.SemaphoreType.DMA((devices,)),
            pltpu.SemaphoreType.DMA,
        ],
        cost_estimate=pl.CostEstimate(flops=0, bytes_accessed=4 * devices * blocks * BLOCK * width, transcendentals=0),
        name="place",
    )(order, *pieces)


def spread_kernel(sizes, order, *refs):
    terms, refs = refs[: len(sizes)], refs[len(sizes) :]
    outs, (held, came, left) = refs[:2], refs[2:]
    half = outs[0].shape[0]
    spans = [pl.ds(sum(sizes[:i]), size) for i, size in enumerate(sizes)]
    for i, term in enumerate(terms):
        pltpu.make_async_copy(term, held.at[:, spans[i]], came.at[i]).start()
    for i, term in enumerate(terms):
        pltpu.make_async_copy(term, held.at[:, spans[i]], came.at[i]).wait()
        for index, out in enumerate(outs):

            def put(slot, carry):
                pltpu.make_async_copy(held.at[order[index * half + slot], spans[i]], out.at[slot, spans[i]], left).start()
                return carry

            lax.fori_loop(0, half, put, 0)

    def finish(slot, carry):
        for out in outs:
            for span in spans:
                pltpu.make_async_copy(held.at[slot, span], out.at[slot, span], left).wait()
        return carry

    lax.fori_loop(0, half, finish, 0)


def spread(terms, order):
    devices, _, _, width = terms[0].shape
    sizes = tuple(t.shape[1] for t in terms)
    blocks = sum(sizes)
    shape = jax.ShapeDtypeStruct((devices // 2, blocks, BLOCK, width), BF16)
    anywhere = pl.BlockSpec(memory_space=pl.ANY)
    return pl.pallas_call(
        lambda *refs: spread_kernel(sizes, *refs),
        out_shape=[shape, shape],
        in_specs=[pl.BlockSpec(memory_space=pltpu.SMEM)] + [anywhere] * len(terms),
        out_specs=[anywhere] * 2,
        scratch_shapes=[
            pltpu.VMEM((devices, blocks, BLOCK, width), BF16),
            pltpu.SemaphoreType.DMA((len(sizes),)),
            pltpu.SemaphoreType.DMA,
        ],
        cost_estimate=pl.CostEstimate(flops=0, bytes_accessed=4 * devices * blocks * BLOCK * width, transcendentals=0),
        name="spread",
    )(order, *terms)


def seat(index):
    return index % BLOCK, LANES * (index // BLOCK)


def pack_vectors_kernel(*refs):
    out, held = refs[-2:]
    held[...] = jnp.zeros(held.shape, F32)
    for i, ref in enumerate(refs[:-2]):
        row, lane = seat(i)
        held[row : row + 1, lane : lane + ref.shape[1]] = ref[...].astype(F32)
    out[...] = held[...].astype(BF16)


def pack_vectors(vectors, width):
    return pl.pallas_call(
        pack_vectors_kernel,
        out_shape=jax.ShapeDtypeStruct((BLOCK, width), BF16),
        in_specs=[pl.BlockSpec(memory_space=pltpu.VMEM)] * len(vectors),
        out_specs=pl.BlockSpec(memory_space=pltpu.VMEM),
        scratch_shapes=[pltpu.VMEM((BLOCK, width), F32)],
        name="pack_vectors",
    )(*[v.reshape(1, -1) for v in vectors])


def unpack_vectors_kernel(blocks, out, wide):
    rows = out.shape[1] // blocks.shape[0]
    span = wide.shape[1] // blocks.shape[0]
    row, lane = seat(VECTORS)
    for d in range(blocks.shape[0]):
        for half in range(2):
            part = blocks[d, :, LANES * half : LANES * (half + 1)].astype(F32)
            out[half * BLOCK : (half + 1) * BLOCK, d * rows : (d + 1) * rows] = part[:, :rows]
            if half == lane // LANES:
                wide[:, d * span : (d + 1) * span] = part[row : row + 1, :span]


def unpack_vectors(blocks, width, wide):
    return pl.pallas_call(
        unpack_vectors_kernel,
        grid=(1,),
        in_specs=[pl.BlockSpec((blocks.shape[0], BLOCK, 2 * LANES), lambda i: (0, 0, 0))],
        out_specs=[pl.BlockSpec((2 * BLOCK, width), lambda i: (0, 0)), pl.BlockSpec((1, wide), lambda i: (0, 0))],
        out_shape=[jax.ShapeDtypeStruct((2 * BLOCK, width), F32), jax.ShapeDtypeStruct((1, wide), F32)],
        name="unpack_vectors",
    )(blocks)


def pack_sums_kernel(*refs):
    out = refs[-1]
    vectors, wide = refs[:-2], refs[-2]
    devices = out.shape[0]
    rows = vectors[0].shape[0] // devices
    span = wide.shape[1] // devices
    table = jnp.concatenate([v[...].reshape(1, -1) for v in vectors] + [jnp.zeros((2 * BLOCK - len(vectors), vectors[0].shape[0]), F32)], axis=0)
    row, lane = seat(VECTORS)
    blank = jnp.zeros((BLOCK, LANES - rows), F32)
    empty = jnp.zeros((BLOCK, out.shape[2] - 2 * LANES), F32)
    line = lax.broadcasted_iota(jnp.int32, (BLOCK, LANES), 0)
    for d in range(devices):
        parts = [table[half * BLOCK : (half + 1) * BLOCK, d * rows : (d + 1) * rows] for half in range(2)]
        parts = [jnp.concatenate([part, blank], axis=1) for part in parts]
        strip = jnp.concatenate([wide[:, d * span : (d + 1) * span], jnp.zeros((1, LANES - span), F32)], axis=1)
        parts[lane // LANES] = jnp.where(line == row, strip, parts[lane // LANES])
        out[d] = jnp.concatenate(parts + [empty], axis=1).astype(BF16)


def pack_sums(vectors, wide, width):
    return pl.pallas_call(
        pack_sums_kernel,
        out_shape=jax.ShapeDtypeStruct((owners(), BLOCK, width), BF16),
        in_specs=[pl.BlockSpec(memory_space=pltpu.VMEM)] * (len(vectors) + 1),
        out_specs=pl.BlockSpec(memory_space=pltpu.VMEM),
        name="pack_sums",
    )(*[v.reshape(-1) for v in vectors], wide)


def gather_start(shards):
    parts = jnp.concatenate(list(shards), axis=0) if len(shards) > 1 else shards[0]
    return parts.reshape(1, -1, BLOCK, parts.shape[1]) if staged() else parts


def gather_step(value, plan, stage):
    return jnp.concatenate([value, stage_swap(value, plan, stage)], axis=0) if staged() else value


def gather_last(value, plan):
    return (value, stage_swap(value, plan, len(plan[0]) - 1), core_swap(value)) if staged() else (value,)


def gather_finish(halves):
    return halves + (core_swap(halves[1]),) if staged() else (lax.all_gather(halves[0], ALL, axis=0, tiled=False),)


def unpack(pieces, plan, count, rows):
    width = pieces[0].shape[-1]
    if not staged():
        whole = pieces[0]
        weights = [whole[:, i * rows : (i + 1) * rows].reshape(-1, width) for i in range(count)]
        return weights + [whole[:, count * rows :]]
    found = place(pieces, slot_owners(plan), count, rows // BLOCK)
    return [w.reshape(-1, width) for w in found[:count]] + [t.reshape(-1, BLOCK, width) for t in found[count:]]


def reduce_start(terms, plan, tail=None):
    devices = owners()
    width = terms[0].shape[1]
    parts = [t.astype(BF16).reshape(devices, -1, width) for t in terms]
    if tail is not None:
        parts.append(tail)
    if not staged():
        return (jnp.concatenate(parts, axis=1),) * 2
    return tuple(spread([p.reshape(devices, -1, BLOCK, width) for p in parts], slot_owners(plan)))


def add_halves(mine, got):
    half = mine.shape[0] // 2
    add = lambda a, b: (a.astype(F32) + b.astype(F32)).astype(BF16)
    return add(mine[:half], got[:half]), add(mine[half:], got[half:])


def reduce_core(halves):
    own, other = halves
    return add_halves(own, core_swap(other)) if staged() else (own, own)


def reduce_step(pair, plan, stage):
    if not staged():
        return pair
    got = stage_swap(pair[1], plan, stage)
    if stage:
        return add_halves(pair[0], got)
    return (pair[0].astype(F32) + got.astype(F32),) * 2


def reduce_finish(pair):
    if staged():
        return pair[0].reshape(-1, pair[0].shape[-1])
    return lax.psum_scatter(pair[0], ALL, scatter_dimension=0, tiled=False).astype(F32)


def per_device_by_rows(target, memory, cotangent, target_segments, memory_segments, *shards):
    p = Params(*shards)
    target = target[0]
    memory = memory[0]
    local, width = target.shape
    seq = lax.axis_size("seq")
    place_in_row = lax.axis_index("seq")
    offsets = seq_offsets(seq)
    bits = seq_bits()
    block = local
    rows = p.query_weight.shape[0]
    wide = p.expand_weight.shape[1]
    last = NEAR_LAST

    expand_weight = lax.all_gather(p.expand_weight, ALL, axis=0, tiled=True)
    shrink_weight = lax.all_gather(p.shrink_weight, ALL, axis=0, tiled=True)
    vectors = pack_vectors(vectors_of(p) + (p.expand_bias,), width)
    one = gather_start([p.query_weight, p.key_weight, p.value_weight, p.output_weight, vectors])
    two = gather_start([p.probe_weight, p.lookup_weight, p.content_weight, p.merge_weight])
    marks = jnp.stack([target_segments[0], memory_segments[0]]).astype(BF16)
    marks = jnp.pad(marks, ((0, BLOCK - 2), (0, width - local)))
    target_pack = jnp.concatenate([target, marks], axis=0)[None]
    memory_row = memory[None]
    one = gather_step(one, last, 0)
    target_pack = seq_gather(target_pack, bits[:1])
    one, target_pack, two = tie(one, target_pack, two)
    one = gather_step(one, last, 1)
    target_pack = seq_gather(target_pack, bits[1:])
    one, target_pack, two = tie(one, target_pack, two)
    one = gather_step(one, last, 2)
    two = gather_step(two, last, 0)
    target_row = target_pack[:, :local].reshape(-1, width)
    key_places = jnp.concatenate([(place_in_row ^ o) * local + jnp.arange(local, dtype=jnp.int32) for o in offsets])[None]
    target_marks = target_pack[:, local, :local].reshape(1, -1).astype(jnp.int32)
    memory_marks = target_pack[:, local + 1, :local].reshape(1, -1).astype(jnp.int32)
    own_marks = target_segments.reshape(local, 1)
    start = (place_in_row * local).astype(jnp.int32).reshape(1)
    self_masks = (start, own_marks, target_marks, key_places)
    cross_masks = (start, own_marks, memory_marks, jnp.zeros_like(key_places))
    one, two = tie(one, two)
    one = gather_last(one, last)
    two = gather_step(two, last, 1)
    one, two, memory_row = tie(one, two, memory_row)

    wq, wk, wv, wo, blocks = unpack(gather_finish(one), last, 4, rows)
    two = gather_step(two, last, 2)
    memory_row = seq_gather(memory_row, bits[:1])
    named, expand_bias = unpack_vectors(blocks, width, wide)
    (
        query_bias,
        value_bias,
        output_bias,
        first_gain,
        first_shift,
        probe_bias,
        content_bias,
        merge_bias,
        second_gain,
        second_shift,
        shrink_bias,
        third_gain,
        third_shift,
    ) = (named[i : i + 1] for i in range(VECTORS))
    query_one = ((dot(target, wq) + query_bias) * 0.125).astype(BF16)
    key_one = dot(target_row, wk).astype(BF16)
    value_one = (dot(target_row, wv) + value_bias).astype(BF16)
    query_one, key_one, value_one, two, memory_row = tie(query_one, key_one, value_one, two, memory_row)
    mixed_one, log_one = attend_forward(query_one, key_one, value_one, self_masks, block)
    two = gather_last(two, last)
    memory_row = seq_gather(memory_row, bits[1:]).reshape(-1, width)
    mixed_one, log_one, two, memory_row = tie(mixed_one, log_one, two, memory_row)
    first_sum = target.astype(F32) + dot(mixed_one, wo) + output_bias
    first_full, normed_one, inverse_one = norm_forward(first_sum, first_gain, first_shift)
    first_out = first_full.astype(BF16)
    wp, wl, wc, wm, *_ = unpack(gather_finish(two), last, 4, rows)
    query_two = ((dot(first_out, wp) + probe_bias) * 0.125).astype(BF16)
    key_two = dot(memory_row, wl).astype(BF16)
    value_two = (dot(memory_row, wc) + content_bias).astype(BF16)
    mixed_two, log_two = attend_forward(query_two, key_two, value_two, cross_masks, block)
    second_sum = first_out.astype(F32) + dot(mixed_two, wm) + merge_bias
    second_full, normed_two, inverse_two = norm_forward(second_sum, second_gain, second_shift)
    second_out = second_full.astype(BF16)
    pre_act = dot(second_out, expand_weight) + expand_bias
    hidden = exact_gelu(pre_act).astype(BF16)
    third_sum = second_out.astype(F32) + dot(hidden, shrink_weight) + shrink_bias
    third_full, normed_three, inverse_three = norm_forward(third_sum, third_gain, third_shift)
    layer_output = third_full.astype(BF16)

    upstream = cotangent[0].astype(F32)
    third_grad, third_gain_grad, third_shift_grad = norm_backward(upstream, normed_three, inverse_three, third_gain)
    shrink_in = third_grad.astype(BF16)
    shrink_bias_grad = token_sum(shrink_in)
    shrink_grad = t_dot(hidden, shrink_in).astype(BF16)
    shrink_grad, shrink_in, third_grad = tie(shrink_grad, shrink_in, third_grad)
    four = lax.psum_scatter(shrink_grad, ALL, scatter_dimension=0, tiled=True).astype(F32)
    hidden_grad = dot_t(shrink_in, shrink_weight)
    act_grad = jax.vjp(exact_gelu, pre_act)[1](hidden_grad)[0].astype(BF16)
    expand_bias_grad = token_sum(act_grad)
    three = reduce_start([t_dot(second_out, act_grad)], last)
    three, act_grad, third_grad = tie(three, act_grad, third_grad)
    three = reduce_core(three)
    second_grad = third_grad + dot_t(act_grad, expand_weight)
    second_sum_grad, second_gain_grad, second_shift_grad = norm_backward(second_grad, normed_two, inverse_two, second_gain)
    merge_in = second_sum_grad.astype(BF16)
    merge_bias_grad = token_sum(merge_in)
    mixed_two_grad = dot_t(merge_in, wm).astype(BF16)
    mixed_two_grad, three = tie(mixed_two_grad, three)
    three = reduce_step(three, last, 3)
    probe_in, lookup_part, content_part = attend_backward(query_two, key_two, value_two, mixed_two, mixed_two_grad, log_two, cross_masks, block)
    probe_in, lookup_part, content_part, three = tie(probe_in, lookup_part, content_part, three)
    three = reduce_step(three, last, 2)
    probe_bias_grad = token_sum(probe_in)
    content_bias_grad = token_sum(content_part)
    cross_grads = [t_dot(first_out, probe_in), t_dot(memory_row, lookup_part), t_dot(memory_row, content_part), t_dot(mixed_two, merge_in)]
    two = reduce_start(cross_grads, last)
    first_grad = second_sum_grad + dot_t(probe_in, wp)
    first_sum_grad, first_gain_grad, first_shift_grad = norm_backward(first_grad, normed_one, inverse_one, first_gain)
    output_in = first_sum_grad.astype(BF16)
    output_bias_grad = token_sum(output_in)
    mixed_one_grad = dot_t(output_in, wo).astype(BF16)
    two, three, lookup_part, content_part = tie(two, three, lookup_part, content_part)
    two = reduce_core(two)
    three = reduce_step(three, last, 1)
    memory_part = (dot_t(lookup_part, wl) + dot_t(content_part, wc)).reshape(seq, local, width)
    mixed_one_grad, two, three, memory_part = tie(mixed_one_grad, two, three, memory_part)
    two = reduce_step(two, last, 3)
    three = reduce_step(three, last, 0)
    query_in, key_part, value_part = attend_backward(query_one, key_one, value_one, mixed_one, mixed_one_grad, log_one, self_masks, block)
    query_in, key_part, value_part, two, three, memory_part = tie(query_in, key_part, value_part, two, three, memory_part)
    two = reduce_step(two, last, 2)
    memory_part = seq_reduce(memory_part, bits[:0:-1])
    query_bias_grad = token_sum(query_in)
    value_bias_grad = token_sum(value_part)
    self_grads = [t_dot(target, query_in), t_dot(target_row, key_part), t_dot(target_row, value_part), t_dot(mixed_one, output_in)]
    vector_grads = (
        query_bias_grad,
        value_bias_grad,
        output_bias_grad,
        first_gain_grad,
        first_shift_grad,
        probe_bias_grad,
        content_bias_grad,
        merge_bias_grad,
        second_gain_grad,
        second_shift_grad,
        shrink_bias_grad,
        third_gain_grad,
        third_shift_grad,
    )
    one = reduce_start(self_grads, last, pack_sums(vector_grads, expand_bias_grad, width))
    one, two, memory_part, key_part, value_part, query_in = tie(one, two, memory_part, key_part, value_part, query_in)
    one = reduce_core(one)
    two = reduce_step(two, last, 1)
    target_part = (dot_t(key_part, wk) + dot_t(value_part, wv)).reshape(seq, local, width)
    one, two, memory_part, target_part = tie(one, two, memory_part, target_part)
    one = reduce_step(one, last, 3)
    two = reduce_step(two, last, 0)
    target_part = seq_reduce(target_part, bits[:0:-1])
    target_grad = first_sum_grad + dot_t(query_in, wq)
    one, memory_part, target_part, target_grad = tie(one, memory_part, target_part, target_grad)
    one = reduce_step(one, last, 2)
    memory_grad = seq_reduce(memory_part, bits[:1])[0]
    one, target_part, memory_grad = tie(one, target_part, memory_grad)
    one = reduce_step(one, last, 1)
    target_grad = target_grad + seq_reduce(target_part, bits[:1])[0]
    one = reduce_step(one, last, 0)

    one, two, three = (reduce_finish(t) for t in (one, two, three))
    wide_sum = one[4 * rows :]
    sums = [wide_sum[seat(i)[0], seat(i)[1] : seat(i)[1] + rows] for i in range(VECTORS)]
    row, lane = seat(VECTORS)
    result = Params(
        query_weight=one[:rows],
        key_weight=one[rows : 2 * rows],
        value_weight=one[2 * rows : 3 * rows],
        output_weight=one[3 * rows : 4 * rows],
        probe_weight=two[:rows],
        lookup_weight=two[rows : 2 * rows],
        content_weight=two[2 * rows : 3 * rows],
        merge_weight=two[3 * rows :],
        expand_weight=three.reshape(rows, wide),
        shrink_weight=four,
        expand_bias=wide_sum[row, lane : lane + wide // owners()],
        query_bias=sums[0],
        value_bias=sums[1],
        output_bias=sums[2],
        first_gain=sums[3],
        first_shift=sums[4],
        probe_bias=sums[5],
        content_bias=sums[6],
        merge_bias=sums[7],
        second_gain=sums[8],
        second_shift=sums[9],
        shrink_bias=sums[10],
        third_gain=sums[11],
        third_shift=sums[12],
    )
    return (layer_output[None], target_grad[None], memory_grad[None]) + tuple(result)


def per_device(target, memory, cotangent, target_segments, memory_segments, *shards):
    p = Params(*shards)
    target = target[0]
    memory = memory[0]
    local, width = target.shape
    seq = lax.axis_size("seq")
    place_in_row = lax.axis_index("seq")
    me = place_in_row.astype(jnp.int32).reshape(1)
    offsets = seq_offsets(seq)
    bits = seq_bits()
    block = local
    rows = p.query_weight.shape[0]
    wide = p.expand_weight.shape[1]
    last, near, back = NEAR_LAST, DP_LAST, NEAR_BACK
    heads = width // HEAD_DIM // seq
    span = heads * HEAD_DIM
    space = -(-span // PAIR) * PAIR

    vectors = pack_vectors(vectors_of(p) + (p.expand_bias,), width)
    packed = pack_heads([p.query_weight, p.key_weight, p.value_weight], vectors, me, seq)
    two = gather_start([p.output_weight, p.probe_weight, p.lookup_weight, p.content_weight, p.merge_weight])
    three, four = gather_start([p.expand_weight]), gather_start([p.shrink_weight])
    marks = jnp.stack([target_segments[0], memory_segments[0]]).astype(BF16)
    marks = jnp.pad(marks, ((0, BLOCK - 2), (0, width - local)))
    target_pack = jnp.concatenate([target, marks], axis=0)[None]
    one = jnp.stack(exchange([packed[d] for d in range(seq)]))
    target_pack = seq_gather(target_pack, bits[:1])
    two = gather_step(two, back, 0)
    one, three, four = tie(one, three, four)
    one = gather_step(one, near, 0)
    one, target_pack, two, memory_row = tie(one, target_pack, two, memory[None])
    one = gather_step(one, near, 1)
    target_pack = seq_gather(target_pack, bits[1:])
    memory_row = seq_gather(memory_row, bits[:1])
    target_row = target_pack[:, :local].reshape(-1, width)
    block_places = jnp.stack([(place_in_row ^ o) * local for o in offsets]).astype(jnp.int32)
    key_places = (block_places[:, None] + jnp.arange(local, dtype=jnp.int32)).reshape(1, -1)
    target_marks = target_pack[:, local, :local].reshape(1, -1).astype(jnp.int32)
    memory_marks = target_pack[:, local + 1, :local].reshape(1, -1).astype(jnp.int32)
    own_marks = target_segments.reshape(local, 1)
    self_masks = (block_places, target_marks.reshape(-1, 1), target_marks, key_places)
    cross_masks = (block_places[:1], own_marks, memory_marks, jnp.zeros_like(key_places))
    one, two, memory_row = tie(one, two, memory_row)
    got = stage_swap(one, near, 2)
    two = gather_step(two, back, 1)
    one, got, three, four = tie(one, got, three, four)

    two = gather_step(two, back, 2)
    three = gather_step(three, back, 0)
    four = gather_step(four, back, 0)
    memory_row = seq_gather(memory_row, bits[1:]).reshape(-1, width)
    pieces = [v.reshape(v.shape[0], -1, BLOCK, width) for v in (one, got)]
    wqkv, blocks = place(pieces, group_owners(near), 1, rows // BLOCK)
    wqkv = wqkv.reshape(-1, width)
    named, expand_bias = unpack_vectors(blocks.reshape(-1, BLOCK, width), width, wide)
    (
        query_bias,
        value_bias,
        output_bias,
        first_gain,
        first_shift,
        probe_bias,
        content_bias,
        merge_bias,
        second_gain,
        second_shift,
        shrink_bias,
        third_gain,
        third_shift,
    ) = (named[i : i + 1] for i in range(VECTORS))
    mine = lambda v: jnp.pad(lax.dynamic_slice(v, (0, place_in_row * span), (1, span)), ((0, 0), (0, space - span)))
    row_bias = jnp.concatenate([mine(query_bias), jnp.zeros((1, space), F32), mine(value_bias)], axis=1)
    scale = jnp.where(jnp.arange(3 * space) < space, 0.125, 1.0)[None]
    qkv = ((dot(target_row, wqkv) + row_bias) * scale).astype(BF16)
    qkv, two, three, four, memory_row = tie(qkv, two, three, four, memory_row)
    two = gather_last(two, back)
    three = gather_step(three, back, 1)
    four = gather_step(four, back, 1)
    mixed_row, log_one = row_forward(qkv, self_masks, heads, local, block)
    mixed_row, two, three, four = tie(mixed_row, two, three, four)
    sent = [mixed_row[i * local : (i + 1) * local] for i in range(seq)]
    mixed_one = join_heads(exchange([sent[offsets.index(d)] for d in range(seq)]), me, span)
    two_pieces = gather_finish(two)
    mixed_one, two_pieces, three, four = tie(mixed_one, two_pieces, three, four)
    three = gather_step(three, back, 2)
    four = gather_step(four, back, 2)
    wo, wp, wl, wc, wm, *_ = unpack(two_pieces, back, 5, rows)
    first_sum = target.astype(F32) + dot(mixed_one, wo) + output_bias
    first_full, normed_one, inverse_one = norm_forward(first_sum, first_gain, first_shift)
    first_out = first_full.astype(BF16)
    query_two = ((dot(first_out, wp) + probe_bias) * 0.125).astype(BF16)
    key_two = dot(memory_row, wl).astype(BF16)
    value_two = (dot(memory_row, wc) + content_bias).astype(BF16)
    query_two, key_two, value_two, three, four = tie(query_two, key_two, value_two, three, four)
    three = gather_last(three, back)
    mixed_two, log_two = attend_forward(query_two, key_two, value_two, cross_masks, block)
    mixed_two, three, four = tie(mixed_two, three, four)
    four = gather_last(four, back)
    three = gather_finish(three)
    second_sum = first_out.astype(F32) + dot(mixed_two, wm) + merge_bias
    second_full, normed_two, inverse_two = norm_forward(second_sum, second_gain, second_shift)
    second_out = second_full.astype(BF16)
    expand_weight, *_ = unpack(three, back, 1, rows)
    second_out, expand_weight, four = tie(second_out, expand_weight, four)
    four = gather_finish(four)
    hidden, slope = expand_gelu(second_out, expand_weight, expand_bias)
    hidden, four = tie(hidden, four)
    shrink_weight, *_ = unpack(four, back, 1, p.shrink_weight.shape[0])
    third_sum = second_out.astype(F32) + dot(hidden, shrink_weight) + shrink_bias
    third_full, normed_three, inverse_three = norm_forward(third_sum, third_gain, third_shift)
    layer_output = third_full.astype(BF16)

    upstream = cotangent[0].astype(F32)
    third_grad, third_gain_grad, third_shift_grad = norm_backward(upstream, normed_three, inverse_three, third_gain)
    shrink_in = third_grad.astype(BF16)
    shrink_bias_grad = token_sum(shrink_in)
    shrink_grad = t_dot(hidden, shrink_in).astype(BF16)
    four = reduce_start([shrink_grad], last)
    four, shrink_in, third_grad = tie(four, shrink_in, third_grad)
    four = reduce_core(four)
    act_grad = (dot_t(shrink_in, shrink_weight) * slope).astype(BF16)
    expand_bias_grad = token_sum(act_grad)
    three = reduce_start([t_dot(second_out, act_grad)], last)
    three, four, act_grad, third_grad = tie(three, four, act_grad, third_grad)
    three = reduce_core(three)
    four = reduce_step(four, last, 3)
    second_grad = third_grad + dot_t(act_grad, expand_weight)
    second_sum_grad, second_gain_grad, second_shift_grad = norm_backward(second_grad, normed_two, inverse_two, second_gain)
    merge_in = second_sum_grad.astype(BF16)
    merge_bias_grad = token_sum(merge_in)
    mixed_two_grad = dot_t(merge_in, wm).astype(BF16)
    mixed_two_grad, three = tie(mixed_two_grad, three)
    three = reduce_step(three, last, 3)
    probe_in, lookup_part, content_part = attend_backward(query_two, key_two, value_two, mixed_two, mixed_two_grad, log_two, cross_masks, block)
    probe_in, lookup_part, content_part, three, four = tie(probe_in, lookup_part, content_part, three, four)
    three = reduce_step(three, last, 2)
    four = reduce_step(four, last, 2)
    first_grad = second_sum_grad + dot_t(probe_in, wp)
    first_sum_grad, first_gain_grad, first_shift_grad = norm_backward(first_grad, normed_one, inverse_one, first_gain)
    output_in = first_sum_grad.astype(BF16)
    mixed_one_grad = dot_t(output_in, wo).astype(BF16)
    split = split_heads(mixed_one_grad, me, seq, space)
    split, probe_in, lookup_part, content_part, output_in = tie(split, probe_in, lookup_part, content_part, output_in)
    came = exchange([split[d] for d in range(seq)])
    mixed_row_grad = jnp.concatenate([came[o] for o in offsets], axis=0)
    output_bias_grad = token_sum(output_in)
    probe_bias_grad = token_sum(probe_in)
    content_bias_grad = token_sum(content_part)
    cross_grads = [
        t_dot(mixed_one, output_in),
        t_dot(first_out, probe_in),
        t_dot(memory_row, lookup_part),
        t_dot(memory_row, content_part),
        t_dot(mixed_two, merge_in),
    ]
    two = reduce_start(cross_grads, back)
    mixed_row_grad, two, three, four, lookup_part, content_part = tie(mixed_row_grad, two, three, four, lookup_part, content_part)
    two = reduce_core(two)
    three = reduce_step(three, last, 1)
    four = reduce_step(four, last, 1)
    memory_part = (dot_t(lookup_part, wl) + dot_t(content_part, wc)).reshape(seq, local, width)
    mixed_row_grad, two, memory_part = tie(mixed_row_grad, two, memory_part)
    two = reduce_step(two, back, 3)
    memory_part = seq_reduce(memory_part, bits[:0:-1])
    qkv_grad = row_backward(qkv, mixed_row, mixed_row_grad, log_one, self_masks, heads, local, block)
    qkv_grad, two, three, four, memory_part = tie(qkv_grad, two, three, four, memory_part)
    three = reduce_step(three, last, 0)
    four = reduce_step(four, last, 0)
    two = reduce_step(two, back, 2)
    memory_grad = seq_reduce(memory_part, bits[:1])[0]
    row_grad = t_dot(target_row, qkv_grad)
    sums = token_sum(qkv_grad)
    spot = lambda v: lax.dynamic_update_slice(jnp.zeros((1, width), F32), v, (0, place_in_row * span))
    vector_grads = (
        spot(sums[:, :span]),
        spot(sums[:, 2 * space : 2 * space + span]),
        output_bias_grad,
        first_gain_grad,
        first_shift_grad,
        probe_bias_grad,
        content_bias_grad,
        merge_bias_grad,
        second_gain_grad,
        second_shift_grad,
        shrink_bias_grad,
        third_gain_grad,
        third_shift_grad,
    )
    tail = pack_sums(vector_grads, expand_bias_grad, width)
    terms = [row_grad.astype(BF16).reshape(owners(), -1, BLOCK, width), tail.reshape(owners(), -1, BLOCK, width)]
    one = tuple(spread(terms, group_owners(near)))
    one, qkv_grad = tie(one, qkv_grad)
    one = reduce_step(one, near, 2)
    two = reduce_step(two, back, 1)
    target_part = dot_t(qkv_grad, wqkv).reshape(seq, local, width)
    one, two, target_part = tie(one, two, target_part)
    one = reduce_step(one, near, 1)
    target_part = seq_reduce(target_part, bits[:0:-1])
    one, two, target_part = tie(one, two, target_part)
    one = reduce_step(one, near, 0)
    target_grad = first_sum_grad + seq_reduce(target_part, bits[:1])[0]
    slots = one[0].astype(BF16).reshape(seq, -1, width)
    slots, two = tie(slots, two)
    one = exchange([slots[d] for d in range(seq)])
    two = reduce_step(two, back, 0)

    query_grad, key_grad, value_grad, wide_sum = unpack_heads(one, me, 3, rows)
    two, three, four = (reduce_finish(t) for t in (two, three, four))
    sums = [wide_sum[seat(i)[0], seat(i)[1] : seat(i)[1] + rows] for i in range(VECTORS)]
    row, lane = seat(VECTORS)
    result = Params(
        query_weight=query_grad,
        key_weight=key_grad,
        value_weight=value_grad,
        output_weight=two[:rows],
        probe_weight=two[rows : 2 * rows],
        lookup_weight=two[2 * rows : 3 * rows],
        content_weight=two[3 * rows : 4 * rows],
        merge_weight=two[4 * rows :],
        expand_weight=three.reshape(rows, wide),
        shrink_weight=four,
        expand_bias=wide_sum[row, lane : lane + wide // owners()],
        query_bias=sums[0],
        value_bias=sums[1],
        output_bias=sums[2],
        first_gain=sums[3],
        first_shift=sums[4],
        probe_bias=sums[5],
        content_bias=sums[6],
        merge_bias=sums[7],
        second_gain=sums[8],
        second_shift=sums[9],
        shrink_bias=sums[10],
        third_gain=sums[11],
        third_shift=sums[12],
    )
    return (layer_output[None], target_grad[None], memory_grad[None]) + tuple(result)


def solution(mesh):
    tokens = P("dp", "seq", None)
    matrix = P(ALL, None)
    vector = P(ALL)
    params = Params(*[vector] * len(Params._fields))._replace(
        query_weight=matrix,
        key_weight=matrix,
        value_weight=matrix,
        output_weight=matrix,
        probe_weight=matrix,
        lookup_weight=matrix,
        content_weight=matrix,
        merge_weight=matrix,
        expand_weight=matrix,
        shrink_weight=matrix,
    )
    split = mesh.size == FLAT and mesh.shape["seq"] == 4
    return jax.shard_map(
        per_device if split else per_device_by_rows,
        mesh=mesh,
        in_specs=(tokens, tokens, tokens, P("dp", "seq"), P("dp", "seq")) + tuple(params),
        out_specs=(tokens, tokens, tokens) + tuple(params),
        check_vma=False,
    )
```
